32 devices in a mesh: lat: 8 (over z, x), lon: 4 (over y, core).
Axes of the slice: x: 2, y: 2, z: 4, core: 2. Of those that a mesh axis runs over, the one named last changes fastest.
Arguments:
- wind_u: float32 [4, 1536, 2560], P(None, 'lat', 'lon'), may hold values from -6 to 6
- wind_v: float32 [4, 1536, 2560], P(None, 'lat', 'lon'), may hold values from -6 to 6
- basis: bfloat16 [800, 640, 768], P('lat'), may hold values from -6 to 6
- wave_slots: int32 [640], replicated, may hold values from 0 to 799, as said below
- degree_count: int32 [640], replicated, may hold values from 1 to 640, as said below
- viscosity: float32 [4], replicated, may hold values from 0.5 to 50
Outputs:
- spectral: float32 [800, 4, 2, 2, 640], P('lat', 'lon')
- tendency: float32 [4, 2, 1536, 2560], P(None, None, 'lat', 'lon')
The draws below stay inside these ranges and needn't reach their ends.
Inputs may be any that keep to these rules, and one draw needn't show every extreme that they name: `wave_slots`: all values differ; slot s belongs to owner s // 100, so an owner holds at most 100 wavenumbers, and one owner holds exactly 100. degree_count[0] = 640, and degree_count[m] <= 640 - m.
All inputs are finite; a program needn't handle non-finite values.
Results may differ from the reference program's by a relative error of at most 0.0048.
Values may be sent and summed in bfloat16 or wider, within the bound.
No kernel may reach another device: no remote copies, remote signals or barrier semaphores. Data moves between devices by JAX's collectives and lax.ppermute only.
A program may use at most 256 MiB of HBM per device.

```python
import math
import jax
import jax.numpy as jnp
from jax import lax

NLAT = 1536
NLON = 2560
TRUNC = 640
LEV = 4
CAP = 100
SLOTS = 800


def draw_wave_slots(key, part):
    base = jax.random.fold_in(key, 7)
    owner_key, order_key = jax.random.split(base)
    full_owner = jax.random.randint(owner_key, (), 0, SLOTS // CAP)
    ranking = jax.random.permutation(order_key, SLOTS)
    owners = jnp.arange(SLOTS) // CAP
    priority = jnp.where(owners == full_owner, -1, ranking)
    chosen = jnp.argsort(priority, stable=True)
    return chosen[:TRUNC].astype(jnp.int32)


def draw_degree_count(key, part):
    base = jax.random.fold_in(key, 13)
    shortening = jax.random.randint(base, (TRUNC,), 0, 32)
    shortening = shortening.at[0].set(0)
    wave_ids = jnp.arange(TRUNC)
    return jnp.maximum(1, TRUNC - wave_ids - shortening).astype(jnp.int32)


def block_levels(stream_key, extent, pieces, smallest, largest):
    def one(axis_at, blocks):
        heights = jax.random.uniform(jax.random.fold_in(jax.random.fold_in(stream_key, 6), axis_at), (blocks,), jnp.float32, smallest / len(pieces), largest / len(pieces))
        return jnp.repeat(jnp.exp(heights), extent[axis_at] // blocks).reshape((-1,) + (1,) * (len(extent) - axis_at - 1))

    loudness = one(*pieces[0])
    for cut in pieces[1:]:
        loudness = loudness * one(*cut)
    return loudness


def normal_values(own_key, shape, deviation, limit, pieces=(), kind=jnp.bfloat16):
    factor_of = block_levels(own_key, shape, pieces, -0.22, 0.18) if pieces else 1.0
    drawn = jax.random.normal(own_key, shape, jnp.float32) * deviation * factor_of
    return jnp.minimum(jnp.maximum(drawn, -limit), limit).astype(kind)


def setup_inputs(seed: int = 0) -> dict:
    key_of = jax.random.split(jax.random.key(seed), 7)
    wind_u = normal_values(key_of[0], (LEV, NLAT, NLON), 1.0, 6.0, ((1, 8), (2, 4)), jnp.float32)
    wind_v = normal_values(key_of[1], (LEV, NLAT, NLON), 1.0, 6.0, ((1, 8), (2, 4)), jnp.float32)
    basis = normal_values(key_of[2], (SLOTS, TRUNC, NLAT // 2), 1.0, 6.0, ((0, 8),))
    wave_slots = draw_wave_slots(jax.random.fold_in(key_of[6], 71), 0)
    degree_count = draw_degree_count(jax.random.fold_in(key_of[6], 71), 0)
    viscosity = jnp.clip(jnp.exp(jax.random.uniform(key_of[5], (LEV,), jnp.float32, math.log(0.5), math.log(50.0))), 0.5, 50.0)
    return dict(wind_u=wind_u, wind_v=wind_v, basis=basis, wave_slots=wave_slots, degree_count=degree_count, viscosity=viscosity)


def reference(wind_u, wind_v, basis, wave_slots, degree_count, viscosity):
    products = jnp.stack([wind_u * wind_v, wind_u * wind_u - wind_v * wind_v], axis=1)
    spectrum = jnp.fft.rfft(products, axis=-1)[..., :TRUNC] / math.sqrt(NLON)
    fourier = jnp.stack([jnp.real(spectrum), jnp.imag(spectrum)], axis=-1).astype(jnp.float32)
    fourier = lax.optimization_barrier(fourier.astype(jnp.bfloat16))
    by_wave = jnp.transpose(fourier, (3, 0, 1, 2, 4))
    slot_fourier = jnp.zeros((SLOTS,) + by_wave.shape[1:], jnp.bfloat16).at[wave_slots].set(by_wave)
    wave_ids = jnp.arange(TRUNC, dtype=jnp.int32)
    wave_of_slot = jnp.zeros((SLOTS,), jnp.int32).at[wave_slots].set(wave_ids)
    count_of_slot = jnp.zeros((SLOTS,), jnp.int32).at[wave_slots].set(degree_count.astype(jnp.int32))
    degree_ids = jnp.arange(TRUNC, dtype=jnp.int32)
    parity = jnp.where(degree_ids % 2 == 0, 1.0, -1.0).astype(jnp.float32)

    def per_slot(packed):
        basis_rows, slot_rows, wavenumber, kept_count = packed
        north = basis_rows.astype(jnp.float32)
        basis_wide = jnp.concatenate([north, parity[:, None] * north[:, ::-1]], axis=1)
        raw_coeffs = jnp.einsum('lfar,ja->lfrj', slot_rows.astype(jnp.float32), basis_wide) * (1.0 / math.sqrt(NLAT))
        total_degree = wavenumber + degree_ids
        scaled = (total_degree * (total_degree + 1)).astype(jnp.float32) / float(TRUNC * (TRUNC + 1))
        damping = 1.0 / (1.0 + viscosity[:, None, None, None] * (scaled * scaled)[None, None, None, :])
        damped = jnp.where((degree_ids < kept_count)[None, None, None, :], raw_coeffs * damping, jnp.float32(0.0))
        rounded = lax.optimization_barrier(damped.astype(jnp.bfloat16))
        back_rows = jnp.einsum('lfrj,ja->lfar', rounded.astype(jnp.float32), basis_wide) * (1.0 / math.sqrt(TRUNC))
        return (damped, back_rows.astype(jnp.bfloat16))
    spectral, returned = lax.map(per_slot, (basis, slot_fourier, wave_of_slot, count_of_slot))
    by_slot = returned[wave_slots]
    back_wave = jnp.transpose(by_slot, (1, 2, 3, 0, 4)).astype(jnp.float32)
    complex_rows = back_wave[..., 0] + 1j * back_wave[..., 1]
    padded = jnp.pad(complex_rows, ((0, 0), (0, 0), (0, 0), (0, NLON // 2 + 1 - TRUNC)))
    tendency = (jnp.fft.irfft(padded, n=NLON, axis=-1) * math.sqrt(NLON)).astype(jnp.float32)
    return (spectral, tendency)
```

```python
import functools
import math

import jax
import jax.numpy as jnp
from jax import lax
from jax.experimental import pallas as pl
from jax.experimental.pallas import tpu as pltpu
from jax.sharding import PartitionSpec as P

BF16 = jnp.bfloat16
F32 = jnp.float32
VMEM_LIMIT = 60 * 1024 * 1024
STEP = 128
LANES = 128
DEPTH = 3
NT = (((1,), (1,)), ((), ()))
NN = (((1,), (0,)), ((), ()))


def dot(a, b, dims=NN):
    return lax.dot_general(a, b, dims, preferred_element_type=F32)


def split_high_low(value):
    high = lax.reduce_precision(value, 8, 7)
    return high.astype(BF16), (value - high).astype(BF16)


def wave_tables(sectors, columns, waves):
    length = sectors * columns
    wave_ids = jnp.arange(waves, dtype=jnp.int32)
    unit = 2.0 * math.pi / length

    def angle(places):
        return (wave_ids[:, None] * places[None, :] % length).astype(F32) * unit

    inner = angle(jnp.arange(columns, dtype=jnp.int32))
    outer = angle(jnp.arange(sectors, dtype=jnp.int32) * columns)
    scaling = 1.0 / math.sqrt(length)
    near_cos, near_sin = lax.optimization_barrier((jnp.cos(inner) * scaling, jnp.sin(inner) * scaling))
    far_cos, far_sin = jnp.cos(outer).T[:, :, None], jnp.sin(outer).T[:, :, None]
    real = far_cos * near_cos - far_sin * near_sin
    imag = -(far_sin * near_cos + far_cos * near_sin)
    return split_high_low(real) + split_high_low(imag)


def forward_kernel(lines, real_hi, real_lo, imag_hi, imag_lo, one_hot, mirror, out, by_wave):
    step = pl.program_id(0)
    sectors, rows, _ = lines.shape
    owners = one_hot.shape[0]
    size = real_hi.shape[1]
    place = pl.ds(pl.multiple_of(step * size, size), size)
    for part, (high, low) in enumerate(((real_hi, real_lo), (imag_hi, imag_lo))):
        total = None
        for sector in range(sectors):
            line = lines[sector]
            term = dot(high[sector], line, NT) + dot(low[sector], line, NT)
            total = term if total is None else total + term
        by_wave[part, place, :] = total.astype(BF16)

    @pl.when(step == pl.num_programs(0) - 1)
    def _():
        for part in range(2):
            turned = dot(by_wave[part], mirror[...]).astype(BF16)
            for owner in range(owners):
                out[owner, :, part * rows : (part + 1) * rows] = dot(one_hot[owner], turned).astype(BF16)


def to_owners(lines, tables, one_hot, mirror):
    sectors, rows, columns = lines.shape
    owners, capacity, waves = one_hot.shape
    size = 128
    table_spec = pl.BlockSpec((sectors, size, columns), lambda i: (0, i, 0))
    return pl.pallas_call(
        forward_kernel,
        grid=(waves // size,),
        in_specs=[pl.BlockSpec((sectors, rows, columns), lambda i: (0, 0, 0))]
        + [table_spec] * 4
        + [
            pl.BlockSpec((owners, capacity, waves), lambda i: (0, 0, 0)),
            pl.BlockSpec((rows, rows), lambda i: (0, 0)),
        ],
        out_specs=pl.BlockSpec((owners, capacity, 2 * rows), lambda i: (0, 0, 0)),
        out_shape=jax.ShapeDtypeStruct((owners, capacity, 2 * rows), BF16),
        scratch_shapes=[pltpu.VMEM((2, waves, rows), BF16)],
        compiler_params=pltpu.CompilerParams(vmem_limit_bytes=VMEM_LIMIT),
        name="to_owners",
    )(lines, *tables, one_hot, mirror)


def backward_kernel(slot_rows, real_hi, real_lo, imag_hi, imag_lo, one_hot, mirror, out, by_wave):
    owners, capacity, waves = one_hot.shape
    rows = mirror.shape[0]

    @pl.when(pl.program_id(0) == 0)
    def _():
        wave_ids = lax.broadcasted_iota(jnp.int32, (1, waves), 1)
        weight = jnp.where(wave_ids == 0, 1.0, 2.0).astype(F32)
        for part in range(2):
            total = None
            for owner in range(owners):
                piece = slot_rows[owner, :, part * rows : (part + 1) * rows]
                turned = dot(mirror[...], piece, NT).astype(BF16)
                term = dot(turned, one_hot[owner])
                total = term if total is None else total + term
            by_wave[part] = (total * weight).astype(BF16)

    real, imag = by_wave[0], by_wave[1]
    total = dot(real, real_hi[0]) + dot(real, real_lo[0]) + dot(imag, imag_hi[0]) + dot(imag, imag_lo[0])
    out[0] = total.astype(BF16)


def to_sectors(slot_rows, tables, one_hot, mirror):
    owners, capacity, waves = one_hot.shape
    sectors, _, columns = tables[0].shape
    rows = mirror.shape[0]
    table_spec = pl.BlockSpec((1, waves, columns), lambda i: (i, 0, 0))
    return pl.pallas_call(
        backward_kernel,
        grid=(sectors,),
        in_specs=[pl.BlockSpec((owners, capacity, 2 * rows), lambda i: (0, 0, 0))]
        + [table_spec] * 4
        + [
            pl.BlockSpec((owners, capacity, waves), lambda i: (0, 0, 0)),
            pl.BlockSpec((rows, rows), lambda i: (0, 0)),
        ],
        out_specs=pl.BlockSpec((1, rows, columns), lambda i: (i, 0, 0)),
        out_shape=jax.ShapeDtypeStruct((sectors, rows, columns), BF16),
        scratch_shapes=[pltpu.VMEM((2, rows, waves), BF16)],
        compiler_params=pltpu.CompilerParams(vmem_limit_bytes=VMEM_LIMIT),
        name="to_sectors",
    )(slot_rows, *tables, one_hot, mirror)


def legendre_kernel(fields, lat_rows, group, order, blocks, received, damping, basis, spectral, returned, held, buffer, sems):
    sources, capacity, _ = received.shape
    degrees, half_lat = basis.shape[1:]
    half_sources = sources // 2
    combos = 2 * fields
    lane_blocks = held.shape[0]
    stride = held.shape[1] // (2 * combos)
    groups = capacity // group
    most = degrees // STEP
    scale = 1.0 / math.sqrt(degrees)

    def copies(index, count):
        ring = lax.rem(index, DEPTH)
        rows = pl.ds(0, count * STEP)
        return [
            pltpu.make_async_copy(
                basis.at[order[index * group + i], rows, :], buffer.at[ring, i, rows, :], sems.at[ring, i]
            )
            for i in range(group)
        ]

    def fetch(index):
        for count in range(1, most + 1):

            @pl.when(blocks[index] == count)
            def _():
                for copy in copies(index, count):
                    copy.start()

    for index in range(min(DEPTH - 1, groups)):
        fetch(index)

    def place_of(source):
        side, near = (0, source) if source < half_sources else (1, sources - 1 - source)
        return side, near * lat_rows

    def pieces(source, part, field):
        side, lane = place_of(source)
        row = (side * combos + field * 2 + part) * stride
        column = (part * fields + field) * lat_rows
        end = lane + lat_rows
        while lane < end:
            width = min(LANES - lane % LANES, end - lane)
            yield row, lane // LANES, lane % LANES, column, width
            lane, column = lane + width, column + width

    def load_slot(slot):
        rows = pl.ds(slot, 2 * combos, stride=stride)
        return jnp.concatenate([held[block, rows, :] for block in range(lane_blocks)], axis=1)

    def store_slot(slot, value):
        rows = pl.ds(slot, 2 * combos, stride=stride)
        for block in range(lane_blocks):
            held[block, rows, :] = value[:, block * LANES : (block + 1) * LANES]

    for source in range(sources):
        for part in range(2):
            for field in range(fields):
                for row, block, lane, column, width in pieces(source, part, field):
                    held[block, row : row + capacity, lane : lane + width] = received[
                        source, :, column : column + width
                    ].astype(F32)

    def one_group(index, count):
        ring = lax.rem(index, DEPTH)
        slots = [order[index * group + i] for i in range(group)]
        if count == 0:
            for slot in slots:
                spectral[slot] = jnp.zeros(spectral.shape[1:], F32)
                store_slot(slot, jnp.zeros((2 * combos, half_lat), F32))
            return
        width = count * STEP
        for copy in copies(index, count):
            copy.wait()
        parity = 1.0 - 2.0 * (lax.broadcasted_iota(jnp.int32, (1, width), 1) % 2).astype(F32)
        left = [load_slot(slot).astype(BF16) for slot in slots]
        sums = [dot(left[i], buffer[ring, i, :width, :], NT) for i in range(group)]
        damped = []
        for i, slot in enumerate(slots):
            swapped = jnp.concatenate([sums[i][combos:], sums[i][:combos]], axis=0)
            damped.append((sums[i] + parity * swapped) * damping[slot, :, :width])
        backs = [dot(damped[i].astype(BF16), buffer[ring, i, :width, :]) * scale for i in range(group)]
        for i, slot in enumerate(slots):
            for field in range(fields):
                spectral[slot, field // 2, field % 2, :, :width] = damped[i][2 * field : 2 * field + 2]
                if width < degrees:
                    spectral[slot, field // 2, field % 2, :, width:] = jnp.zeros((2, degrees - width), F32)
        for i, slot in enumerate(slots):
            store_slot(slot, backs[i])

    def loop_body(index, carry):
        @pl.when(index + DEPTH - 1 < groups)
        def _():
            fetch(index + DEPTH - 1)

        for count in range(most + 1):
            pl.when(blocks[index] == count)(functools.partial(one_group, index, count))
        return carry

    lax.fori_loop(0, groups, loop_body, 0)

    for source in range(sources):
        for part in range(2):
            for field in range(fields):
                for row, block, lane, column, width in pieces(source, part, field):
                    returned[source, :, column : column + width] = held[
                        block, row : row + capacity, lane : lane + width
                    ].astype(BF16)


def legendre(received, basis, damping, order, blocks, level_dev, lat_rows, group):
    sources, capacity, lanes = received.shape
    degrees, half_lat = basis.shape[1:]
    fields = 2 * level_dev
    stride = -(-capacity // 8) * 8
    smem, vmem, hbm = (pl.BlockSpec(memory_space=space) for space in (pltpu.SMEM, pltpu.VMEM, pl.ANY))
    return pl.pallas_call(
        functools.partial(legendre_kernel, fields, lat_rows, group),
        in_specs=[smem, smem, vmem, vmem, hbm],
        out_specs=[vmem, vmem],
        out_shape=[
            jax.ShapeDtypeStruct((capacity, level_dev, 2, 2, degrees), F32),
            jax.ShapeDtypeStruct((sources, capacity, lanes), BF16),
        ],
        scratch_shapes=[
            pltpu.VMEM((half_lat // LANES, 4 * fields * stride, LANES), F32),
            pltpu.VMEM((DEPTH, group, degrees, half_lat), BF16),
            pltpu.SemaphoreType.DMA((DEPTH, group)),
        ],
        compiler_params=pltpu.CompilerParams(vmem_limit_bytes=VMEM_LIMIT),
        name="legendre",
    )(order, blocks, received, damping, basis)


def body(wind_u, wind_v, basis, wave_slots, degree_count, viscosity):
    sectors = lax.axis_size("lon")
    owners = lax.axis_size("lat")
    sector_index = lax.axis_index("lon")
    owner_index = lax.axis_index("lat")
    levels, lat_rows, lon_cols = wind_u.shape
    level_dev = levels // sectors
    assert level_dev == 1
    capacity, degrees, half_lat = basis.shape
    latitudes = 2 * half_lat
    waves = wave_slots.shape[0]
    slot_total = capacity * owners
    rows = level_dev * 2 * lat_rows
    products = jnp.stack([wind_u * wind_v, wind_u * wind_u - wind_v * wind_v], axis=1)
    products = products.astype(BF16).reshape(sectors, rows, lon_cols)
    lines = lax.all_to_all(products, "lon", split_axis=0, concat_axis=0, tiled=True)

    slot_ids = jnp.arange(slot_total, dtype=jnp.int32)
    matches = wave_slots[:, None] == slot_ids[None, :]
    wave_ids = jnp.arange(waves, dtype=jnp.int32)
    wave_of_slot = jnp.sum(jnp.where(matches, wave_ids[:, None] + 1, 0), axis=0) - 1
    count_of_slot = jnp.sum(jnp.where(matches, degree_count[:, None], 0), axis=0)
    one_hot = (wave_of_slot.reshape(owners, capacity, 1) == wave_ids).astype(BF16)
    row_ids = jnp.arange(rows, dtype=jnp.int32)
    mirrored = row_ids // lat_rows * lat_rows + (lat_rows - 1 - row_ids % lat_rows)
    south = owner_index >= owners // 2
    mirror = (row_ids[:, None] == jnp.where(south, mirrored, row_ids)[None, :]).astype(BF16)
    tables = wave_tables(sectors, lon_cols, waves)

    wave_here = lax.dynamic_slice_in_dim(wave_of_slot, owner_index * capacity, capacity)
    count_here = lax.dynamic_slice_in_dim(count_of_slot, owner_index * capacity, capacity)
    rates = lax.dynamic_slice_in_dim(viscosity, sector_index * level_dev, level_dev)
    degree_ids = jnp.arange(degrees, dtype=jnp.int32)
    total_degree = wave_here[:, None] + degree_ids[None, :]
    scaled = (total_degree * (total_degree + 1)).astype(F32) / float(degrees * (degrees + 1))
    damping = 1.0 / (1.0 + rates[0] * (scaled * scaled))
    kept = degree_ids[None, :] < count_here[:, None]
    damping = jnp.where(kept, damping * (1.0 / math.sqrt(latitudes)), 0.0)[:, None, :]
    here_ids = jnp.arange(capacity, dtype=jnp.int32)
    ahead = (count_here[None, :] > count_here[:, None]) | (
        (count_here[None, :] == count_here[:, None]) & (here_ids[None, :] < here_ids[:, None])
    )
    rank = jnp.sum(ahead.astype(jnp.int32), axis=1)
    sorted_here = rank[:, None] == here_ids[None, :]
    order = jnp.sum(jnp.where(sorted_here, here_ids[:, None], 0), axis=0)
    sorted_count = jnp.sum(jnp.where(sorted_here, count_here[:, None], 0), axis=0)
    group = max(size for size in range(1, 6) if capacity % size == 0)
    blocks = (sorted_count[::group] + (STEP - 1)) // STEP

    fourier = to_owners(lines, tables, one_hot, mirror)
    received = lax.all_to_all(fourier, "lat", split_axis=0, concat_axis=0, tiled=True)
    spectral, returned = legendre(received, basis, damping, order, blocks, level_dev, lat_rows, group)
    regrouped = lax.all_to_all(returned, "lat", split_axis=0, concat_axis=0, tiled=True)
    grid_lines = to_sectors(regrouped, tables, one_hot, mirror)
    tendency = lax.all_to_all(grid_lines, "lon", split_axis=0, concat_axis=0, tiled=True)
    return spectral, tendency.astype(F32).reshape(levels, 2, lat_rows, lon_cols)


def solution(mesh):
    return jax.shard_map(
        body,
        mesh=mesh,
        in_specs=(
            P(None, "lat", "lon"),
            P(None, "lat", "lon"),
            P("lat", None, None),
            P(),
            P(),
            P(),
        ),
        out_specs=(P("lat", "lon", None, None, None), P(None, None, "lat", "lon")),
        check_vma=False,
    )
```

```python
import functools
import math

import jax
import jax.numpy as jnp
from jax import lax
from jax.experimental import pallas as pl
from jax.experimental.pallas import tpu as pltpu
from jax.sharding import PartitionSpec as P

BF16 = jnp.bfloat16
F32 = jnp.float32
VMEM_LIMIT = 60 * 1024 * 1024
STEP = 128
LANES = 128
DEPTH = 3
NT = (((1,), (1,)), ((), ()))
NN = (((1,), (0,)), ((), ()))


def dot(a, b, dims=NN):
    return lax.dot_general(a, b, dims, preferred_element_type=F32)


def split_high_low(value):
    high = lax.reduce_precision(value, 8, 7)
    return high.astype(BF16), (value - high).astype(BF16)


def wave_tables(sectors, columns, waves):
    length = sectors * columns
    wave_ids = jnp.arange(waves, dtype=jnp.int32)
    unit = 2.0 * math.pi / length

    def angle(places):
        return (wave_ids[:, None] * places[None, :] % length).astype(F32) * unit

    inner = angle(jnp.arange(columns, dtype=jnp.int32))
    outer = angle(jnp.arange(sectors, dtype=jnp.int32) * columns)
    scaling = 1.0 / math.sqrt(length)
    near_cos, near_sin = lax.optimization_barrier((jnp.cos(inner) * scaling, jnp.sin(inner) * scaling))
    far_cos, far_sin = jnp.cos(outer).T[:, :, None], jnp.sin(outer).T[:, :, None]
    real = far_cos * near_cos - far_sin * near_sin
    imag = -(far_sin * near_cos + far_cos * near_sin)
    return split_high_low(real) + split_high_low(imag)


def forward_kernel(lines, real_hi, real_lo, imag_hi, imag_lo, one_hot, mirror, *rest):
    outs, by_wave = rest[:-1], rest[-1]
    step = pl.program_id(0)
    sectors, rows, _ = lines.shape
    owners = one_hot.shape[0]
    size = real_hi.shape[1]
    place = pl.ds(pl.multiple_of(step * size, size), size)
    for part, (high, low) in enumerate(((real_hi, real_lo), (imag_hi, imag_lo))):
        total = None
        for sector in range(sectors):
            line = lines[sector]
            term = dot(high[sector], line, NT) + dot(low[sector], line, NT)
            total = term if total is None else total + term
        by_wave[part, place, :] = total.astype(BF16)

    @pl.when(step == pl.num_programs(0) - 1)
    def _():
        for part in range(2):
            turned = dot(by_wave[part], mirror[...]).astype(BF16)
            for owner in range(owners):
                first = 0
                for out in outs:
                    last = first + out.shape[1]
                    out[owner, :, part * rows : (part + 1) * rows] = dot(
                        one_hot[owner, first:last, :], turned
                    ).astype(BF16)
                    first = last


def to_owners(lines, tables, one_hot, mirror, chunks):
    sectors, rows, columns = lines.shape
    owners, capacity, waves = one_hot.shape
    size = 128
    table_spec = pl.BlockSpec((sectors, size, columns), lambda i: (0, i, 0))
    return pl.pallas_call(
        forward_kernel,
        grid=(waves // size,),
        in_specs=[pl.BlockSpec((sectors, rows, columns), lambda i: (0, 0, 0))]
        + [table_spec] * 4
        + [
            pl.BlockSpec((owners, capacity, waves), lambda i: (0, 0, 0)),
            pl.BlockSpec((rows, rows), lambda i: (0, 0)),
        ],
        out_specs=[pl.BlockSpec((owners, chunk, 2 * rows), lambda i: (0, 0, 0)) for chunk in chunks],
        out_shape=[jax.ShapeDtypeStruct((owners, chunk, 2 * rows), BF16) for chunk in chunks],
        scratch_shapes=[pltpu.VMEM((2, waves, rows), BF16)],
        compiler_params=pltpu.CompilerParams(vmem_limit_bytes=VMEM_LIMIT),
        name="to_owners",
    )(lines, *tables, one_hot, mirror)


def backward_kernel(count, *refs):
    pieces, (real_hi, real_lo, imag_hi, imag_lo, one_hot, mirror, out, by_wave) = refs[:count], refs[count:]
    owners, capacity, waves = one_hot.shape
    rows = mirror.shape[0]

    @pl.when(pl.program_id(0) == 0)
    def _():
        wave_ids = lax.broadcasted_iota(jnp.int32, (1, waves), 1)
        weight = jnp.where(wave_ids == 0, 1.0, 2.0).astype(F32)
        for part in range(2):
            total = None
            for owner in range(owners):
                first = 0
                for piece in pieces:
                    last = first + piece.shape[1]
                    turned = dot(mirror[...], piece[owner, :, part * rows : (part + 1) * rows], NT).astype(BF16)
                    term = dot(turned, one_hot[owner, first:last, :])
                    total = term if total is None else total + term
                    first = last
            by_wave[part] = (total * weight).astype(BF16)

    real, imag = by_wave[0], by_wave[1]
    total = dot(real, real_hi[0]) + dot(real, real_lo[0]) + dot(imag, imag_hi[0]) + dot(imag, imag_lo[0])
    out[0] = total.astype(BF16)


def to_sectors(pieces, tables, one_hot, mirror):
    owners, capacity, waves = one_hot.shape
    sectors, _, columns = tables[0].shape
    rows = mirror.shape[0]
    table_spec = pl.BlockSpec((1, waves, columns), lambda i: (i, 0, 0))
    return pl.pallas_call(
        functools.partial(backward_kernel, len(pieces)),
        grid=(sectors,),
        in_specs=[pl.BlockSpec(piece.shape, lambda i: (0, 0, 0)) for piece in pieces]
        + [table_spec] * 4
        + [
            pl.BlockSpec((owners, capacity, waves), lambda i: (0, 0, 0)),
            pl.BlockSpec((rows, rows), lambda i: (0, 0)),
        ],
        out_specs=pl.BlockSpec((1, rows, columns), lambda i: (i, 0, 0)),
        out_shape=jax.ShapeDtypeStruct((sectors, rows, columns), BF16),
        scratch_shapes=[pltpu.VMEM((2, rows, waves), BF16)],
        compiler_params=pltpu.CompilerParams(vmem_limit_bytes=VMEM_LIMIT),
        name="to_sectors",
    )(*pieces, *tables, one_hot, mirror)


def legendre_kernel(fields, lat_rows, group, start, aliased, order, blocks, received, damping, basis, *rest):
    spectral_out, returned, spectral, held, buffer, sems, out_sem = rest[aliased:]
    sources, capacity, _ = received.shape
    degrees, half_lat = basis.shape[1:]
    half_sources = sources // 2
    combos = 2 * fields
    lane_blocks = held.shape[0]
    stride = held.shape[1] // (2 * combos)
    groups = capacity // group
    most = degrees // STEP
    scale = 1.0 / math.sqrt(degrees)

    def copies(index, count):
        ring = lax.rem(index, DEPTH)
        rows = pl.ds(0, count * STEP)
        return [
            pltpu.make_async_copy(
                basis.at[start + order[index * group + i], rows, :], buffer.at[ring, i, rows, :], sems.at[ring, i]
            )
            for i in range(group)
        ]

    def fetch(index):
        for count in range(1, most + 1):

            @pl.when(blocks[index] == count)
            def _():
                for copy in copies(index, count):
                    copy.start()

    for index in range(min(DEPTH - 1, groups)):
        fetch(index)

    def place_of(source):
        side, near = (0, source) if source < half_sources else (1, sources - 1 - source)
        return side, near * lat_rows

    def pieces(source, part, field):
        side, lane = place_of(source)
        row = (side * combos + field * 2 + part) * stride
        column = (part * fields + field) * lat_rows
        end = lane + lat_rows
        while lane < end:
            width = min(LANES - lane % LANES, end - lane)
            yield row, lane // LANES, lane % LANES, column, width
            lane, column = lane + width, column + width

    def load_slot(slot):
        rows = pl.ds(slot, 2 * combos, stride=stride)
        return jnp.concatenate([held[block, rows, :] for block in range(lane_blocks)], axis=1)

    def store_slot(slot, value):
        rows = pl.ds(slot, 2 * combos, stride=stride)
        for block in range(lane_blocks):
            held[block, rows, :] = value[:, block * LANES : (block + 1) * LANES]

    for source in range(sources):
        for part in range(2):
            for field in range(fields):
                for row, block, lane, column, width in pieces(source, part, field):
                    held[block, row : row + capacity, lane : lane + width] = received[
                        source, :, column : column + width
                    ].astype(F32)

    def one_group(index, count):
        ring = lax.rem(index, DEPTH)
        slots = [order[index * group + i] for i in range(group)]
        if count == 0:
            for slot in slots:
                spectral[slot] = jnp.zeros(spectral.shape[1:], F32)
                store_slot(slot, jnp.zeros((2 * combos, half_lat), F32))
            return
        width = count * STEP
        for copy in copies(index, count):
            copy.wait()
        parity = 1.0 - 2.0 * (lax.broadcasted_iota(jnp.int32, (1, width), 1) % 2).astype(F32)
        left = [load_slot(slot).astype(BF16) for slot in slots]
        sums = [dot(left[i], buffer[ring, i, :width, :], NT) for i in range(group)]
        damped = []
        for i, slot in enumerate(slots):
            swapped = jnp.concatenate([sums[i][combos:], sums[i][:combos]], axis=0)
            damped.append((sums[i] + parity * swapped) * damping[slot, :, :width])
        backs = [dot(damped[i].astype(BF16), buffer[ring, i, :width, :]) * scale for i in range(group)]
        for i, slot in enumerate(slots):
            for field in range(fields):
                spectral[slot, field // 2, field % 2, :, :width] = damped[i][2 * field : 2 * field + 2]
                if width < degrees:
                    spectral[slot, field // 2, field % 2, :, width:] = jnp.zeros((2, degrees - width), F32)
        for i, slot in enumerate(slots):
            store_slot(slot, backs[i])

    def loop_body(index, carry):
        @pl.when(index + DEPTH - 1 < groups)
        def _():
            fetch(index + DEPTH - 1)

        for count in range(most + 1):
            pl.when(blocks[index] == count)(functools.partial(one_group, index, count))
        return carry

    lax.fori_loop(0, groups, loop_body, 0)
    spectral_copy = pltpu.make_async_copy(spectral, spectral_out.at[pl.ds(start, capacity)], out_sem)
    spectral_copy.start()

    for source in range(sources):
        for part in range(2):
            for field in range(fields):
                for row, block, lane, column, width in pieces(source, part, field):
                    returned[source, :, column : column + width] = held[
                        block, row : row + capacity, lane : lane + width
                    ].astype(BF16)
    spectral_copy.wait()


def legendre(received, basis, damping, order, blocks, level_dev, lat_rows, group, start, spectral=None):
    sources, capacity, lanes = received.shape
    slots, degrees, half_lat = basis.shape
    fields = 2 * level_dev
    stride = -(-capacity // 8) * 8
    smem, vmem, hbm = (pl.BlockSpec(memory_space=space) for space in (pltpu.SMEM, pltpu.VMEM, pl.ANY))
    earlier = () if spectral is None else (spectral,)
    spectral_shape = (level_dev, 2, 2, degrees)
    return pl.pallas_call(
        functools.partial(legendre_kernel, fields, lat_rows, group, start, len(earlier)),
        in_specs=[smem, smem, vmem, vmem, hbm] + [hbm] * len(earlier),
        out_specs=[hbm, vmem],
        out_shape=[
            jax.ShapeDtypeStruct((slots,) + spectral_shape, F32),
            jax.ShapeDtypeStruct((sources, capacity, lanes), BF16),
        ],
        scratch_shapes=[
            pltpu.VMEM((capacity,) + spectral_shape, F32),
            pltpu.VMEM((half_lat // LANES, 4 * fields * stride, LANES), F32),
            pltpu.VMEM((DEPTH, group, degrees, half_lat), BF16),
            pltpu.SemaphoreType.DMA((DEPTH, group)),
            pltpu.SemaphoreType.DMA,
        ],
        input_output_aliases={5: 0} if earlier else {},
        cost_estimate=pl.CostEstimate(
            flops=4 * capacity * degrees * half_lat * 4 * fields,
            bytes_accessed=2 * capacity * degrees * half_lat,
            transcendentals=0,
        ),
        compiler_params=pltpu.CompilerParams(vmem_limit_bytes=VMEM_LIMIT),
        name="legendre",
    )(order, blocks, received, damping, basis, *earlier)


def degree_order(counts):
    size = counts.shape[0]
    ids = jnp.arange(size, dtype=jnp.int32)
    ahead = (counts[None, :] > counts[:, None]) | ((counts[None, :] == counts[:, None]) & (ids[None, :] < ids[:, None]))
    rank = jnp.sum(ahead.astype(jnp.int32), axis=1)
    placed = rank[:, None] == ids[None, :]
    order = jnp.sum(jnp.where(placed, ids[:, None], 0), axis=0)
    sorted_counts = jnp.sum(jnp.where(placed, counts[:, None], 0), axis=0)
    group = max(g for g in range(1, 6) if size % g == 0)
    return order, (sorted_counts[::group] + (STEP - 1)) // STEP, group


def body(wind_u, wind_v, basis, wave_slots, degree_count, viscosity):
    sectors = lax.axis_size("lon")
    owners = lax.axis_size("lat")
    sector_index = lax.axis_index("lon")
    owner_index = lax.axis_index("lat")
    levels, lat_rows, lon_cols = wind_u.shape
    level_dev = levels // sectors
    assert level_dev == 1
    capacity, degrees, half_lat = basis.shape
    latitudes = 2 * half_lat
    waves = wave_slots.shape[0]
    slot_total = capacity * owners
    rows = level_dev * 2 * lat_rows
    products = jnp.stack([wind_u * wind_v, wind_u * wind_u - wind_v * wind_v], axis=1)
    products = products.astype(BF16).reshape(sectors, rows, lon_cols)
    lines = lax.all_to_all(products, "lon", split_axis=0, concat_axis=0, tiled=True)

    slot_ids = jnp.arange(slot_total, dtype=jnp.int32)
    matches = wave_slots[:, None] == slot_ids[None, :]
    wave_ids = jnp.arange(waves, dtype=jnp.int32)
    wave_of_slot = jnp.sum(jnp.where(matches, wave_ids[:, None] + 1, 0), axis=0) - 1
    count_of_slot = jnp.sum(jnp.where(matches, degree_count[:, None], 0), axis=0)
    one_hot = (wave_of_slot.reshape(owners, capacity, 1) == wave_ids).astype(BF16)
    row_ids = jnp.arange(rows, dtype=jnp.int32)
    mirrored = row_ids // lat_rows * lat_rows + (lat_rows - 1 - row_ids % lat_rows)
    south = owner_index >= owners // 2
    mirror = (row_ids[:, None] == jnp.where(south, mirrored, row_ids)[None, :]).astype(BF16)
    tables = wave_tables(sectors, lon_cols, waves)

    wave_here = lax.dynamic_slice_in_dim(wave_of_slot, owner_index * capacity, capacity)
    count_here = lax.dynamic_slice_in_dim(count_of_slot, owner_index * capacity, capacity)
    rates = lax.dynamic_slice_in_dim(viscosity, sector_index * level_dev, level_dev)
    degree_ids = jnp.arange(degrees, dtype=jnp.int32)
    total_degree = wave_here[:, None] + degree_ids[None, :]
    scaled = (total_degree * (total_degree + 1)).astype(F32) / float(degrees * (degrees + 1))
    damping = 1.0 / (1.0 + rates[0] * (scaled * scaled))
    kept = degree_ids[None, :] < count_here[:, None]
    damping = jnp.where(kept, damping * (1.0 / math.sqrt(latitudes)), 0.0)[:, None, :]
    head = capacity // 32 * 16 or capacity
    chunks = (head, capacity - head) if head < capacity else (capacity,)

    fourier = to_owners(lines, tables, one_hot, mirror, chunks)
    spectral, start, regrouped = None, 0, []
    for piece in fourier:
        end = start + piece.shape[1]
        received = lax.all_to_all(piece, "lat", split_axis=0, concat_axis=0, tiled=True)
        order, blocks, group = degree_order(count_here[start:end])
        spectral, returned = legendre(
            received, basis, damping[start:end], order, blocks, level_dev, lat_rows, group, start, spectral
        )
        regrouped.append(lax.all_to_all(returned, "lat", split_axis=0, concat_axis=0, tiled=True))
        start = end
    grid_lines = to_sectors(regrouped, tables, one_hot, mirror)
    tendency = lax.all_to_all(grid_lines, "lon", split_axis=0, concat_axis=0, tiled=True)
    return spectral, tendency.astype(F32).reshape(levels, 2, lat_rows, lon_cols)


def solution(mesh):
    return jax.shard_map(
        body,
        mesh=mesh,
        in_specs=(
            P(None, "lat", "lon"),
            P(None, "lat", "lon"),
            P("lat", None, None),
            P(),
            P(),
            P(),
        ),
        out_specs=(P("lat", "lon", None, None, None), P(None, None, "lat", "lon")),
        check_vma=False,
    )
```

```python
import functools
import math

import jax
import jax.numpy as jnp
import numpy as np
from jax import lax
from jax.experimental import pallas as pl
from jax.experimental.pallas import tpu as pltpu
from jax.sharding import PartitionSpec as P

BF16 = jnp.bfloat16
F32 = jnp.float32
VMEM_LIMIT = 60 * 1024 * 1024
STEP = 128
LANES = 128
DEPTH = 3
NT = (((1,), (1,)), ((), ()))
NN = (((1,), (0,)), ((), ()))


def dot(a, b, dims=NN):
    return lax.dot_general(a, b, dims, preferred_element_type=F32)


def split_high_low(value):
    high = lax.reduce_precision(value, 8, 7)
    return high.astype(BF16), (value - high).astype(BF16)


def wave_tables(sectors, columns, waves):
    length = sectors * columns
    places = jnp.arange(columns, dtype=jnp.int32)
    wave_ids = jnp.arange(waves, dtype=jnp.int32)
    angles = (places[:, None] * wave_ids[None, :] % length).astype(F32) * (2.0 * math.pi / length)
    scaling = 1.0 / math.sqrt(length)
    cos_hi, cos_lo = split_high_low(jnp.cos(angles) * scaling)
    sin_hi, sin_lo = split_high_low(jnp.sin(angles) * scaling)
    size = min(LANES, waves)

    def side_by_side(a, b):
        shape = (columns, waves // size, size)
        return jnp.concatenate([a.reshape(shape), b.reshape(shape)], axis=2).reshape(columns, 2 * waves)

    forward = jnp.concatenate([side_by_side(cos_hi, sin_hi), side_by_side(cos_lo, sin_lo)], axis=0)
    quarters = (cos_hi, sin_hi, cos_lo, sin_lo)
    if columns != waves:
        quarters = tuple(quarter.T for quarter in quarters)
    return forward, jnp.concatenate(quarters, axis=0)


def sector_turns(sectors, waves):
    turns = 2.0 * np.pi * (np.arange(sectors)[:, None] * np.arange(waves)[None, :] % sectors) / sectors
    return tuple(np.round(f(turns), 12).astype(np.float32)[:, None, :] for f in (np.cos, np.sin))


def forward_kernel(lines, table, turn_cos, turn_sin, one_hot, mirror, out, by_wave, by_slot):
    step = pl.program_id(0)
    sectors, rows, columns = lines.shape
    size = table.shape[1] // 2
    devices, wire_rows, lanes = out.shape
    padded = one_hot.shape[0] // devices
    blocks = 2 * rows // lanes
    share = wire_rows // blocks
    both = jnp.concatenate([lines[...].reshape(sectors * rows, columns)] * 2, axis=1)
    sums = dot(both, table[...])
    real = imag = None
    for sector in range(sectors):
        own = sums[sector * rows : (sector + 1) * rows]
        own_cos, own_sin = own[:, :size], own[:, size:]
        cos, sin = turn_cos[sector], turn_sin[sector]
        own_real, own_imag = own_cos * cos - own_sin * sin, own_cos * sin + own_sin * cos
        real, imag = (own_real, own_imag) if real is None else (real + own_real, imag + own_imag)
    place = pl.ds(pl.multiple_of(step * size, size), size)
    by_wave[0, :, place] = real.astype(BF16)
    by_wave[1, :, place] = (-imag).astype(BF16)

    @pl.when(step == pl.num_programs(0) - 1)
    def _():
        for part in range(2):
            turned = dot(mirror[...], by_wave[part]).astype(BF16)
            by_slot[:, part * rows : (part + 1) * rows] = dot(one_hot[...], turned, NT)
        for device in range(devices):
            own = by_slot[device * padded : (device + 1) * padded, :]
            out[device] = jnp.concatenate(
                [own[:share, block * lanes : (block + 1) * lanes] for block in range(blocks)], axis=0
            ).astype(BF16)


def to_owners(lines, table, turns, one_hot, mirror, share):
    sectors, rows, columns = lines.shape
    slots, waves = one_hot.shape
    devices = slots // round_up(share, 8)
    size = min(LANES, waves)
    lanes = wire_lanes(rows)
    out = (devices, share * (2 * rows // lanes), lanes)
    turn_spec = pl.BlockSpec((sectors, 1, size), lambda i: (0, 0, i))
    return pl.pallas_call(
        forward_kernel,
        grid=(waves // size,),
        in_specs=[
            pl.BlockSpec((sectors, rows, columns), lambda i: (0, 0, 0)),
            pl.BlockSpec((2 * columns, 2 * size), lambda i: (0, i)),
            turn_spec,
            turn_spec,
            pl.BlockSpec((slots, waves), lambda i: (0, 0)),
            pl.BlockSpec((rows, rows), lambda i: (0, 0)),
        ],
        out_specs=pl.BlockSpec(out, lambda i: (0, 0, 0)),
        out_shape=jax.ShapeDtypeStruct(out, BF16),
        scratch_shapes=[pltpu.VMEM((2, rows, waves), BF16), pltpu.VMEM((slots, 2 * rows), F32)],
        cost_estimate=pl.CostEstimate(flops=8 * sectors * rows * columns * waves, bytes_accessed=10**7, transcendentals=0),
        compiler_params=pltpu.CompilerParams(vmem_limit_bytes=VMEM_LIMIT),
        name="to_owners",
    )(lines, table, *turns, one_hot, mirror)


def backward_kernel(exact, wire, table, turn_cos, turn_sin, one_hot, mirror, out, by_slot, by_wave):
    devices, wire_rows, lanes = wire.shape
    sectors, rows, columns = out.shape
    waves = table.shape[0] // 4
    padded = by_slot.shape[0] // devices
    blocks = 2 * rows // lanes
    share = wire_rows // blocks

    @pl.when(pl.program_id(0) == 0)
    def _():
        for device in range(devices):
            own = wire[device].astype(F32)
            for block in range(blocks):
                piece = own[block * share : (block + 1) * share]
                if padded > share:
                    piece = jnp.concatenate([piece, jnp.zeros((padded - share, lanes), F32)], axis=0)
                by_slot[device * padded : (device + 1) * padded, block * lanes : (block + 1) * lanes] = piece.astype(BF16)
        wave_ids = lax.broadcasted_iota(jnp.int32, (1, waves), 1)
        weight = jnp.where(wave_ids == 0, 1.0, 2.0).astype(F32)
        for part in range(2):
            ordered = dot(one_hot[...], by_slot[:, part * rows : (part + 1) * rows]).astype(BF16)
            by_wave[part] = dot(mirror[...], ordered, NT) * weight

    left = []
    for sector in range(sectors):
        cos, sin = turn_cos[sector], turn_sin[sector]
        real = by_wave[0] * cos - by_wave[1] * sin
        minus = -(by_wave[0] * sin) - by_wave[1] * cos
        left.append(jnp.concatenate([real, minus], axis=1))
    left = jnp.concatenate(left, axis=0)
    high = left.astype(BF16)
    total = dot(jnp.concatenate([high, high], axis=1), table[...])
    if not exact:
        low = (left - high.astype(F32)).astype(BF16)
        total += dot(low, table[: 2 * waves])
    out[...] = total.reshape(sectors, rows, columns).astype(BF16)


def to_sectors(wire, table, turns, one_hot, mirror, share):
    devices, wire_rows, lanes = wire.shape
    rows = mirror.shape[0]
    waves, slots = one_hot.shape
    columns = table.shape[1]
    sectors = turns[0].shape[0]
    together = 2 if sectors % 2 == 0 else 1
    turn_spec = pl.BlockSpec((together, 1, waves), lambda i: (i, 0, 0))
    return pl.pallas_call(
        functools.partial(backward_kernel, sectors in (1, 2, 4)),
        grid=(sectors // together,),
        in_specs=[
            pl.BlockSpec(wire.shape, lambda i: (0, 0, 0)),
            pl.BlockSpec(table.shape, lambda i: (0, 0)),
            turn_spec,
            turn_spec,
            pl.BlockSpec((waves, slots), lambda i: (0, 0)),
            pl.BlockSpec((rows, rows), lambda i: (0, 0)),
        ],
        out_specs=pl.BlockSpec((together, rows, columns), lambda i: (i, 0, 0)),
        out_shape=jax.ShapeDtypeStruct((sectors, rows, columns), BF16),
        scratch_shapes=[pltpu.VMEM((slots, 2 * rows), BF16), pltpu.VMEM((2, rows, waves), F32)],
        cost_estimate=pl.CostEstimate(flops=8 * sectors * rows * columns * waves, bytes_accessed=10**7, transcendentals=0),
        compiler_params=pltpu.CompilerParams(vmem_limit_bytes=VMEM_LIMIT),
        name="to_sectors",
    )(wire, table, *turns, one_hot, mirror)


def round_up(value, unit):
    return -(-value // unit) * unit


def wire_lanes(rows):
    return LANES if 2 * rows % LANES == 0 else 2 * rows


def legendre_kernel(sides, lat_rows, group, first, order, blocks, received, damping, basis, spectral, returned, held, buffer, sems):
    devices, wire_rows, lanes = received.shape
    sectors, share = spectral.shape[:2]
    slots, degrees, half_lat = basis.shape
    sources = devices // sectors
    fields = sides // 2
    combos = sectors * sides
    lane_blocks = held.shape[0]
    stride = held.shape[1] // (2 * combos)
    wire_blocks = wire_rows // share
    groups = share // group
    most = degrees // STEP
    scale = 1.0 / math.sqrt(degrees)

    def copies(index, count):
        ring = lax.rem(index, DEPTH)
        rows = pl.ds(0, count * STEP)
        return [
            pltpu.make_async_copy(
                basis.at[jnp.minimum(first[0] + order[index * group + i], slots - 1), rows, :],
                buffer.at[ring, i, rows, :],
                sems.at[ring, i],
            )
            for i in range(group)
        ]

    def fetch(index):
        for count in range(1, most + 1):

            @pl.when(blocks[index] == count)
            def _():
                for copy in copies(index, count):
                    copy.start()

    for index in range(min(DEPTH - 1, groups)):
        fetch(index)

    def wire_pieces(device, wire_block):
        source, sector = divmod(device, sectors)
        side, near = (0, source) if source < sources // 2 else (1, sources - 1 - source)
        column, end = wire_block * lanes, (wire_block + 1) * lanes
        while column < end:
            part_field, lat = divmod(column, lat_rows)
            part, field = divmod(part_field, fields)
            row = (side * combos + sector * sides + field * 2 + part) * stride
            place = near * lat_rows + lat
            width = min(end - column, lat_rows - lat, LANES - place % LANES)
            yield column - wire_block * lanes, width, row, place // LANES, place % LANES
            column += width

    for device in range(devices):
        own = received[device].astype(F32)
        for wire_block in range(wire_blocks):
            piece = own[wire_block * share : (wire_block + 1) * share]
            for at, width, row, block, lane in wire_pieces(device, wire_block):
                held[block, row : row + share, lane : lane + width] = piece[:, at : at + width]

    def load_slot(slot):
        rows = pl.ds(slot, 2 * combos, stride=stride)
        return jnp.concatenate([held[block, rows, :] for block in range(lane_blocks)], axis=1)

    def store_slot(slot, value):
        rows = pl.ds(slot, 2 * combos, stride=stride)
        for block in range(lane_blocks):
            held[block, rows, :] = value[:, block * LANES : (block + 1) * LANES]

    def one_group(index, count):
        ring = lax.rem(index, DEPTH)
        here = [order[index * group + i] for i in range(group)]
        if count == 0:
            for slot in here:
                for sector in range(sectors):
                    spectral[sector, slot] = jnp.zeros(spectral.shape[2:], F32)
                store_slot(slot, jnp.zeros((2 * combos, half_lat), F32))
            return
        width = count * STEP
        for copy in copies(index, count):
            copy.wait()
        parity = 1.0 - 2.0 * (lax.broadcasted_iota(jnp.int32, (1, width), 1) % 2).astype(F32)
        left = [load_slot(slot).astype(BF16) for slot in here]
        sums = [dot(left[i], buffer[ring, i, :width, :], NT) for i in range(group)]
        damped = [
            (sums[i][:combos] + parity * sums[i][combos:]) * damping[slot, :, :width] for i, slot in enumerate(here)
        ]
        turned = [jnp.concatenate([value, parity * value], axis=0).astype(BF16) for value in damped]
        backs = [dot(turned[i], buffer[ring, i, :width, :]) * scale for i in range(group)]
        for i, slot in enumerate(here):
            for sector in range(sectors):
                spectral[sector, slot, :, :width] = damped[i][sector * sides : (sector + 1) * sides]
                if width < degrees:
                    spectral[sector, slot, :, width:] = jnp.zeros((sides, degrees - width), F32)
        for i, slot in enumerate(here):
            store_slot(slot, backs[i])

    def loop_body(index, carry):
        @pl.when(index + DEPTH - 1 < groups)
        def _():
            fetch(index + DEPTH - 1)

        for count in range(most + 1):
            pl.when(blocks[index] == count)(functools.partial(one_group, index, count))
        return carry

    lax.fori_loop(0, groups, loop_body, 0)

    for device in range(devices):
        pieces = []
        for wire_block in range(wire_blocks):
            parts = [
                held[block, row : row + share, lane : lane + width]
                for _, width, row, block, lane in wire_pieces(device, wire_block)
            ]
            pieces.append(jnp.concatenate(parts, axis=1) if len(parts) > 1 else parts[0])
        returned[device] = jnp.concatenate(pieces, axis=0).astype(BF16)


def legendre(received, basis, damping, first, order, blocks, sectors, sides, lat_rows, group):
    share = order.shape[0]
    degrees, half_lat = basis.shape[1:]
    combos = sectors * sides
    smem, vmem, hbm = (pl.BlockSpec(memory_space=space) for space in (pltpu.SMEM, pltpu.VMEM, pl.ANY))
    return pl.pallas_call(
        functools.partial(legendre_kernel, sides, lat_rows, group),
        in_specs=[smem, smem, smem, vmem, vmem, hbm],
        out_specs=[vmem, vmem],
        out_shape=[
            jax.ShapeDtypeStruct((sectors, share, sides, degrees), F32),
            jax.ShapeDtypeStruct(received.shape, BF16),
        ],
        scratch_shapes=[
            pltpu.VMEM((half_lat // LANES, 2 * combos * round_up(share, 8), LANES), F32),
            pltpu.VMEM((DEPTH, group, degrees, half_lat), BF16),
            pltpu.SemaphoreType.DMA((DEPTH, group)),
        ],
        cost_estimate=pl.CostEstimate(
            flops=4 * share * degrees * half_lat * 2 * combos,
            bytes_accessed=2 * share * degrees * half_lat,
            transcendentals=0,
        ),
        compiler_params=pltpu.CompilerParams(vmem_limit_bytes=VMEM_LIMIT),
        name="legendre",
    )(first, order, blocks, received, damping, basis)


def degree_order(counts):
    size = counts.shape[0]
    ids = jnp.arange(size, dtype=jnp.int32)
    ahead = (counts[None, :] > counts[:, None]) | ((counts[None, :] == counts[:, None]) & (ids[None, :] < ids[:, None]))
    rank = jnp.sum(ahead.astype(jnp.int32), axis=1)
    placed = rank[:, None] == ids[None, :]
    order = jnp.sum(jnp.where(placed, ids[:, None], 0), axis=0)
    sorted_counts = jnp.sum(jnp.where(placed, counts[:, None], 0), axis=0)
    group = max(g for g in range(1, 6) if size % g == 0)
    return order, (sorted_counts[::group] + (STEP - 1)) // STEP, group


def body(wind_u, wind_v, basis, wave_slots, degree_count, viscosity):
    sectors = lax.axis_size("lon")
    owners = lax.axis_size("lat")
    sector_index = lax.axis_index("lon")
    owner_index = lax.axis_index("lat")
    levels, lat_rows, lon_cols = wind_u.shape
    capacity, degrees, half_lat = basis.shape
    waves = wave_slots.shape[0]
    slot_total = capacity * owners
    level_dev = levels // sectors
    fields = 2 * level_dev
    rows = fields * lat_rows
    share = -(-capacity // sectors)
    padded = round_up(share, 8)
    products = jnp.stack([wind_u * wind_v, wind_u * wind_u - wind_v * wind_v], axis=1)
    products = products.astype(BF16).reshape(sectors, rows, lon_cols)
    lines = lax.all_to_all(products, "lon", split_axis=0, concat_axis=0, tiled=True)

    slot_ids = jnp.arange(slot_total, dtype=jnp.int32)
    matches = wave_slots[:, None] == slot_ids[None, :]
    wave_ids = jnp.arange(waves, dtype=jnp.int32)
    wave_of_slot = jnp.sum(jnp.where(matches, wave_ids[:, None] + 1, 0), axis=0) - 1
    count_of_slot = jnp.sum(jnp.where(matches, degree_count[:, None], 0), axis=0)
    places = jnp.arange(owners * sectors * padded, dtype=jnp.int32)
    place_owner, place_sector, place_slot = places // (sectors * padded), places // padded % sectors, places % padded
    in_owner = place_sector * share + place_slot
    named = jnp.where((place_slot < share) & (in_owner < capacity), place_owner * capacity + in_owner, -1)
    one_hot = (named[:, None] == wave_slots[None, :]).astype(BF16)
    one_hot_turned = (wave_slots[:, None] == named[None, :]).astype(BF16)
    row_ids = jnp.arange(rows, dtype=jnp.int32)
    mirrored = row_ids // lat_rows * lat_rows + (lat_rows - 1 - row_ids % lat_rows)
    south = owner_index >= owners // 2
    mirror = (row_ids[:, None] == jnp.where(south, mirrored, row_ids)[None, :]).astype(BF16)
    forward_table, backward_table = wave_tables(sectors, lon_cols, waves)
    turns = tuple(jnp.asarray(turn) for turn in sector_turns(sectors, waves))

    first = sector_index * share
    local_ids = jnp.arange(share, dtype=jnp.int32)
    inside = first + local_ids < capacity
    at = owner_index * capacity + jnp.minimum(first + local_ids, capacity - 1)
    here = at[:, None] == slot_ids[None, :]
    wave_here = jnp.sum(jnp.where(here, wave_of_slot[None, :], 0), axis=1)
    count_here = jnp.where(inside, jnp.sum(jnp.where(here, count_of_slot[None, :], 0), axis=1), 0)
    degree_ids = jnp.arange(degrees, dtype=jnp.int32)
    total_degree = wave_here[:, None] + degree_ids[None, :]
    scaled = (total_degree * (total_degree + 1)).astype(F32) / float(degrees * (degrees + 1))
    kept = degree_ids[None, :] < count_here[:, None]
    sides = 2 * fields
    rates = jnp.repeat(viscosity, 4)
    damping = 1.0 / (1.0 + rates[None, :, None] * (scaled * scaled)[:, None, :])
    damping = jnp.where(kept[:, None, :], damping * (1.0 / math.sqrt(2 * half_lat)), 0.0)
    order, blocks, group = degree_order(count_here)
    lines, forward_table, backward_table, one_hot, one_hot_turned, mirror, damping, order, blocks = lax.optimization_barrier(
        (lines, forward_table, backward_table, one_hot, one_hot_turned, mirror, damping, order, blocks)
    )

    fourier = to_owners(lines, forward_table, turns, one_hot, mirror, share)
    received = lax.all_to_all(fourier, ("lat", "lon"), split_axis=0, concat_axis=0, tiled=True)
    spectral, returned = legendre(
        received, basis, damping, first[None], order, blocks, sectors, sides, lat_rows, group
    )
    regrouped = lax.all_to_all(returned, ("lat", "lon"), split_axis=0, concat_axis=0, tiled=True)
    spectral = lax.all_to_all(spectral.astype(BF16), "lon", split_axis=0, concat_axis=0, tiled=True)
    spectral = spectral.reshape(sectors * share, level_dev, 2, 2, degrees)[:capacity].astype(F32)
    grid_lines = to_sectors(regrouped, backward_table, turns, one_hot_turned, mirror, share)
    tendency = lax.all_to_all(grid_lines, "lon", split_axis=0, concat_axis=0, tiled=True)
    return spectral, tendency.astype(F32).reshape(levels, 2, lat_rows, lon_cols)


def solution(mesh):
    return jax.shard_map(
        body,
        mesh=mesh,
        in_specs=(
            P(None, "lat", "lon"),
            P(None, "lat", "lon"),
            P("lat", None, None),
            P(),
            P(),
            P(),
        ),
        out_specs=(P("lat", "lon", None, None, None), P(None, None, "lat", "lon")),
        check_vma=False,
    )
```

```python
import functools
import math

import jax
import jax.numpy as jnp
import numpy as np
from jax import lax
from jax.experimental import pallas as pl
from jax.experimental.pallas import tpu as pltpu
from jax.sharding import PartitionSpec as P

BF16 = jnp.bfloat16
F32 = jnp.float32
VMEM_LIMIT = 60 * 1024 * 1024
STEP = 128
LANES = 128
DEPTH = 3
NT = (((1,), (1,)), ((), ()))
NN = (((1,), (0,)), ((), ()))


def dot(a, b, dims=NN):
    return lax.dot_general(a, b, dims, preferred_element_type=F32)


def phases(rows, columns, length):
    turns = 2.0 * np.pi * (rows[:, None] * columns[None, :] % length) / length
    return np.cos(turns), np.sin(turns)


def table_kernel(interleaved, near_cos, near_sin, far_cos, far_sin, out):
    near, lanes = near_cos.shape
    count = far_cos.shape[0] * near
    size = min(LANES, lanes)
    for step in range(far_cos.shape[0]):
        cos = far_cos[step] * near_cos[...] - far_sin[step] * near_sin[...]
        sin = far_sin[step] * near_cos[...] + far_cos[step] * near_sin[...]
        high = (cos.astype(BF16), sin.astype(BF16))
        low = tuple((value - top.astype(F32)).astype(BF16) for value, top in zip((cos, sin), high))
        for term, pair in enumerate((high, low)):
            for which, value in enumerate(pair):
                if interleaved:
                    row = term * count + step * near
                    for block in range(lanes // size):
                        lane = (2 * block + which) * size
                        out[row : row + near, lane : lane + size] = value[:, block * size : (block + 1) * size]
                else:
                    row = (2 * term + which) * count + step * near
                    out[row : row + near, :] = value


def wave_table(rows, columns, length, interleaved):
    near = 32
    near_cos, near_sin = phases(np.arange(near), np.arange(columns), length)
    far_cos, far_sin = phases(np.arange(rows // near) * near, np.arange(columns), length)
    scaling = 1.0 / math.sqrt(length)
    shape = (2 * rows, 2 * columns) if interleaved else (4 * rows, columns)
    return pl.pallas_call(
        functools.partial(table_kernel, interleaved),
        out_shape=jax.ShapeDtypeStruct(shape, BF16),
        compiler_params=pltpu.CompilerParams(vmem_limit_bytes=VMEM_LIMIT),
        name="wave_table",
    )(
        jnp.asarray(near_cos * scaling, F32),
        jnp.asarray(near_sin * scaling, F32),
        jnp.asarray(far_cos[:, None, :], F32),
        jnp.asarray(far_sin[:, None, :], F32),
    )


def sector_turns(sectors, waves):
    both = phases(np.arange(sectors), np.arange(waves), sectors)
    return tuple(jnp.asarray(np.round(turn, 12)[:, None, :], F32) for turn in both)


def product_kernel(count, chosen, *refs):
    winds, outs = refs[: 2 * count], refs[2 * count :]
    for i in range(count):
        u, v = winds[2 * i][0], winds[2 * i + 1][0]
        lat_rows = u.shape[0]
        outs[i][:lat_rows] = (u * v).astype(BF16)
        outs[i][lat_rows:] = (u * u - v * v).astype(BF16)


def wind_products(wind_u, wind_v, chosen):
    _, lat_rows, columns = wind_u.shape
    count = chosen.shape[0]
    specs = [
        pl.BlockSpec((1, lat_rows, columns), functools.partial(lambda i, step, chosen: (chosen[i], 0, 0), i))
        for i in range(count)
        for _ in range(2)
    ]
    return pl.pallas_call(
        functools.partial(product_kernel, count),
        grid_spec=pltpu.PrefetchScalarGridSpec(
            num_scalar_prefetch=1,
            grid=(1,),
            in_specs=specs,
            out_specs=[pl.BlockSpec((2 * lat_rows, columns), lambda step, chosen: (0, 0))] * count,
        ),
        out_shape=[jax.ShapeDtypeStruct((2 * lat_rows, columns), BF16)] * count,
        compiler_params=pltpu.CompilerParams(vmem_limit_bytes=VMEM_LIMIT),
        name="wind_products",
    )(chosen, *[wind_u, wind_v] * count)


def forward_kernel(count, begun, ends, *refs):
    lines, refs = refs[:count], refs[count:]
    table, turn_cos, turn_sin = refs[:3]
    earlier, refs = (refs[3], refs[4:]) if begun else (None, refs[3:])
    step = pl.program_id(0)
    size = table.shape[1] // 2
    rows = lines[0].shape[0]
    both = jnp.concatenate([jnp.concatenate([line[...]] * 2, axis=1) for line in lines], axis=0)
    sums = dot(both, table[...])
    real, imag = (earlier[0], earlier[1]) if begun else (None, None)
    for i in range(count):
        own = sums[i * rows : (i + 1) * rows]
        own_cos, own_sin = own[:, :size], own[:, size:]
        cos, sin = turn_cos[i], turn_sin[i]
        own_real, own_imag = own_cos * cos - own_sin * sin, own_cos * sin + own_sin * cos
        real, imag = (own_real, own_imag) if real is None else (real + own_real, imag + own_imag)
    if not ends:
        refs[0][0], refs[0][1] = real, imag
        return
    one_hot, mirror, out, by_wave, by_slot = refs
    devices, wire_rows, lanes = out.shape
    padded = one_hot.shape[0] // devices
    blocks = 2 * rows // lanes
    share = wire_rows // blocks
    place = pl.ds(pl.multiple_of(step * size, size), size)
    by_wave[0, :, place] = real.astype(BF16)
    by_wave[1, :, place] = (-imag).astype(BF16)

    @pl.when(step == pl.num_programs(0) - 1)
    def _():
        for part in range(2):
            turned = dot(mirror[...], by_wave[part]).astype(BF16)
            by_slot[:, part * rows : (part + 1) * rows] = dot(one_hot[...], turned, NT)
        for device in range(devices):
            own = by_slot[device * padded : (device + 1) * padded, :]
            out[device] = jnp.concatenate(
                [own[:share, block * lanes : (block + 1) * lanes] for block in range(blocks)], axis=0
            ).astype(BF16)


def forward(lines, table, turns, earlier=None, end=None):
    rows, columns = lines[0].shape
    waves = table.shape[1] // 2
    size = min(LANES, waves)
    turn_spec = pl.BlockSpec((len(lines), 1, size), lambda i: (0, 0, i))
    sum_spec = pl.BlockSpec((2, rows, size), lambda i: (0, 0, i))
    args = list(lines) + [table, *turns]
    in_specs = [pl.BlockSpec((rows, columns), lambda i: (0, 0))] * len(lines)
    in_specs += [pl.BlockSpec((2 * columns, 2 * size), lambda i: (0, i)), turn_spec, turn_spec]
    if earlier is not None:
        args.append(earlier)
        in_specs.append(sum_spec)
    if end is None:
        out_shape, out_spec, scratch = jax.ShapeDtypeStruct((2, rows, waves), F32), sum_spec, []
    else:
        one_hot, mirror, share = end
        slots = one_hot.shape[0]
        lanes = wire_lanes(rows)
        out = (slots // round_up(share, 8), share * (2 * rows // lanes), lanes)
        args += [one_hot, mirror]
        in_specs += [pl.BlockSpec((slots, waves), lambda i: (0, 0)), pl.BlockSpec((rows, rows), lambda i: (0, 0))]
        out_shape, out_spec = jax.ShapeDtypeStruct(out, BF16), pl.BlockSpec(out, lambda i: (0, 0, 0))
        scratch = [pltpu.VMEM((2, rows, waves), BF16), pltpu.VMEM((slots, 2 * rows), F32)]
    return pl.pallas_call(
        functools.partial(forward_kernel, len(lines), earlier is not None, end is not None),
        grid=(waves // size,),
        in_specs=in_specs,
        out_specs=out_spec,
        out_shape=out_shape,
        scratch_shapes=scratch,
        cost_estimate=pl.CostEstimate(
            flops=8 * len(lines) * rows * columns * waves, bytes_accessed=10**7, transcendentals=0
        ),
        compiler_params=pltpu.CompilerParams(vmem_limit_bytes=VMEM_LIMIT),
        name="forward",
    )(*args)


def sector_lines(exact, by_wave, table, turn_cos, turn_sin):
    count = turn_cos.shape[0]
    left = []
    for i in range(count):
        cos, sin = turn_cos[i], turn_sin[i]
        real = by_wave[0] * cos - by_wave[1] * sin
        minus = -(by_wave[0] * sin) - by_wave[1] * cos
        left.append(jnp.concatenate([real, minus], axis=1))
    left = jnp.concatenate(left, axis=0) if count > 1 else left[0]
    high = left.astype(BF16)
    total = dot(jnp.concatenate([high, high], axis=1), table[...])
    if not exact:
        low = (left - high.astype(F32)).astype(BF16)
        total += dot(low, table[: low.shape[1]])
    return total.astype(BF16)


def backward_first_kernel(exact, wire, table_hbm, turn_cos, turn_sin, one_hot, mirror, out, by_wave, by_slot, table, sem):
    table_copy = pltpu.make_async_copy(table_hbm, table, sem)
    table_copy.start()
    devices, wire_rows, lanes = wire.shape
    rows = out.shape[0]
    waves = one_hot.shape[0]
    padded = by_slot.shape[0] // devices
    blocks = 2 * rows // lanes
    share = wire_rows // blocks
    for device in range(devices):
        own = wire[device].astype(F32)
        for block in range(blocks):
            piece = own[block * share : (block + 1) * share]
            if padded > share:
                piece = jnp.concatenate([piece, jnp.zeros((padded - share, lanes), F32)], axis=0)
            by_slot[device * padded : (device + 1) * padded, block * lanes : (block + 1) * lanes] = piece.astype(BF16)
    wave_ids = lax.broadcasted_iota(jnp.int32, (1, waves), 1)
    weight = jnp.where(wave_ids == 0, 1.0, 2.0).astype(F32)
    for part in range(2):
        ordered = dot(one_hot[...], by_slot[:, part * rows : (part + 1) * rows]).astype(BF16)
        by_wave[part] = dot(mirror[...], ordered, NT) * weight
    table_copy.wait()
    out[...] = sector_lines(exact, by_wave, table, turn_cos, turn_sin)


def backward_first(wire, table, turns, one_hot, mirror, exact):
    rows = mirror.shape[0]
    waves, slots = one_hot.shape
    vmem, hbm = pl.BlockSpec(memory_space=pltpu.VMEM), pl.BlockSpec(memory_space=pl.ANY)
    return pl.pallas_call(
        functools.partial(backward_first_kernel, exact),
        in_specs=[vmem, hbm, vmem, vmem, vmem, vmem],
        out_specs=[vmem, vmem],
        out_shape=[
            jax.ShapeDtypeStruct((rows, table.shape[1]), BF16),
            jax.ShapeDtypeStruct((2, rows, waves), F32),
        ],
        scratch_shapes=[
            pltpu.VMEM((slots, 2 * rows), BF16),
            pltpu.VMEM(table.shape, BF16),
            pltpu.SemaphoreType.DMA,
        ],
        cost_estimate=pl.CostEstimate(flops=10**9, bytes_accessed=10**7, transcendentals=0),
        compiler_params=pltpu.CompilerParams(vmem_limit_bytes=VMEM_LIMIT),
        name="backward_first",
    )(wire, table, *turns, one_hot, mirror)


def backward_rest_kernel(exact, by_wave, table, turn_cos, turn_sin, *outs):
    rows = outs[0].shape[0]
    total = sector_lines(exact, by_wave, table, turn_cos, turn_sin)
    for i, out in enumerate(outs):
        out[...] = total[i * rows : (i + 1) * rows]


def backward_rest(by_wave, table, turns, exact):
    _, rows, _ = by_wave.shape
    count = turns[0].shape[0]
    vmem = pl.BlockSpec(memory_space=pltpu.VMEM)
    return pl.pallas_call(
        functools.partial(backward_rest_kernel, exact),
        in_specs=[vmem] * 4,
        out_specs=[vmem] * count,
        out_shape=[jax.ShapeDtypeStruct((rows, table.shape[1]), BF16)] * count,
        cost_estimate=pl.CostEstimate(flops=3 * 10**9, bytes_accessed=10**7, transcendentals=0),
        compiler_params=pltpu.CompilerParams(vmem_limit_bytes=VMEM_LIMIT),
        name="backward_rest",
    )(by_wave, table, *turns)


def placing_kernel(count, chosen, *refs):
    blocks, (out, wide, sems) = refs[:count], refs[-3:]
    copies = []
    for i in range(count):
        wide[i] = blocks[i][...].astype(F32)
        copies.append(pltpu.make_async_copy(wide.at[i], out.at[chosen[i]], sems.at[i]))
        copies[-1].start()
    for copy in copies:
        copy.wait()


def placed(blocks, chosen, total, earlier=None):
    count = len(blocks)
    shape = blocks[0].shape
    smem, vmem, hbm = (pl.BlockSpec(memory_space=space) for space in (pltpu.SMEM, pltpu.VMEM, pl.ANY))
    more = () if earlier is None else (earlier,)
    return pl.pallas_call(
        functools.partial(placing_kernel, count),
        in_specs=[smem] + [vmem] * count + [hbm] * len(more),
        out_specs=hbm,
        out_shape=jax.ShapeDtypeStruct((total,) + shape, F32),
        scratch_shapes=[pltpu.VMEM((count,) + shape, F32), pltpu.SemaphoreType.DMA((count,))],
        input_output_aliases={1 + count: 0} if more else {},
        compiler_params=pltpu.CompilerParams(vmem_limit_bytes=VMEM_LIMIT),
        name="placed",
    )(chosen, *blocks, *more)


def round_up(value, unit):
    return -(-value // unit) * unit


def wire_lanes(rows):
    return LANES if 2 * rows % LANES == 0 else 2 * rows


def legendre_kernel(sides, lat_rows, group, place, order, blocks, received, damping, basis, spectral, returned, held, buffer, sems):
    devices, wire_rows, lanes = received.shape
    sectors, share = spectral.shape[:2]
    slots, degrees, half_lat = basis.shape
    sources = devices // sectors
    fields = sides // 2
    combos = sectors * sides
    lane_blocks = held.shape[0]
    stride = held.shape[1] // (2 * combos)
    wire_blocks = wire_rows // share
    groups = share // group
    most = degrees // STEP
    scale = 1.0 / math.sqrt(degrees)

    def copies(index, count):
        ring = lax.rem(index, DEPTH)
        rows = pl.ds(0, count * STEP)
        return [
            pltpu.make_async_copy(
                basis.at[jnp.minimum(place[0] + order[index * group + i], slots - 1), rows, :],
                buffer.at[ring, i, rows, :],
                sems.at[ring, i],
            )
            for i in range(group)
        ]

    def fetch(index):
        for count in range(1, most + 1):

            @pl.when(blocks[index] == count)
            def _():
                for copy in copies(index, count):
                    copy.start()

    for index in range(min(DEPTH - 1, groups)):
        fetch(index)

    def wire_pieces(device, wire_block):
        source, sector = divmod(device, sectors)
        side, near = (0, source) if source < sources // 2 else (1, sources - 1 - source)
        column, end = wire_block * lanes, (wire_block + 1) * lanes
        while column < end:
            part_field, lat = divmod(column, lat_rows)
            part, field = divmod(part_field, fields)
            row = (side * combos + sector * sides + field * 2 + part) * stride
            place = near * lat_rows + lat
            width = min(end - column, lat_rows - lat, LANES - place % LANES)
            yield column - wire_block * lanes, width, row, place // LANES, place % LANES
            column += width

    for device in range(devices):
        own = received[device].astype(F32)
        for wire_block in range(wire_blocks):
            piece = own[wire_block * share : (wire_block + 1) * share]
            for at, width, row, block, lane in wire_pieces(device, wire_block):
                held[block, row : row + share, lane : lane + width] = piece[:, at : at + width]

    def load_slot(slot):
        rows = pl.ds(slot, 2 * combos, stride=stride)
        return jnp.concatenate([held[block, rows, :] for block in range(lane_blocks)], axis=1)

    def store_slot(slot, value):
        rows = pl.ds(slot, 2 * combos, stride=stride)
        for block in range(lane_blocks):
            held[block, rows, :] = value[:, block * LANES : (block + 1) * LANES]

    def one_group(index, count):
        ring = lax.rem(index, DEPTH)
        here = [order[index * group + i] for i in range(group)]
        if count == 0:
            for slot in here:
                for sector in range(sectors):
                    spectral[place[1] ^ sector, slot] = jnp.zeros(spectral.shape[2:], F32)
                store_slot(slot, jnp.zeros((2 * combos, half_lat), F32))
            return
        width = count * STEP
        for copy in copies(index, count):
            copy.wait()
        parity = 1.0 - 2.0 * (lax.broadcasted_iota(jnp.int32, (1, width), 1) % 2).astype(F32)
        left = [load_slot(slot).astype(BF16) for slot in here]
        sums = [dot(left[i], buffer[ring, i, :width, :], NT) for i in range(group)]
        damped = [
            (sums[i][:combos] + parity * sums[i][combos:]) * damping[slot, :, :width] for i, slot in enumerate(here)
        ]
        turned = [jnp.concatenate([value, parity * value], axis=0).astype(BF16) for value in damped]
        backs = [dot(turned[i], buffer[ring, i, :width, :]) * scale for i in range(group)]
        for i, slot in enumerate(here):
            for sector in range(sectors):
                spectral[place[1] ^ sector, slot, :, :width] = damped[i][sector * sides : (sector + 1) * sides]
                if width < degrees:
                    spectral[place[1] ^ sector, slot, :, width:] = jnp.zeros((sides, degrees - width), F32)
        for i, slot in enumerate(here):
            store_slot(slot, backs[i])

    def loop_body(index, carry):
        @pl.when(index + DEPTH - 1 < groups)
        def _():
            fetch(index + DEPTH - 1)

        for count in range(most + 1):
            pl.when(blocks[index] == count)(functools.partial(one_group, index, count))
        return carry

    lax.fori_loop(0, groups, loop_body, 0)

    for device in range(devices):
        pieces = []
        for wire_block in range(wire_blocks):
            parts = [
                held[block, row : row + share, lane : lane + width]
                for _, width, row, block, lane in wire_pieces(device, wire_block)
            ]
            pieces.append(jnp.concatenate(parts, axis=1) if len(parts) > 1 else parts[0])
        returned[device] = jnp.concatenate(pieces, axis=0).astype(BF16)


def legendre(received, basis, damping, place, order, blocks, sectors, sides, lat_rows, group):
    share = order.shape[0]
    degrees, half_lat = basis.shape[1:]
    combos = sectors * sides
    smem, vmem, hbm = (pl.BlockSpec(memory_space=space) for space in (pltpu.SMEM, pltpu.VMEM, pl.ANY))
    return pl.pallas_call(
        functools.partial(legendre_kernel, sides, lat_rows, group),
        in_specs=[smem, smem, smem, vmem, vmem, hbm],
        out_specs=[vmem, vmem],
        out_shape=[
            jax.ShapeDtypeStruct((sectors, share, sides, degrees), F32),
            jax.ShapeDtypeStruct(received.shape, BF16),
        ],
        scratch_shapes=[
            pltpu.VMEM((half_lat // LANES, 2 * combos * round_up(share, 8), LANES), F32),
            pltpu.VMEM((DEPTH, group, degrees, half_lat), BF16),
            pltpu.SemaphoreType.DMA((DEPTH, group)),
        ],
        cost_estimate=pl.CostEstimate(
            flops=4 * share * degrees * half_lat * 2 * combos,
            bytes_accessed=2 * share * degrees * half_lat,
            transcendentals=0,
        ),
        compiler_params=pltpu.CompilerParams(vmem_limit_bytes=VMEM_LIMIT),
        name="legendre",
    )(place, order, blocks, received, damping, basis)


def degree_order(counts):
    size = counts.shape[0]
    ids = jnp.arange(size, dtype=jnp.int32)
    ahead = (counts[None, :] > counts[:, None]) | ((counts[None, :] == counts[:, None]) & (ids[None, :] < ids[:, None]))
    rank = jnp.sum(ahead.astype(jnp.int32), axis=1)
    placed = rank[:, None] == ids[None, :]
    order = jnp.sum(jnp.where(placed, ids[:, None], 0), axis=0)
    sorted_counts = jnp.sum(jnp.where(placed, counts[:, None], 0), axis=0)
    group = max(g for g in range(1, 6) if size % g == 0)
    return order, (sorted_counts[::group] + (STEP - 1)) // STEP, group


def body(wind_u, wind_v, basis, wave_slots, degree_count, viscosity):
    sectors = lax.axis_size("lon")
    owners = lax.axis_size("lat")
    sector_index = lax.axis_index("lon")
    owner_index = lax.axis_index("lat")
    levels, lat_rows, lon_cols = wind_u.shape
    capacity, degrees, half_lat = basis.shape
    waves = wave_slots.shape[0]
    slot_total = capacity * owners
    assert levels == sectors and sectors & (sectors - 1) == 0
    rows = 2 * lat_rows
    share = -(-capacity // sectors)
    padded = round_up(share, 8)
    length = sectors * lon_cols
    masks = [sectors // 2] + [mask for mask in range(sectors - 1, 0, -1) if mask != sectors // 2] + [0]

    def across(value, mask):
        return lax.ppermute(value, "lon", [(i, i ^ mask) for i in range(sectors)]) if mask else value

    def partners(some):
        return jnp.stack([sector_index ^ mask for mask in some]).astype(jnp.int32)

    far, rest = masks[:1], masks[1:]
    sent = list(wind_products(wind_u, wind_v, partners(far))) + list(wind_products(wind_u, wind_v, partners(rest)))
    lines = {mask: across(value, mask) for mask, value in zip(masks, sent)}

    slot_ids = jnp.arange(slot_total, dtype=jnp.int32)
    wave_ids = jnp.arange(waves, dtype=jnp.int32)
    places = jnp.arange(owners * sectors * padded, dtype=jnp.int32)
    place_owner, place_sector, place_slot = places // (sectors * padded), places // padded % sectors, places % padded
    in_owner = place_sector * share + place_slot
    named = jnp.where((place_slot < share) & (in_owner < capacity), place_owner * capacity + in_owner, -1)
    one_hot = (named[:, None] == wave_slots[None, :]).astype(BF16)
    one_hot_turned = (wave_slots[:, None] == named[None, :]).astype(BF16)
    row_ids = jnp.arange(rows, dtype=jnp.int32)
    mirrored = row_ids // lat_rows * lat_rows + (lat_rows - 1 - row_ids % lat_rows)
    south = owner_index >= owners // 2
    mirror = (row_ids[:, None] == jnp.where(south, mirrored, row_ids)[None, :]).astype(BF16)
    forward_table = wave_table(lon_cols, waves, length, True)
    backward_table = wave_table(waves, lon_cols, length, False)
    turns = sector_turns(sectors, waves)

    def turns_of(some):
        at = partners(some)
        return tuple(jnp.take(turn, at, axis=0) for turn in turns)

    first = sector_index * share
    local_ids = jnp.arange(share, dtype=jnp.int32)
    inside = first + local_ids < capacity
    at = owner_index * capacity + jnp.minimum(first + local_ids, capacity - 1)
    here = at[:, None] == wave_slots[None, :]
    wave_here = jnp.sum(jnp.where(here, wave_ids[None, :], 0), axis=1)
    count_here = jnp.where(inside, jnp.sum(jnp.where(here, degree_count[None, :], 0), axis=1), 0)
    degree_ids = jnp.arange(degrees, dtype=jnp.int32)
    total_degree = wave_here[:, None] + degree_ids[None, :]
    scaled = (total_degree * (total_degree + 1)).astype(F32) / float(degrees * (degrees + 1))
    kept = degree_ids[None, :] < count_here[:, None]
    sides = 4
    rates = jnp.repeat(viscosity, sides)
    damping = 1.0 / (1.0 + rates[None, :, None] * (scaled * scaled)[:, None, :])
    damping = jnp.where(kept[:, None, :], damping * (1.0 / math.sqrt(2 * half_lat)), 0.0)
    order, blocks, group = degree_order(count_here)

    by_arrival = [0, *[mask for mask in reversed(masks) if mask and mask < sectors // 2], *masks]
    by_arrival = list(dict.fromkeys(by_arrival))
    early, late = by_arrival[:-1], by_arrival[-1:]
    sums = forward([lines[mask] for mask in early], forward_table, turns_of(early))
    fourier = forward([lines[mask] for mask in late], forward_table, turns_of(late), sums, (one_hot, mirror, share))
    received = lax.all_to_all(fourier, ("lat", "lon"), split_axis=0, concat_axis=0, tiled=True)
    place = jnp.stack([first, sector_index]).astype(jnp.int32)
    spectral, returned = legendre(
        received, basis, damping, place, order, blocks, sectors, sides, lat_rows, group
    )
    regrouped = lax.all_to_all(returned, ("lat", "lon"), split_axis=0, concat_axis=0, tiled=True)

    coefficients = jnp.zeros((sectors * share, 1, 2, 2, degrees), F32)
    for mask in masks:
        own = across(spectral[mask].astype(BF16), mask).astype(F32).reshape(share, 1, 2, 2, degrees)
        coefficients = lax.dynamic_update_slice_in_dim(coefficients, own, (sector_index ^ mask) * share, 0)

    exact = sectors in (1, 2, 4)
    far_lines, by_wave = backward_first(regrouped, backward_table, turns_of(far), one_hot_turned, mirror, exact)
    made = [far_lines, *backward_rest(by_wave, backward_table, turns_of(rest), exact)]
    back = {mask: across(value, mask) for mask, value in zip(masks, made)}
    tendency = placed([back[mask] for mask in early], partners(early), sectors)
    tendency = placed([back[mask] for mask in late], partners(late), sectors, tendency)
    return coefficients[:capacity], tendency.reshape(levels, 2, lat_rows, lon_cols)


def solution(mesh):
    return jax.shard_map(
        body,
        mesh=mesh,
        in_specs=(
            P(None, "lat", "lon"),
            P(None, "lat", "lon"),
            P("lat", None, None),
            P(),
            P(),
            P(),
        ),
        out_specs=(P("lat", "lon", None, None, None), P(None, None, "lat", "lon")),
        check_vma=False,
    )
```

```python
import functools
import math

import jax
import jax.numpy as jnp
import numpy as np
from jax import lax
from jax.experimental import pallas as pl
from jax.experimental.pallas import tpu as pltpu
from jax.sharding import PartitionSpec as P


BF16 = jnp.bfloat16
F32 = jnp.float32
MIB = 1024 * 1024
VMEM_LIMIT = 24 * MIB
LEGENDRE_LIMIT = 36 * MIB
WHOLE_LIMIT = 60 * MIB
STEP = 128
LANES = 128
DEPTH = 3
NT = (((1,), (1,)), ((), ()))
NN = (((1,), (0,)), ((), ()))


def dot(a, b, dims=NN):
    return lax.dot_general(a, b, dims, preferred_element_type=F32)


def phases(rows, columns, length):
    turns = 2.0 * np.pi * (rows[:, None] * columns[None, :] % length) / length
    return np.cos(turns), np.sin(turns)


def table_kernel(interleaved, near_cos, near_sin, far_cos, far_sin, out):
    near, lanes = near_cos.shape
    count = far_cos.shape[0] * near
    size = min(LANES, lanes)
    for step in range(far_cos.shape[0]):
        cos = far_cos[step] * near_cos[...] - far_sin[step] * near_sin[...]
        sin = far_sin[step] * near_cos[...] + far_cos[step] * near_sin[...]
        high = (cos.astype(BF16), sin.astype(BF16))
        low = tuple((value - top.astype(F32)).astype(BF16) for value, top in zip((cos, sin), high))
        for term, pair in enumerate((high, low)):
            for which, value in enumerate(pair):
                if interleaved:
                    row = term * count + step * near
                    for block in range(lanes // size):
                        lane = (2 * block + which) * size
                        out[row : row + near, lane : lane + size] = value[:, block * size : (block + 1) * size]
                else:
                    row = (2 * term + which) * count + step * near
                    out[row : row + near, :] = value


def wave_table(rows, columns, length, interleaved):
    near = 32
    near_cos, near_sin = phases(np.arange(near), np.arange(columns), length)
    far_cos, far_sin = phases(np.arange(rows // near) * near, np.arange(columns), length)
    scaling = 1.0 / math.sqrt(length)
    shape = (2 * rows, 2 * columns) if interleaved else (4 * rows, columns)
    return pl.pallas_call(
        functools.partial(table_kernel, interleaved),
        out_shape=jax.ShapeDtypeStruct(shape, BF16),
        compiler_params=pltpu.CompilerParams(vmem_limit_bytes=WHOLE_LIMIT),
        name="wave_table",
    )(
        jnp.asarray(near_cos * scaling, F32),
        jnp.asarray(near_sin * scaling, F32),
        jnp.asarray(far_cos[:, None, :], F32),
        jnp.asarray(far_sin[:, None, :], F32),
    )


def sector_turns(sectors, waves):
    both = phases(np.arange(sectors), np.arange(waves), sectors)
    return tuple(jnp.asarray(np.round(turn, 12)[:, None, :], F32) for turn in both)


def product_kernel(count, chosen, mirror, *refs):
    winds, outs = refs[: 2 * count], refs[2 * count :]
    for i in range(count):
        u, v = winds[2 * i][0], winds[2 * i + 1][0]
        lat_rows = u.shape[0]
        outs[i][:lat_rows] = dot(mirror[...], (u * v).astype(BF16)).astype(BF16)
        outs[i][lat_rows:] = dot(mirror[...], (u * u - v * v).astype(BF16)).astype(BF16)


def wind_products(wind_u, wind_v, mirror, chosen):
    _, lat_rows, columns = wind_u.shape
    count = chosen.shape[0]
    specs = [
        pl.BlockSpec((1, lat_rows, columns), functools.partial(lambda i, step, chosen: (chosen[i], 0, 0), i))
        for i in range(count)
        for _ in range(2)
    ]
    return pl.pallas_call(
        functools.partial(product_kernel, count),
        grid_spec=pltpu.PrefetchScalarGridSpec(
            num_scalar_prefetch=1,
            grid=(1,),
            in_specs=[pl.BlockSpec((lat_rows, lat_rows), lambda step, chosen: (0, 0))] + specs,
            out_specs=[pl.BlockSpec((2 * lat_rows, columns), lambda step, chosen: (0, 0))] * count,
        ),
        out_shape=[jax.ShapeDtypeStruct((2 * lat_rows, columns), BF16)] * count,
        compiler_params=pltpu.CompilerParams(vmem_limit_bytes=WHOLE_LIMIT),
        name="wind_products",
    )(chosen, mirror, *[wind_u, wind_v] * count)


def forward_kernel(count, begun, ends, *refs):
    lines, refs = refs[:count], refs[count:]
    table, turn_cos, turn_sin = refs[:3]
    earlier, refs = (refs[3], refs[4:]) if begun else (None, refs[3:])
    step = pl.program_id(0)
    size = table.shape[1] // 2
    rows = lines[0].shape[0]
    both = jnp.concatenate([jnp.concatenate([line[...]] * 2, axis=1) for line in lines], axis=0)
    sums = dot(both, table[...])
    real, imag = (earlier[0], earlier[1]) if begun else (None, None)
    for i in range(count):
        own = sums[i * rows : (i + 1) * rows]
        own_cos, own_sin = own[:, :size], own[:, size:]
        cos, sin = turn_cos[i], turn_sin[i]
        own_real, own_imag = own_cos * cos - own_sin * sin, own_cos * sin + own_sin * cos
        real, imag = (own_real, own_imag) if real is None else (real + own_real, imag + own_imag)
    if not ends:
        refs[0][0], refs[0][1] = real, imag
        return
    one_hot, out, by_wave, by_slot = refs
    devices, wire_rows, lanes = out.shape
    padded = one_hot.shape[0] // devices
    blocks = 2 * rows // lanes
    share = wire_rows // blocks
    place = pl.ds(pl.multiple_of(step * size, size), size)
    by_wave[0, :, place] = real.astype(BF16)
    by_wave[1, :, place] = (-imag).astype(BF16)

    @pl.when(step == pl.num_programs(0) - 1)
    def _():
        for part in range(2):
            by_slot[:, part * rows : (part + 1) * rows] = dot(one_hot[...], by_wave[part], NT)
        for device in range(devices):
            own = by_slot[device * padded : (device + 1) * padded, :]
            out[device] = pack_rows(
                [own[:share, block * lanes : (block + 1) * lanes] for block in range(blocks)]
            ).astype(BF16)


def forward(lines, table, turns, earlier=None, end=None):
    rows, columns = lines[0].shape
    waves = table.shape[1] // 2
    size = min(LANES, waves)
    turn_spec = pl.BlockSpec((len(lines), 1, size), lambda i: (0, 0, i))
    sum_spec = pl.BlockSpec((2, rows, size), lambda i: (0, 0, i))
    args = list(lines) + [table, *turns]
    in_specs = [pl.BlockSpec((rows, columns), lambda i: (0, 0))] * len(lines)
    in_specs += [pl.BlockSpec((2 * columns, 2 * size), lambda i: (0, i)), turn_spec, turn_spec]
    if earlier is not None:
        args.append(earlier)
        in_specs.append(sum_spec)
    if end is None:
        out_shape, out_spec, scratch = jax.ShapeDtypeStruct((2, rows, waves), F32), sum_spec, []
    else:
        one_hot, share = end
        slots = one_hot.shape[0]
        lanes = wire_lanes(rows)
        out = (slots // round_up(share, 8), share * (2 * rows // lanes), lanes)
        args.append(one_hot)
        in_specs.append(pl.BlockSpec((slots, waves), lambda i: (0, 0)))
        out_shape, out_spec = jax.ShapeDtypeStruct(out, BF16), pl.BlockSpec(out, lambda i: (0, 0, 0))
        scratch = [pltpu.VMEM((2, rows, waves), BF16), pltpu.VMEM((slots, 2 * rows), F32)]
    return pl.pallas_call(
        functools.partial(forward_kernel, len(lines), earlier is not None, end is not None),
        grid=(waves // size,),
        in_specs=in_specs,
        out_specs=out_spec,
        out_shape=out_shape,
        scratch_shapes=scratch,
        cost_estimate=pl.CostEstimate(
            flops=8 * len(lines) * rows * columns * waves, bytes_accessed=10**7, transcendentals=0
        ),
        compiler_params=pltpu.CompilerParams(vmem_limit_bytes=VMEM_LIMIT),
        name="forward",
    )(*args)


def sector_lines(exact, by_wave, table, turn_cos, turn_sin):
    count = turn_cos.shape[0]
    left = []
    for i in range(count):
        cos, sin = turn_cos[i], turn_sin[i]
        own_real, own_imag = by_wave[0].astype(F32), by_wave[1].astype(F32)
        real = own_real * cos - own_imag * sin
        minus = -(own_real * sin) - own_imag * cos
        left.append(jnp.concatenate([real, minus], axis=1))
    left = jnp.concatenate(left, axis=0) if count > 1 else left[0]
    high = left.astype(BF16)
    total = dot(jnp.concatenate([high, high], axis=1), table[...])
    if not exact:
        low = (left - high.astype(F32)).astype(BF16)
        total += dot(low, table[: low.shape[1]])
    return total.astype(BF16)


def backward_first_kernel(exact, wire, table_hbm, turn_cos, turn_sin, one_hot, mirror, out, by_wave, by_slot, table, sem):
    table_copy = pltpu.make_async_copy(table_hbm, table, sem)
    table_copy.start()
    devices, _, lanes = wire.shape
    rows = out.shape[0]
    waves = one_hot.shape[0]
    lat_rows = mirror.shape[0]
    padded = by_slot.shape[0] // devices
    blocks = 2 * rows // lanes
    for device in range(devices):
        for block, piece in enumerate(unpack_rows(wire[device].astype(F32), blocks, padded)):
            by_slot[device * padded : (device + 1) * padded, block * lanes : (block + 1) * lanes] = piece.astype(BF16)
    wave_ids = lax.broadcasted_iota(jnp.int32, (1, waves), 1)
    weight = jnp.where(wave_ids == 0, 1.0, 2.0).astype(F32)
    for part in range(2):
        ordered = dot(one_hot[...], by_slot[:, part * rows : (part + 1) * rows]).astype(BF16)
        for field in range(2):
            own = slice(field * lat_rows, (field + 1) * lat_rows)
            by_wave[part, own, :] = (dot(mirror[...], ordered[:, own], NT) * weight).astype(BF16)
    table_copy.wait()
    out[...] = sector_lines(exact, by_wave, table, turn_cos, turn_sin)


def backward_first(wire, table, turns, one_hot, mirror, exact):
    rows = 2 * mirror.shape[0]
    waves, slots = one_hot.shape
    vmem, hbm = pl.BlockSpec(memory_space=pltpu.VMEM), pl.BlockSpec(memory_space=pl.ANY)
    return pl.pallas_call(
        functools.partial(backward_first_kernel, exact),
        in_specs=[vmem, hbm, vmem, vmem, vmem, vmem],
        out_specs=[vmem, vmem],
        out_shape=[
            jax.ShapeDtypeStruct((rows, table.shape[1]), BF16),
            jax.ShapeDtypeStruct((2, rows, waves), BF16),
        ],
        scratch_shapes=[
            pltpu.VMEM((slots, 2 * rows), BF16),
            pltpu.VMEM(table.shape, BF16),
            pltpu.SemaphoreType.DMA,
        ],
        cost_estimate=pl.CostEstimate(flops=10**9, bytes_accessed=10**7, transcendentals=0),
        compiler_params=pltpu.CompilerParams(vmem_limit_bytes=VMEM_LIMIT),
        name="backward_first",
    )(wire, table, *turns, one_hot, mirror)


def backward_rest_kernel(exact, by_wave, table, turn_cos, turn_sin, *outs):
    rows = outs[0].shape[0]
    total = sector_lines(exact, by_wave, table, turn_cos, turn_sin)
    for i, out in enumerate(outs):
        out[...] = total[i * rows : (i + 1) * rows]


def backward_rest(by_wave, table, turns, exact):
    _, rows, _ = by_wave.shape
    count = turns[0].shape[0]
    vmem = pl.BlockSpec(memory_space=pltpu.VMEM)
    return pl.pallas_call(
        functools.partial(backward_rest_kernel, exact),
        in_specs=[vmem] * 4,
        out_specs=[vmem] * count,
        out_shape=[jax.ShapeDtypeStruct((rows, table.shape[1]), BF16)] * count,
        cost_estimate=pl.CostEstimate(flops=3 * 10**9, bytes_accessed=10**7, transcendentals=0),
        compiler_params=pltpu.CompilerParams(vmem_limit_bytes=WHOLE_LIMIT),
        name="backward_rest",
    )(by_wave, table, *turns)


def placing_kernel(count, chosen, *refs):
    blocks, (out, wide, sems) = refs[:count], refs[-3:]
    copies = []
    rows, parts = wide.shape[1], sems.shape[1]
    for i in range(count):
        for part in range(parts):
            own = pl.ds(part * (rows // parts), rows // parts)
            wide[i, own] = blocks[i][own].astype(F32)
            copies.append(pltpu.make_async_copy(wide.at[i, own], out.at[chosen[i], own], sems.at[i, part]))
            copies[-1].start()
    for copy in copies:
        copy.wait()


def placed(blocks, chosen, total, earlier=None):
    count = len(blocks)
    shape = blocks[0].shape
    parts = 4 if shape[0] % 64 == 0 else 1
    smem, vmem, hbm = (pl.BlockSpec(memory_space=space) for space in (pltpu.SMEM, pltpu.VMEM, pl.ANY))
    more = () if earlier is None else (earlier,)
    return pl.pallas_call(
        functools.partial(placing_kernel, count),
        in_specs=[smem] + [vmem] * count + [hbm] * len(more),
        out_specs=hbm,
        out_shape=jax.ShapeDtypeStruct((total,) + shape, F32),
        scratch_shapes=[pltpu.VMEM((count,) + shape, F32), pltpu.SemaphoreType.DMA((count, parts))],
        input_output_aliases={1 + count: 0} if more else {},
        compiler_params=pltpu.CompilerParams(vmem_limit_bytes=VMEM_LIMIT),
        name="placed",
    )(chosen, *blocks, *more)


def round_up(value, unit):
    return -(-value // unit) * unit


def pack_rows(pieces):
    share = pieces[0].shape[0]
    main = share // 8 * 8
    parts = [piece[:main] for piece in pieces] if main else []
    parts += [piece[main:] for piece in pieces] if main < share else []
    return jnp.concatenate(parts, axis=0) if len(parts) > 1 else parts[0]


def unpack_rows(value, count, fill):
    share = value.shape[0] // count
    main = share // 8 * 8
    rest = share - main
    pieces = []
    for i in range(count):
        parts = [value[i * main : (i + 1) * main]] if main else []
        parts += [value[count * main + i * rest : count * main + (i + 1) * rest]] if rest else []
        parts += [jnp.zeros((fill - share, value.shape[1]), value.dtype)] if fill > share else []
        pieces.append(jnp.concatenate(parts, axis=0) if len(parts) > 1 else parts[0])
    return pieces


def wire_lanes(rows):
    return LANES if 2 * rows % LANES == 0 else 2 * rows


def legendre_kernel(sides, lat_rows, group, place, order, blocks, received, damping, basis, *rest):
    spectral_out, returned_out, spectral, returned, held, buffer, sems, out_sems, spectral_sem = rest
    devices, wire_rows, lanes = received.shape
    sectors, share = spectral.shape[:2]
    slots, degrees, half_lat = basis.shape
    sources = devices // sectors
    fields = sides // 2
    combos = sectors * sides
    lane_blocks = held.shape[0]
    stride = held.shape[1] // (2 * combos)
    wire_blocks = wire_rows // share
    groups = share // group
    most = degrees // STEP
    scale = 1.0 / math.sqrt(degrees)
    out_step = devices // out_sems.shape[0]

    def copies(index, count):
        ring = lax.rem(index, DEPTH)
        rows = pl.ds(0, count * STEP)
        return [
            pltpu.make_async_copy(
                basis.at[jnp.minimum(place[0] + order[index * group + i], slots - 1), rows, :],
                buffer.at[ring, i, rows, :],
                sems.at[ring, i],
            )
            for i in range(group)
        ]

    def fetch(index):
        for count in range(1, most + 1):

            @pl.when(blocks[index] == count)
            def _():
                for copy in copies(index, count):
                    copy.start()

    for index in range(min(DEPTH - 1, groups)):
        fetch(index)

    def wire_pieces(device, wire_block):
        source, sector = divmod(device, sectors)
        side, near = (0, source) if source < sources // 2 else (1, sources - 1 - source)
        column, end = wire_block * lanes, (wire_block + 1) * lanes
        while column < end:
            part_field, lat = divmod(column, lat_rows)
            part, field = divmod(part_field, fields)
            row = (side * combos + sector * sides + field * 2 + part) * stride
            place = near * lat_rows + lat
            width = min(end - column, lat_rows - lat, LANES - place % LANES)
            yield column - wire_block * lanes, width, row, place // LANES, place % LANES
            column += width

    for device in range(devices):
        for wire_block, piece in enumerate(unpack_rows(received[device].astype(F32), wire_blocks, stride)):
            for at, width, row, block, lane in wire_pieces(device, wire_block):
                held[block, row : row + stride, lane : lane + width] = piece[:, at : at + width]

    def load_slot(slot):
        rows = pl.ds(slot, 2 * combos, stride=stride)
        return jnp.concatenate([held[block, rows, :] for block in range(lane_blocks)], axis=1)

    def store_slot(slot, value):
        rows = pl.ds(slot, 2 * combos, stride=stride)
        for block in range(lane_blocks):
            held[block, rows, :] = value[:, block * LANES : (block + 1) * LANES]

    def one_group(index, count):
        ring = lax.rem(index, DEPTH)
        here = [order[index * group + i] for i in range(group)]
        if count == 0:
            for slot in here:
                for sector in range(sectors):
                    spectral[place[1] ^ sector, slot] = jnp.zeros(spectral.shape[2:], F32)
                store_slot(slot, jnp.zeros((2 * combos, half_lat), F32))
            return
        width = count * STEP
        for copy in copies(index, count):
            copy.wait()
        parity = 1.0 - 2.0 * (lax.broadcasted_iota(jnp.int32, (1, width), 1) % 2).astype(F32)
        left = [load_slot(slot).astype(BF16) for slot in here]
        sums = [dot(left[i], buffer[ring, i, :width, :], NT) for i in range(group)]
        damped = [
            (sums[i][:combos] + parity * sums[i][combos:]) * damping[slot, :, :width] for i, slot in enumerate(here)
        ]
        turned = [jnp.concatenate([value, parity * value], axis=0).astype(BF16) for value in damped]
        backs = [dot(turned[i], buffer[ring, i, :width, :]) * scale for i in range(group)]
        for i, slot in enumerate(here):
            for sector in range(sectors):
                spectral[place[1] ^ sector, slot, :, :width] = damped[i][sector * sides : (sector + 1) * sides]
                if width < degrees:
                    spectral[place[1] ^ sector, slot, :, width:] = jnp.zeros((sides, degrees - width), F32)
        for i, slot in enumerate(here):
            store_slot(slot, backs[i])

    def loop_body(index, carry):
        @pl.when(index + DEPTH - 1 < groups)
        def _():
            fetch(index + DEPTH - 1)

        for count in range(most + 1):
            pl.when(blocks[index] == count)(functools.partial(one_group, index, count))
        return carry

    lax.fori_loop(0, groups, loop_body, 0)

    spectral_copy = pltpu.make_async_copy(spectral, spectral_out, spectral_sem)
    spectral_copy.start()
    out_copies = []
    for device in range(devices):
        pieces = []
        for wire_block in range(wire_blocks):
            parts = [
                held[block, row : row + share, lane : lane + width]
                for _, width, row, block, lane in wire_pieces(device, wire_block)
            ]
            pieces.append(jnp.concatenate(parts, axis=1) if len(parts) > 1 else parts[0])
        returned[device] = pack_rows(pieces).astype(BF16)
        if (device + 1) % out_step == 0:
            part = pl.ds(device + 1 - out_step, out_step)
            out_copies.append(
                pltpu.make_async_copy(returned.at[part], returned_out.at[part], out_sems.at[device // out_step])
            )
            out_copies[-1].start()
    for copy in (*out_copies, spectral_copy):
        copy.wait()


def legendre(received, basis, damping, place, order, blocks, sectors, sides, lat_rows, group):
    share = order.shape[0]
    degrees, half_lat = basis.shape[1:]
    combos = sectors * sides
    smem, vmem, hbm = (pl.BlockSpec(memory_space=space) for space in (pltpu.SMEM, pltpu.VMEM, pl.ANY))
    return pl.pallas_call(
        functools.partial(legendre_kernel, sides, lat_rows, group),
        in_specs=[smem, smem, smem, vmem, vmem, hbm],
        out_specs=[pl.BlockSpec(memory_space=pltpu.HBM)] * 2,
        out_shape=[
            jax.ShapeDtypeStruct((sectors, share, sides, degrees), F32),
            jax.ShapeDtypeStruct(received.shape, BF16),
        ],
        scratch_shapes=[
            pltpu.VMEM((sectors, share, sides, degrees), F32),
            pltpu.VMEM(received.shape, BF16),
            pltpu.VMEM((half_lat // LANES, 2 * combos * round_up(share, 8), LANES), F32),
            pltpu.VMEM((DEPTH, group, degrees, half_lat), BF16),
            pltpu.SemaphoreType.DMA((DEPTH, group)),
            pltpu.SemaphoreType.DMA((8,)),
            pltpu.SemaphoreType.DMA,
        ],
        cost_estimate=pl.CostEstimate(
            flops=4 * share * degrees * half_lat * 2 * combos,
            bytes_accessed=2 * share * degrees * half_lat,
            transcendentals=0,
        ),
        compiler_params=pltpu.CompilerParams(vmem_limit_bytes=LEGENDRE_LIMIT),
        name="legendre",
    )(place, order, blocks, received, damping, basis)


def degree_order(counts):
    size = counts.shape[0]
    ids = jnp.arange(size, dtype=jnp.int32)
    ahead = (counts[None, :] > counts[:, None]) | ((counts[None, :] == counts[:, None]) & (ids[None, :] < ids[:, None]))
    rank = jnp.sum(ahead.astype(jnp.int32), axis=1)
    placed = rank[:, None] == ids[None, :]
    order = jnp.sum(jnp.where(placed, ids[:, None], 0), axis=0)
    sorted_counts = jnp.sum(jnp.where(placed, counts[:, None], 0), axis=0)
    group = max(g for g in range(1, 6) if size % g == 0)
    return order, (sorted_counts[::group] + (STEP - 1)) // STEP, group


def body(wind_u, wind_v, basis, wave_slots, degree_count, viscosity):
    sectors = lax.axis_size("lon")
    owners = lax.axis_size("lat")
    sector_index = lax.axis_index("lon")
    owner_index = lax.axis_index("lat")
    levels, lat_rows, lon_cols = wind_u.shape
    capacity, degrees, half_lat = basis.shape
    waves = wave_slots.shape[0]
    slot_total = capacity * owners
    assert levels == sectors and sectors & (sectors - 1) == 0
    share = -(-capacity // sectors)
    padded = round_up(share, 8)
    length = sectors * lon_cols
    masks = [sectors // 2] + [mask for mask in range(sectors - 1, 0, -1) if mask != sectors // 2] + [0]

    def across(value, mask):
        return lax.ppermute(value, "lon", [(i, i ^ mask) for i in range(sectors)]) if mask else value

    def partners(some):
        return jnp.stack([sector_index ^ mask for mask in some]).astype(jnp.int32)

    far, rest = masks[:1], masks[1:]
    row_ids = jnp.arange(lat_rows, dtype=jnp.int32)
    south = owner_index >= owners // 2
    mirror = (row_ids[:, None] == jnp.where(south, lat_rows - 1 - row_ids, row_ids)[None, :]).astype(BF16)

    def exchanged(first, others):
        arrived = {mask: across(value, mask) for mask, value in zip(far, first)}
        made = others()
        arrived.update({mask: across(value, mask) for mask, value in zip(rest, made)})
        return arrived

    lines = exchanged(
        wind_products(wind_u, wind_v, mirror, partners(far)),
        lambda: wind_products(wind_u, wind_v, mirror, partners(rest)),
    )

    slot_ids = jnp.arange(slot_total, dtype=jnp.int32)
    wave_ids = jnp.arange(waves, dtype=jnp.int32)
    places = jnp.arange(owners * sectors * padded, dtype=jnp.int32)
    place_owner, place_sector, place_slot = places // (sectors * padded), places // padded % sectors, places % padded
    in_owner = place_sector * share + place_slot
    named = jnp.where((place_slot < share) & (in_owner < capacity), place_owner * capacity + in_owner, -1)
    one_hot = (named[:, None] == wave_slots[None, :]).astype(BF16)
    one_hot_turned = (wave_slots[:, None] == named[None, :]).astype(BF16)
    forward_table = wave_table(lon_cols, waves, length, True)
    backward_table = wave_table(waves, lon_cols, length, False)
    turns = sector_turns(sectors, waves)

    def turns_of(some):
        at = partners(some)
        return tuple(jnp.take(turn, at, axis=0) for turn in turns)

    first = sector_index * share
    local_ids = jnp.arange(share, dtype=jnp.int32)
    inside = first + local_ids < capacity
    at = owner_index * capacity + jnp.minimum(first + local_ids, capacity - 1)
    here = at[:, None] == wave_slots[None, :]
    wave_here = jnp.sum(jnp.where(here, wave_ids[None, :], 0), axis=1)
    count_here = jnp.where(inside, jnp.sum(jnp.where(here, degree_count[None, :], 0), axis=1), 0)
    degree_ids = jnp.arange(degrees, dtype=jnp.int32)
    total_degree = wave_here[:, None] + degree_ids[None, :]
    scaled = (total_degree * (total_degree + 1)).astype(F32) / float(degrees * (degrees + 1))
    kept = degree_ids[None, :] < count_here[:, None]
    sides = 4
    rates = jnp.repeat(viscosity, sides)
    damping = 1.0 / (1.0 + rates[None, :, None] * (scaled * scaled)[:, None, :])
    damping = jnp.where(kept[:, None, :], damping * (1.0 / math.sqrt(2 * half_lat)), 0.0)
    order, blocks, group = degree_order(count_here)

    by_arrival = [0, *[mask for mask in reversed(masks) if mask and mask < sectors // 2], *masks]
    by_arrival = list(dict.fromkeys(by_arrival))
    early, late = by_arrival[:-1], by_arrival[-1:]
    sums = forward([lines[mask] for mask in early], forward_table, turns_of(early))
    fourier = forward([lines[mask] for mask in late], forward_table, turns_of(late), sums, (one_hot, share))
    received = lax.all_to_all(fourier, ("lat", "lon"), split_axis=0, concat_axis=0, tiled=True)
    place = jnp.stack([first, sector_index]).astype(jnp.int32)
    spectral, returned = legendre(
        received, basis, damping, place, order, blocks, sectors, sides, lat_rows, group
    )
    regrouped = lax.all_to_all(returned, ("lat", "lon"), split_axis=0, concat_axis=0, tiled=True)

    coefficients = jnp.zeros((sectors * share, 1, 2, 2, degrees), F32)
    for mask in masks:
        own = across(spectral[mask].astype(BF16), mask).astype(F32).reshape(share, 1, 2, 2, degrees)
        coefficients = lax.dynamic_update_slice_in_dim(coefficients, own, (sector_index ^ mask) * share, 0)

    exact = sectors in (1, 2, 4)
    far_lines, by_wave = backward_first(regrouped, backward_table, turns_of(far), one_hot_turned, mirror, exact)
    rest_turns = turns_of(rest)
    back = exchanged([far_lines], lambda: backward_rest(by_wave, backward_table, rest_turns, exact))
    tendency = placed([back[mask] for mask in early], partners(early), sectors)
    tendency = placed([back[mask] for mask in late], partners(late), sectors, tendency)
    return coefficients[:capacity], tendency.reshape(levels, 2, lat_rows, lon_cols)


def solution(mesh):
    return jax.shard_map(
        body,
        mesh=mesh,
        in_specs=(
            P(None, "lat", "lon"),
            P(None, "lat", "lon"),
            P("lat", None, None),
            P(),
            P(),
            P(),
        ),
        out_specs=(P("lat", "lon", None, None, None), P(None, None, "lat", "lon")),
        check_vma=False,
    )
```

```python
import functools
import math

import jax
import jax.numpy as jnp
import numpy as np
from jax import lax
from jax.experimental import pallas as pl
from jax.experimental.pallas import tpu as pltpu
from jax.sharding import PartitionSpec as P


BF16 = jnp.bfloat16
F32 = jnp.float32
MIB = 1024 * 1024
VMEM_LIMIT = 24 * MIB
LEGENDRE_LIMIT = 36 * MIB
WHOLE_LIMIT = 60 * MIB
STEP = 128
LANES = 128
DEPTH = 3
NT = (((1,), (1,)), ((), ()))
NN = (((1,), (0,)), ((), ()))


def dot(a, b, dims=NN):
    return lax.dot_general(a, b, dims, preferred_element_type=F32)


def phases(rows, columns, length):
    turns = 2.0 * np.pi * (rows[:, None] * columns[None, :] % length) / length
    return np.cos(turns), np.sin(turns)


def table_kernel(interleaved, near_cos, near_sin, far_cos, far_sin, out):
    near, lanes = near_cos.shape
    count = far_cos.shape[0] * near
    size = min(LANES, lanes)
    for step in range(far_cos.shape[0]):
        cos = far_cos[step] * near_cos[...] - far_sin[step] * near_sin[...]
        sin = far_sin[step] * near_cos[...] + far_cos[step] * near_sin[...]
        high = (cos.astype(BF16), sin.astype(BF16))
        low = tuple((value - top.astype(F32)).astype(BF16) for value, top in zip((cos, sin), high))
        for term, pair in enumerate((high, low)):
            for which, value in enumerate(pair):
                if interleaved:
                    row = term * count + step * near
                    for block in range(lanes // size):
                        lane = (2 * block + which) * size
                        out[row : row + near, lane : lane + size] = value[:, block * size : (block + 1) * size]
                else:
                    row = (2 * term + which) * count + step * near
                    out[row : row + near, :] = value


def wave_table(rows, columns, length, interleaved):
    near = 32
    near_cos, near_sin = phases(np.arange(near), np.arange(columns), length)
    far_cos, far_sin = phases(np.arange(rows // near) * near, np.arange(columns), length)
    scaling = 1.0 / math.sqrt(length)
    shape = (2 * rows, 2 * columns) if interleaved else (4 * rows, columns)
    return pl.pallas_call(
        functools.partial(table_kernel, interleaved),
        out_shape=jax.ShapeDtypeStruct(shape, BF16),
        compiler_params=pltpu.CompilerParams(vmem_limit_bytes=WHOLE_LIMIT),
        name="wave_table",
    )(
        jnp.asarray(near_cos * scaling, F32),
        jnp.asarray(near_sin * scaling, F32),
        jnp.asarray(far_cos[:, None, :], F32),
        jnp.asarray(far_sin[:, None, :], F32),
    )


def sector_turns(sectors, waves):
    both = phases(np.arange(sectors), np.arange(waves), sectors)
    return tuple(jnp.asarray(np.round(turn, 12)[:, None, :], F32) for turn in both)


def chunk_widths(lat_rows):
    main = lat_rows // LANES * LANES
    return (main, lat_rows - main) if main and 2 * (lat_rows - main) == LANES else (lat_rows,)


def chunk_start(widths, chunk, near):
    if len(widths) == 1:
        return 0
    odd = near % 2
    return odd * widths[1] if chunk == 0 else (1 - odd) * widths[0]


def band_place(owner_index, owners):
    south = owner_index >= owners // 2
    return south, jnp.where(south, owners - 1 - owner_index, owner_index)


def product_kernel(masks, widths, wind_u, wind_v, *refs):
    outs, (space, sems) = refs[:-2], refs[-2:]
    _, lat_rows, columns = wind_u.shape
    south, near = band_place(lax.axis_index("lat"), lax.axis_size("lat"))
    pieces = sems.shape[2]
    size = columns // pieces
    copies = {}
    for i, mask in enumerate(masks):
        level = lax.axis_index("lon") ^ mask
        for piece in range(pieces):
            own = pl.ds(piece * size, size)
            for which, wind in enumerate((wind_u, wind_v)):
                copy = pltpu.make_async_copy(
                    wind.at[level, :, own], space.at[i, which, :, own], sems.at[i, which, piece]
                )
                copy.start()
                copies[i, piece, which] = copy
    chosen = []
    for chunk, width in enumerate(widths):
        start = chunk_start(widths, chunk, near)
        ids = start + lax.broadcasted_iota(jnp.int32, (width, lat_rows), 0)
        lats = lax.broadcasted_iota(jnp.int32, (width, lat_rows), 1)
        chosen.append((lats == jnp.where(south, lat_rows - 1 - ids, ids)).astype(F32).astype(BF16))
    for i in range(len(masks)):
        for piece in range(pieces):
            own = pl.ds(piece * size, size)
            copies[i, piece, 0].wait()
            copies[i, piece, 1].wait()
            u, v = space[i, 0, :, own], space[i, 1, :, own]
            for field, product in enumerate((u * v, u * u - v * v)):
                product = product.astype(BF16)
                for chunk, width in enumerate(widths):
                    outs[i * len(widths) + chunk][field * width : (field + 1) * width, own] = dot(
                        chosen[chunk], product
                    ).astype(BF16)


def wind_products(wind_u, wind_v, masks, widths):
    _, lat_rows, columns = wind_u.shape
    hbm, vmem = pl.BlockSpec(memory_space=pl.ANY), pl.BlockSpec(memory_space=pltpu.VMEM)
    outs = pl.pallas_call(
        functools.partial(product_kernel, masks, widths),
        in_specs=[hbm, hbm],
        out_specs=[vmem] * (len(masks) * len(widths)),
        out_shape=[jax.ShapeDtypeStruct((2 * width, columns), BF16) for _ in masks for width in widths],
        scratch_shapes=[
            pltpu.VMEM((len(masks), 2, lat_rows, columns), F32),
            pltpu.SemaphoreType.DMA((len(masks), 2, columns // LANES if columns % LANES == 0 else 1)),
        ],
        compiler_params=pltpu.CompilerParams(vmem_limit_bytes=WHOLE_LIMIT),
        name="wind_products",
    )(wind_u, wind_v)
    return {
        (chunk, mask): outs[i * len(widths) + chunk] for i, mask in enumerate(masks) for chunk in range(len(widths))
    }


def forward_kernel(count, begun, ends, *refs):
    lines, refs = refs[:count], refs[count:]
    table, turn_cos, turn_sin = refs[:3]
    earlier, refs = (refs[3], refs[4:]) if begun else (None, refs[3:])
    step = pl.program_id(0)
    size = table.shape[1] // 2
    rows = lines[0].shape[0]
    both = jnp.concatenate([jnp.concatenate([line[...]] * 2, axis=1) for line in lines], axis=0)
    sums = dot(both, table[...])
    real, imag = (earlier[0], earlier[1]) if begun else (None, None)
    for i in range(count):
        own = sums[i * rows : (i + 1) * rows]
        own_cos, own_sin = own[:, :size], own[:, size:]
        cos, sin = turn_cos[i], turn_sin[i]
        own_real, own_imag = own_cos * cos - own_sin * sin, own_cos * sin + own_sin * cos
        real, imag = (own_real, own_imag) if real is None else (real + own_real, imag + own_imag)
    if not ends:
        refs[0][0], refs[0][1] = real, imag
        return
    one_hot, out, by_wave, by_slot = refs
    devices, wire_rows, lanes = out.shape
    padded = one_hot.shape[0] // devices
    blocks = 2 * rows // lanes
    share = wire_rows // blocks
    place = pl.ds(pl.multiple_of(step * size, size), size)
    by_wave[0, :, place] = real.astype(BF16)
    by_wave[1, :, place] = (-imag).astype(BF16)

    @pl.when(step == pl.num_programs(0) - 1)
    def _():
        for part in range(2):
            by_slot[:, part * rows : (part + 1) * rows] = dot(one_hot[...], by_wave[part], NT)
        for device in range(devices):
            own = by_slot[device * padded : (device + 1) * padded, :]
            out[device] = pack_rows(
                [own[:share, block * lanes : (block + 1) * lanes] for block in range(blocks)]
            ).astype(BF16)


def forward(lines, table, turns, earlier=None, end=None):
    rows, columns = lines[0].shape
    waves = table.shape[1] // 2
    size = min(LANES, waves)
    turn_spec = pl.BlockSpec((len(lines), 1, size), lambda i: (0, 0, i))
    sum_spec = pl.BlockSpec((2, rows, size), lambda i: (0, 0, i))
    args = list(lines) + [table, *turns]
    in_specs = [pl.BlockSpec((rows, columns), lambda i: (0, 0))] * len(lines)
    in_specs += [pl.BlockSpec((2 * columns, 2 * size), lambda i: (0, i)), turn_spec, turn_spec]
    if earlier is not None:
        args.append(earlier)
        in_specs.append(sum_spec)
    if end is None:
        out_shape, out_spec, scratch = jax.ShapeDtypeStruct((2, rows, waves), F32), sum_spec, []
    else:
        one_hot, share = end
        slots = one_hot.shape[0]
        lanes = wire_lanes(rows)
        out = (slots // round_up(share, 8), share * (2 * rows // lanes), lanes)
        args.append(one_hot)
        in_specs.append(pl.BlockSpec((slots, waves), lambda i: (0, 0)))
        out_shape, out_spec = jax.ShapeDtypeStruct(out, BF16), pl.BlockSpec(out, lambda i: (0, 0, 0))
        scratch = [pltpu.VMEM((2, rows, waves), BF16), pltpu.VMEM((slots, 2 * rows), F32)]
    return pl.pallas_call(
        functools.partial(forward_kernel, len(lines), earlier is not None, end is not None),
        grid=(waves // size,),
        in_specs=in_specs,
        out_specs=out_spec,
        out_shape=out_shape,
        scratch_shapes=scratch,
        cost_estimate=pl.CostEstimate(
            flops=8 * len(lines) * rows * columns * waves, bytes_accessed=10**7, transcendentals=0
        ),
        compiler_params=pltpu.CompilerParams(vmem_limit_bytes=VMEM_LIMIT),
        name="forward",
    )(*args)


def sector_lines(exact, by_wave, table, turn_cos, turn_sin):
    count = turn_cos.shape[0]
    left = []
    for i in range(count):
        cos, sin = turn_cos[i], turn_sin[i]
        own_real, own_imag = by_wave[0].astype(F32), by_wave[1].astype(F32)
        real = own_real * cos - own_imag * sin
        minus = -(own_real * sin) - own_imag * cos
        left.append(jnp.concatenate([real, minus], axis=1))
    left = jnp.concatenate(left, axis=0) if count > 1 else left[0]
    high = left.astype(BF16)
    total = dot(jnp.concatenate([high, high], axis=1), table[...])
    if not exact:
        low = (left - high.astype(F32)).astype(BF16)
        total += dot(low, table[: low.shape[1]])
    return total.astype(BF16)


def backward_first_kernel(exact, wire, table_hbm, turn_cos, turn_sin, one_hot, mirror, out, by_wave, by_slot, table, sem):
    table_copy = pltpu.make_async_copy(table_hbm, table, sem)
    table_copy.start()
    devices, _, lanes = wire.shape
    rows = out.shape[0]
    waves = one_hot.shape[0]
    width = mirror.shape[0]
    padded = by_slot.shape[0] // devices
    blocks = 2 * rows // lanes
    for device in range(devices):
        for block, piece in enumerate(unpack_rows(wire[device].astype(F32), blocks, padded)):
            by_slot[device * padded : (device + 1) * padded, block * lanes : (block + 1) * lanes] = piece.astype(BF16)
    wave_ids = lax.broadcasted_iota(jnp.int32, (1, waves), 1)
    weight = jnp.where(wave_ids == 0, 1.0, 2.0).astype(F32)
    for part in range(2):
        ordered = dot(one_hot[...], by_slot[:, part * rows : (part + 1) * rows]).astype(BF16)
        for field in range(2):
            own = slice(field * width, (field + 1) * width)
            by_wave[part, own, :] = (dot(mirror[...], ordered[:, own], NT) * weight).astype(BF16)
    table_copy.wait()
    out[...] = sector_lines(exact, by_wave, table, turn_cos, turn_sin)


def backward_first(wire, table, turns, one_hot, mirror, exact):
    rows = 2 * mirror.shape[0]
    waves, slots = one_hot.shape
    vmem, hbm = pl.BlockSpec(memory_space=pltpu.VMEM), pl.BlockSpec(memory_space=pl.ANY)
    return pl.pallas_call(
        functools.partial(backward_first_kernel, exact),
        in_specs=[vmem, hbm, vmem, vmem, vmem, vmem],
        out_specs=[vmem, vmem],
        out_shape=[
            jax.ShapeDtypeStruct((rows, table.shape[1]), BF16),
            jax.ShapeDtypeStruct((2, rows, waves), BF16),
        ],
        scratch_shapes=[
            pltpu.VMEM((slots, 2 * rows), BF16),
            pltpu.VMEM(table.shape, BF16),
            pltpu.SemaphoreType.DMA,
        ],
        cost_estimate=pl.CostEstimate(flops=10**9, bytes_accessed=10**7, transcendentals=0),
        compiler_params=pltpu.CompilerParams(vmem_limit_bytes=VMEM_LIMIT),
        name="backward_first",
    )(wire, table, *turns, one_hot, mirror)


def backward_rest_kernel(exact, by_wave, table, turn_cos, turn_sin, *outs):
    rows = outs[0].shape[0]
    total = sector_lines(exact, by_wave, table, turn_cos, turn_sin)
    for i, out in enumerate(outs):
        out[...] = total[i * rows : (i + 1) * rows]


def backward_rest(by_wave, table, turns, exact):
    _, rows, _ = by_wave.shape
    count = turns[0].shape[0]
    vmem = pl.BlockSpec(memory_space=pltpu.VMEM)
    return pl.pallas_call(
        functools.partial(backward_rest_kernel, exact),
        in_specs=[vmem] * 4,
        out_specs=[vmem] * count,
        out_shape=[jax.ShapeDtypeStruct((rows, table.shape[1]), BF16)] * count,
        cost_estimate=pl.CostEstimate(flops=3 * 10**9, bytes_accessed=10**7, transcendentals=0),
        compiler_params=pltpu.CompilerParams(vmem_limit_bytes=WHOLE_LIMIT),
        name="backward_rest",
    )(by_wave, table, *turns)


def placing_kernel(parts, widths, *refs):
    blocks, (out, wide, sems) = refs[: len(parts)], refs[-3:]
    _, rows, _ = out.shape
    lat_rows = rows // 2
    south, near = band_place(lax.axis_index("lat"), lax.axis_size("lat"))
    copies = []
    for i, (chunk, mask) in enumerate(parts):
        width = widths[chunk]
        start = chunk_start(widths, chunk, near)
        start = jnp.where(south, lat_rows - start - width, start)
        level = lax.axis_index("lon") ^ mask
        for field in range(2):
            own = slice(field * width, (field + 1) * width)
            wide[i, own] = blocks[i][own].astype(F32)
            place = pl.ds(pl.multiple_of(field * lat_rows + start, math.gcd(*widths, lat_rows)), width)
            copies.append(pltpu.make_async_copy(wide.at[i, own], out.at[level, place], sems.at[i, field]))
            copies[-1].start()
    for copy in copies:
        copy.wait()


def placed(blocks, parts, widths, shape, earlier=None):
    count = len(parts)
    vmem, hbm = pl.BlockSpec(memory_space=pltpu.VMEM), pl.BlockSpec(memory_space=pl.ANY)
    more = () if earlier is None else (earlier,)
    return pl.pallas_call(
        functools.partial(placing_kernel, parts, widths),
        in_specs=[vmem] * count + [hbm] * len(more),
        out_specs=hbm,
        out_shape=jax.ShapeDtypeStruct(shape, F32),
        scratch_shapes=[
            pltpu.VMEM((count, 2 * max(widths[chunk] for chunk, _ in parts), shape[2]), F32),
            pltpu.SemaphoreType.DMA((count, 2)),
        ],
        input_output_aliases={count: 0} if more else {},
        compiler_params=pltpu.CompilerParams(vmem_limit_bytes=VMEM_LIMIT),
        name="placed",
    )(*[blocks[part] for part in parts], *more)


def round_up(value, unit):
    return -(-value // unit) * unit


def pack_rows(pieces):
    share = pieces[0].shape[0]
    main = share // 8 * 8
    parts = [piece[:main] for piece in pieces] if main else []
    parts += [piece[main:] for piece in pieces] if main < share else []
    return jnp.concatenate(parts, axis=0) if len(parts) > 1 else parts[0]


def unpack_rows(value, count, fill):
    share = value.shape[0] // count
    main = share // 8 * 8
    rest = share - main
    pieces = []
    for i in range(count):
        parts = [value[i * main : (i + 1) * main]] if main else []
        parts += [value[count * main + i * rest : count * main + (i + 1) * rest]] if rest else []
        parts += [jnp.zeros((fill - share, value.shape[1]), value.dtype)] if fill > share else []
        pieces.append(jnp.concatenate(parts, axis=0) if len(parts) > 1 else parts[0])
    return pieces


def wire_lanes(rows):
    return LANES if 2 * rows % LANES == 0 else 2 * rows


def legendre_kernel(sides, widths, group, place, order, blocks, damping, basis, *rest):
    wires = len(widths)
    received, rest = rest[:wires], rest[wires:]
    spectral_out, returned_out, rest = rest[0], rest[1 : 1 + wires], rest[1 + wires :]
    spectral, returned, (held, buffer, sems, out_sems, spectral_sem) = rest[0], rest[1 : 1 + wires], rest[1 + wires :]
    lat_rows = sum(widths)
    devices = received[0].shape[0]
    sectors, share = spectral.shape[:2]
    slots, degrees, half_lat = basis.shape
    sources = devices // sectors
    fields = sides // 2
    combos = sectors * sides
    lane_blocks = held.shape[0]
    stride = held.shape[1] // (2 * combos)
    groups = share // group
    most = degrees // STEP
    scale = 1.0 / math.sqrt(degrees)
    out_step = devices // out_sems.shape[1]

    def copies(index, count):
        ring = lax.rem(index, DEPTH)
        rows = pl.ds(0, count * STEP)
        return [
            pltpu.make_async_copy(
                basis.at[jnp.minimum(place[0] + order[index * group + i], slots - 1), rows, :],
                buffer.at[ring, i, rows, :],
                sems.at[ring, i],
            )
            for i in range(group)
        ]

    def fetch(index):
        for count in range(1, most + 1):

            @pl.when(blocks[index] == count)
            def _():
                for copy in copies(index, count):
                    copy.start()

    for index in range(min(DEPTH - 1, groups)):
        fetch(index)

    def wire_pieces(wire, device, wire_block):
        source, sector = divmod(device, sectors)
        side, near = (0, source) if source < sources // 2 else (1, sources - 1 - source)
        lanes, chunk_width = received[wire].shape[2], widths[wire]
        begin = near * lat_rows + chunk_start(widths, wire, near)
        column, end = wire_block * lanes, (wire_block + 1) * lanes
        while column < end:
            part_field, lat = divmod(column, chunk_width)
            part, field = divmod(part_field, fields)
            row = (side * combos + sector * sides + field * 2 + part) * stride
            at = begin + lat
            width = min(end - column, chunk_width - lat, LANES - at % LANES)
            yield column - wire_block * lanes, width, row, at // LANES, at % LANES
            column += width

    for wire in range(wires):
        wire_blocks = received[wire].shape[1] // share
        for device in range(devices):
            own_blocks = unpack_rows(received[wire][device].astype(F32), wire_blocks, stride)
            for wire_block, piece in enumerate(own_blocks):
                for at, width, row, block, lane in wire_pieces(wire, device, wire_block):
                    held[block, row : row + stride, lane : lane + width] = piece[:, at : at + width]

    def load_slot(slot):
        rows = pl.ds(slot, 2 * combos, stride=stride)
        return jnp.concatenate([held[block, rows, :] for block in range(lane_blocks)], axis=1)

    def store_slot(slot, value):
        rows = pl.ds(slot, 2 * combos, stride=stride)
        for block in range(lane_blocks):
            held[block, rows, :] = value[:, block * LANES : (block + 1) * LANES]

    def one_group(index, count):
        ring = lax.rem(index, DEPTH)
        here = [order[index * group + i] for i in range(group)]
        if count == 0:
            for slot in here:
                for sector in range(sectors):
                    spectral[place[1] ^ sector, slot] = jnp.zeros(spectral.shape[2:], F32)
                store_slot(slot, jnp.zeros((2 * combos, half_lat), F32))
            return
        width = count * STEP
        for copy in copies(index, count):
            copy.wait()
        parity = 1.0 - 2.0 * (lax.broadcasted_iota(jnp.int32, (1, width), 1) % 2).astype(F32)
        left = [load_slot(slot).astype(BF16) for slot in here]
        sums = [dot(left[i], buffer[ring, i, :width, :], NT) for i in range(group)]
        damped = [
            (sums[i][:combos] + parity * sums[i][combos:]) * damping[slot, :, :width] for i, slot in enumerate(here)
        ]
        turned = [jnp.concatenate([value, parity * value], axis=0).astype(BF16) for value in damped]
        backs = [dot(turned[i], buffer[ring, i, :width, :]) * scale for i in range(group)]
        for i, slot in enumerate(here):
            for sector in range(sectors):
                spectral[place[1] ^ sector, slot, :, :width] = damped[i][sector * sides : (sector + 1) * sides]
                if width < degrees:
                    spectral[place[1] ^ sector, slot, :, width:] = jnp.zeros((sides, degrees - width), F32)
        for i, slot in enumerate(here):
            store_slot(slot, backs[i])

    def loop_body(index, carry):
        @pl.when(index + DEPTH - 1 < groups)
        def _():
            fetch(index + DEPTH - 1)

        for count in range(most + 1):
            pl.when(blocks[index] == count)(functools.partial(one_group, index, count))
        return carry

    lax.fori_loop(0, groups, loop_body, 0)

    spectral_copy = pltpu.make_async_copy(spectral, spectral_out, spectral_sem)
    spectral_copy.start()
    out_copies = []
    for wire in range(wires):
        wire_blocks = received[wire].shape[1] // share
        for device in range(devices):
            pieces = []
            for wire_block in range(wire_blocks):
                parts = [
                    held[block, row : row + share, lane : lane + width]
                    for _, width, row, block, lane in wire_pieces(wire, device, wire_block)
                ]
                pieces.append(jnp.concatenate(parts, axis=1) if len(parts) > 1 else parts[0])
            returned[wire][device] = pack_rows(pieces).astype(BF16)
            if (device + 1) % out_step == 0:
                part = pl.ds(device + 1 - out_step, out_step)
                copy = pltpu.make_async_copy(
                    returned[wire].at[part], returned_out[wire].at[part], out_sems.at[wire, device // out_step]
                )
                copy.start()
                out_copies.append(copy)
    for copy in (*out_copies, spectral_copy):
        copy.wait()


def legendre(received, basis, damping, place, order, blocks, sectors, sides, widths, group):
    share = order.shape[0]
    degrees, half_lat = basis.shape[1:]
    combos = sectors * sides
    smem, vmem, hbm = (pl.BlockSpec(memory_space=space) for space in (pltpu.SMEM, pltpu.VMEM, pl.ANY))
    return pl.pallas_call(
        functools.partial(legendre_kernel, sides, widths, group),
        in_specs=[smem, smem, smem, vmem, hbm] + [vmem] * len(widths),
        out_specs=[pl.BlockSpec(memory_space=pltpu.HBM)] * (1 + len(widths)),
        out_shape=[
            jax.ShapeDtypeStruct((sectors, share, sides, degrees), F32),
            *[jax.ShapeDtypeStruct(wire.shape, BF16) for wire in received],
        ],
        scratch_shapes=[
            pltpu.VMEM((sectors, share, sides, degrees), F32),
            *[pltpu.VMEM(wire.shape, BF16) for wire in received],
            pltpu.VMEM((half_lat // LANES, 2 * combos * round_up(share, 8), LANES), F32),
            pltpu.VMEM((DEPTH, group, degrees, half_lat), BF16),
            pltpu.SemaphoreType.DMA((DEPTH, group)),
            pltpu.SemaphoreType.DMA((len(widths), 8)),
            pltpu.SemaphoreType.DMA,
        ],
        cost_estimate=pl.CostEstimate(
            flops=4 * share * degrees * half_lat * 2 * combos,
            bytes_accessed=2 * share * degrees * half_lat,
            transcendentals=0,
        ),
        compiler_params=pltpu.CompilerParams(vmem_limit_bytes=LEGENDRE_LIMIT),
        name="legendre",
    )(place, order, blocks, damping, basis, *received)


def degree_order(counts):
    size = counts.shape[0]
    ids = jnp.arange(size, dtype=jnp.int32)
    ahead = (counts[None, :] > counts[:, None]) | ((counts[None, :] == counts[:, None]) & (ids[None, :] < ids[:, None]))
    rank = jnp.sum(ahead.astype(jnp.int32), axis=1)
    placed = rank[:, None] == ids[None, :]
    order = jnp.sum(jnp.where(placed, ids[:, None], 0), axis=0)
    sorted_counts = jnp.sum(jnp.where(placed, counts[:, None], 0), axis=0)
    group = max(g for g in range(1, 6) if size % g == 0)
    return order, (sorted_counts[::group] + (STEP - 1)) // STEP, group


def body(wind_u, wind_v, basis, wave_slots, degree_count, viscosity):
    sectors = lax.axis_size("lon")
    owners = lax.axis_size("lat")
    sector_index = lax.axis_index("lon")
    owner_index = lax.axis_index("lat")
    levels, lat_rows, lon_cols = wind_u.shape
    capacity, degrees, half_lat = basis.shape
    waves = wave_slots.shape[0]
    slot_total = capacity * owners
    assert levels == sectors and sectors & (sectors - 1) == 0
    rows = 2 * lat_rows
    share = -(-capacity // sectors)
    padded = round_up(share, 8)
    length = sectors * lon_cols
    masks = [sectors // 2] + [mask for mask in range(sectors - 1, 0, -1) if mask != sectors // 2] + [0]

    def across(value, mask):
        return lax.ppermute(value, "lon", [(i, i ^ mask) for i in range(sectors)]) if mask else value

    def partners(some):
        return jnp.stack([sector_index ^ mask for mask in some]).astype(jnp.int32)

    far, rest = masks[:1], masks[1:]
    widths = chunk_widths(lat_rows)
    small_first = list(range(len(widths)))[::-1]

    first_made = wind_products(wind_u, wind_v, far, widths)
    lines = {}
    for chunk in small_first[:1]:
        for mask in far:
            lines[chunk, mask] = across(first_made[chunk, mask], mask)
    made = {**first_made, **wind_products(wind_u, wind_v, rest, widths)}
    for chunk in small_first:
        for mask in masks:
            if (chunk, mask) not in lines:
                lines[chunk, mask] = across(made[chunk, mask], mask)

    slot_ids = jnp.arange(slot_total, dtype=jnp.int32)
    wave_ids = jnp.arange(waves, dtype=jnp.int32)
    places = jnp.arange(owners * sectors * padded, dtype=jnp.int32)
    place_owner, place_sector, place_slot = places // (sectors * padded), places // padded % sectors, places % padded
    in_owner = place_sector * share + place_slot
    named = jnp.where((place_slot < share) & (in_owner < capacity), place_owner * capacity + in_owner, -1)
    one_hot = (named[:, None] == wave_slots[None, :]).astype(BF16)
    one_hot_turned = (wave_slots[:, None] == named[None, :]).astype(BF16)
    forward_table = wave_table(lon_cols, waves, length, True)
    backward_table = wave_table(waves, lon_cols, length, False)
    turns = sector_turns(sectors, waves)

    def turns_of(some):
        at = partners(some)
        return tuple(jnp.take(turn, at, axis=0) for turn in turns)

    first = sector_index * share
    local_ids = jnp.arange(share, dtype=jnp.int32)
    inside = first + local_ids < capacity
    at = owner_index * capacity + jnp.minimum(first + local_ids, capacity - 1)
    here = at[:, None] == wave_slots[None, :]
    wave_here = jnp.sum(jnp.where(here, wave_ids[None, :], 0), axis=1)
    count_here = jnp.where(inside, jnp.sum(jnp.where(here, degree_count[None, :], 0), axis=1), 0)
    degree_ids = jnp.arange(degrees, dtype=jnp.int32)
    total_degree = wave_here[:, None] + degree_ids[None, :]
    scaled = (total_degree * (total_degree + 1)).astype(F32) / float(degrees * (degrees + 1))
    kept = degree_ids[None, :] < count_here[:, None]
    sides = 4
    rates = jnp.repeat(viscosity, sides)
    damping = 1.0 / (1.0 + rates[None, :, None] * (scaled * scaled)[:, None, :])
    damping = jnp.where(kept[:, None, :], damping * (1.0 / math.sqrt(2 * half_lat)), 0.0)
    order, blocks, group = degree_order(count_here)

    by_arrival = list(dict.fromkeys([0, *[mask for mask in reversed(masks) if mask < sectors // 2], *masks]))
    early, late = by_arrival[:-1], by_arrival[-1:]
    received = [None] * len(widths)
    for chunk in small_first:
        own = {mask: lines[chunk, mask] for mask in masks}
        if chunk == 0:
            sums = forward([own[mask] for mask in early], forward_table, turns_of(early))
            fourier = forward([own[mask] for mask in late], forward_table, turns_of(late), sums, (one_hot, share))
        else:
            fourier = forward([own[mask] for mask in by_arrival], forward_table, turns_of(by_arrival), None, (one_hot, share))
        received[chunk] = lax.all_to_all(fourier, ("lat", "lon"), split_axis=0, concat_axis=0, tiled=True)
    place = jnp.stack([first, sector_index]).astype(jnp.int32)
    spectral, *returned = legendre(
        received, basis, damping, place, order, blocks, sectors, sides, widths, group
    )

    exact = sectors in (1, 2, 4)
    far_turns, rest_turns = turns_of(far), turns_of(rest)
    south, _ = band_place(owner_index, owners)
    back = {}
    for chunk, width in enumerate(widths):
        regrouped = lax.all_to_all(returned[chunk], ("lat", "lon"), split_axis=0, concat_axis=0, tiled=True)
        ids = jnp.arange(width, dtype=jnp.int32)
        mirror = (ids[:, None] == jnp.where(south, width - 1 - ids, ids)[None, :]).astype(BF16)
        far_lines, by_wave = backward_first(regrouped, backward_table, far_turns, one_hot_turned, mirror, exact)
        back[chunk, far[0]] = across(far_lines, far[0])
        others = backward_rest(by_wave, backward_table, rest_turns, exact)
        for mask, value in zip(rest, others):
            back[chunk, mask] = across(value, mask)

    coefficients = jnp.zeros((sectors * share, 1, 2, 2, degrees), F32)
    for mask in masks:
        own = across(spectral[mask].astype(BF16), mask).astype(F32).reshape(share, 1, 2, 2, degrees)
        coefficients = lax.dynamic_update_slice_in_dim(coefficients, own, (sector_index ^ mask) * share, 0)

    arrival = [(chunk, mask) for chunk in range(len(widths)) for mask in by_arrival]
    cuts = [0, len(early), len(arrival) - 1, len(arrival)]
    tendency = None
    for begin, end in zip(cuts, cuts[1:]):
        if end > begin:
            tendency = placed(back, arrival[begin:end], widths, (sectors, rows, lon_cols), tendency)
    return coefficients[:capacity], tendency.reshape(levels, 2, lat_rows, lon_cols)


def solution(mesh):
    return jax.shard_map(
        body,
        mesh=mesh,
        in_specs=(
            P(None, "lat", "lon"),
            P(None, "lat", "lon"),
            P("lat", None, None),
            P(),
            P(),
            P(),
        ),
        out_specs=(P("lat", "lon", None, None, None), P(None, None, "lat", "lon")),
        check_vma=False,
    )
```

```python
import functools
import math

import jax
import jax.numpy as jnp
import numpy as np
from jax import lax
from jax.experimental import pallas as pl
from jax.experimental.pallas import tpu as pltpu
from jax.sharding import PartitionSpec as P


BF16 = jnp.bfloat16
F32 = jnp.float32
MIB = 1024 * 1024
VMEM_LIMIT = 20 * MIB
LEGENDRE_LIMIT = 36 * MIB
WHOLE_LIMIT = 60 * MIB
STEP = 128
LANES = 128
DEPTH = 3
NT = (((1,), (1,)), ((), ()))
NN = (((1,), (0,)), ((), ()))


def dot(a, b, dims=NN):
    return lax.dot_general(a, b, dims, preferred_element_type=F32)


def phases(rows, columns, length):
    turns = 2.0 * np.pi * (rows[:, None] * columns[None, :] % length) / length
    return np.cos(turns), np.sin(turns)


def table_kernel(interleaved, near_cos, near_sin, far_cos, far_sin, named, wave_slots, out, hot_out, space, hot, sems):
    near, lanes = near_cos.shape
    steps = far_cos.shape[0]
    count = steps * near
    size = min(LANES, lanes)
    if interleaved:
        hot[...] = (named[...] == wave_slots[...]).astype(F32).astype(BF16)
    else:
        slots_down = jnp.broadcast_to(wave_slots[...].astype(F32), (8, wave_slots.shape[1])).T[:, :1]
        hot[...] = (slots_down == named[...].astype(F32)).astype(F32).astype(BF16)
    copies = [pltpu.make_async_copy(hot, hot_out, sems.at[0])]
    copies[0].start()
    for step in range(steps):
        cos = far_cos[step] * near_cos[...] - far_sin[step] * near_sin[...]
        sin = far_sin[step] * near_cos[...] + far_cos[step] * near_sin[...]
        high = (cos.astype(BF16), sin.astype(BF16))
        low = tuple((value - top.astype(F32)).astype(BF16) for value, top in zip((cos, sin), high))
        for term, pair in enumerate((high, low)):
            for which, value in enumerate(pair):
                if interleaved:
                    row = term * count + step * near
                    for block in range(lanes // size):
                        lane = (2 * block + which) * size
                        space[row : row + near, lane : lane + size] = value[:, block * size : (block + 1) * size]
                else:
                    row = (2 * term + which) * count + step * near
                    space[row : row + near, :] = value
    copies.append(pltpu.make_async_copy(space, out, sems.at[1]))
    copies[1].start()
    for copy in copies:
        copy.wait()


def wave_table(rows, columns, length, interleaved, named, wave_slots):
    near = 32
    near_cos, near_sin = phases(np.arange(near), np.arange(columns), length)
    far_cos, far_sin = phases(np.arange(rows // near) * near, np.arange(columns), length)
    scaling = 1.0 / math.sqrt(length)
    shape = (2 * rows, 2 * columns) if interleaved else (4 * rows, columns)
    waves, slots = wave_slots.shape[0], named.shape[0]
    hot_shape = (slots, waves) if interleaved else (waves, slots)
    return pl.pallas_call(
        functools.partial(table_kernel, interleaved),
        out_specs=[pl.BlockSpec(memory_space=pltpu.HBM)] * 2,
        out_shape=[jax.ShapeDtypeStruct(shape, BF16), jax.ShapeDtypeStruct(hot_shape, BF16)],
        scratch_shapes=[pltpu.VMEM(shape, BF16), pltpu.VMEM(hot_shape, BF16), pltpu.SemaphoreType.DMA((2,))],
        compiler_params=pltpu.CompilerParams(vmem_limit_bytes=WHOLE_LIMIT),
        name="wave_table",
    )(
        jnp.asarray(near_cos * scaling, F32),
        jnp.asarray(near_sin * scaling, F32),
        jnp.asarray(far_cos[:, None, :], F32),
        jnp.asarray(far_sin[:, None, :], F32),
        named[:, None] if interleaved else named[None, :],
        wave_slots[None, :],
    )


def sector_turns(sectors, waves):
    both = phases(np.arange(sectors), np.arange(waves), sectors)
    return tuple(jnp.asarray(np.round(turn, 12)[:, None, :], F32) for turn in both)


def chunk_widths(lat_rows):
    main = lat_rows // LANES * LANES
    return (main, lat_rows - main) if main and 2 * (lat_rows - main) == LANES else (lat_rows,)


def chunk_start(widths, chunk, near):
    if len(widths) == 1:
        return 0
    odd = near % 2
    return odd * widths[1] if chunk == 0 else (1 - odd) * widths[0]


def band_place(owner_index, owners):
    south = owner_index >= owners // 2
    return south, jnp.where(south, owners - 1 - owner_index, owner_index)


def product_kernel(masks, widths, wind_u, wind_v, *refs):
    outs, (space, sems) = refs[:-2], refs[-2:]
    _, lat_rows, columns = wind_u.shape
    south, near = band_place(lax.axis_index("lat"), lax.axis_size("lat"))
    pieces = sems.shape[2]
    size = columns // pieces
    copies = {}
    for i, mask in enumerate(masks):
        level = lax.axis_index("lon") ^ mask
        for piece in range(pieces):
            own = pl.ds(piece * size, size)
            for which, wind in enumerate((wind_u, wind_v)):
                copy = pltpu.make_async_copy(
                    wind.at[level, :, own], space.at[i, which, :, own], sems.at[i, which, piece]
                )
                copy.start()
                copies[i, piece, which] = copy
    chosen = []
    for chunk, width in enumerate(widths):
        start = chunk_start(widths, chunk, near)
        ids = start + lax.broadcasted_iota(jnp.int32, (width, lat_rows), 0)
        lats = lax.broadcasted_iota(jnp.int32, (width, lat_rows), 1)
        chosen.append((lats == jnp.where(south, lat_rows - 1 - ids, ids)).astype(F32).astype(BF16))
    for i in range(len(masks)):
        for piece in range(pieces):
            own = pl.ds(piece * size, size)
            copies[i, piece, 0].wait()
            copies[i, piece, 1].wait()
            u, v = space[i, 0, :, own], space[i, 1, :, own]
            for field, product in enumerate((u * v, u * u - v * v)):
                product = product.astype(BF16)
                for chunk, width in enumerate(widths):
                    outs[i * len(widths) + chunk][field * width : (field + 1) * width, own] = dot(
                        chosen[chunk], product
                    ).astype(BF16)


def wind_products(wind_u, wind_v, masks, widths):
    _, lat_rows, columns = wind_u.shape
    hbm, vmem = pl.BlockSpec(memory_space=pl.ANY), pl.BlockSpec(memory_space=pltpu.VMEM)
    outs = pl.pallas_call(
        functools.partial(product_kernel, masks, widths),
        in_specs=[hbm, hbm],
        out_specs=[vmem] * (len(masks) * len(widths)),
        out_shape=[jax.ShapeDtypeStruct((2 * width, columns), BF16) for _ in masks for width in widths],
        scratch_shapes=[
            pltpu.VMEM((len(masks), 2, lat_rows, columns), F32),
            pltpu.SemaphoreType.DMA((len(masks), 2, columns // LANES if columns % LANES == 0 else 1)),
        ],
        compiler_params=pltpu.CompilerParams(vmem_limit_bytes=WHOLE_LIMIT),
        name="wind_products",
    )(wind_u, wind_v)
    return {
        (chunk, mask): outs[i * len(widths) + chunk] for i, mask in enumerate(masks) for chunk in range(len(widths))
    }


def forward_kernel(count, begun, ends, *refs):
    lines, refs = refs[:count], refs[count:]
    table, turn_cos, turn_sin = refs[:3]
    earlier, refs = (refs[3], refs[4:]) if begun else (None, refs[3:])
    step = pl.program_id(0)
    size = table.shape[1] // 2
    rows = lines[0].shape[0]
    both = jnp.concatenate([jnp.concatenate([line[...]] * 2, axis=1) for line in lines], axis=0)
    sums = dot(both, table[...])
    real, imag = (earlier[0], earlier[1]) if begun else (None, None)
    for i in range(count):
        own = sums[i * rows : (i + 1) * rows]
        own_cos, own_sin = own[:, :size], own[:, size:]
        cos, sin = turn_cos[i], turn_sin[i]
        own_real, own_imag = own_cos * cos - own_sin * sin, own_cos * sin + own_sin * cos
        real, imag = (own_real, own_imag) if real is None else (real + own_real, imag + own_imag)
    if not ends:
        refs[0][0], refs[0][1] = real, imag
        return
    one_hot, out, by_wave, by_slot, wire, sems = refs
    devices, wire_rows, lanes = out.shape
    padded = one_hot.shape[0] // devices
    blocks = 2 * rows // lanes
    share = wire_rows // blocks
    place = pl.ds(pl.multiple_of(step * size, size), size)
    by_wave[0, :, place] = real.astype(BF16)
    by_wave[1, :, place] = (-imag).astype(BF16)

    @pl.when(step == pl.num_programs(0) - 1)
    def _():
        for part in range(2):
            by_slot[:, part * rows : (part + 1) * rows] = dot(one_hot[...], by_wave[part], NT)
        copies, out_step = [], devices // sems.shape[0]
        for device in range(devices):
            own = by_slot[device * padded : (device + 1) * padded, :]
            wire[device] = pack_rows(
                [own[:share, block * lanes : (block + 1) * lanes] for block in range(blocks)]
            ).astype(BF16)
            if (device + 1) % out_step == 0:
                piece = pl.ds(device + 1 - out_step, out_step)
                copies.append(pltpu.make_async_copy(wire.at[piece], out.at[piece], sems.at[device // out_step]))
                copies[-1].start()
        for copy in copies:
            copy.wait()


def forward(lines, table, turns, earlier=None, end=None):
    rows, columns = lines[0].shape
    waves = table.shape[1] // 2
    size = min(LANES, waves)
    turn_spec = pl.BlockSpec((len(lines), 1, size), lambda i: (0, 0, i))
    sum_spec = pl.BlockSpec((2, rows, size), lambda i: (0, 0, i))
    args = list(lines) + [table, *turns]
    in_specs = [pl.BlockSpec((rows, columns), lambda i: (0, 0))] * len(lines)
    in_specs += [pl.BlockSpec((2 * columns, 2 * size), lambda i: (0, i)), turn_spec, turn_spec]
    if earlier is not None:
        args.append(earlier)
        in_specs.append(sum_spec)
    if end is None:
        out_shape, out_spec, scratch = jax.ShapeDtypeStruct((2, rows, waves), F32), sum_spec, []
    else:
        one_hot, share = end
        slots = one_hot.shape[0]
        lanes = wire_lanes(rows)
        out = (slots // round_up(share, 8), share * (2 * rows // lanes), lanes)
        args.append(one_hot)
        in_specs.append(pl.BlockSpec((slots, waves), lambda i: (0, 0)))
        out_shape, out_spec = jax.ShapeDtypeStruct(out, BF16), pl.BlockSpec(memory_space=pltpu.HBM)
        scratch = [pltpu.VMEM((2, rows, waves), BF16), pltpu.VMEM((slots, 2 * rows), F32)]
        scratch += [pltpu.VMEM(out, BF16), pltpu.SemaphoreType.DMA((4,))]
    return pl.pallas_call(
        functools.partial(forward_kernel, len(lines), earlier is not None, end is not None),
        grid=(waves // size,),
        in_specs=in_specs,
        out_specs=out_spec,
        out_shape=out_shape,
        scratch_shapes=scratch,
        cost_estimate=pl.CostEstimate(
            flops=8 * len(lines) * rows * columns * waves, bytes_accessed=10**7, transcendentals=0
        ),
        compiler_params=pltpu.CompilerParams(vmem_limit_bytes=VMEM_LIMIT),
        name="forward",
    )(*args)


def sector_lines(exact, by_wave, table, turn_cos, turn_sin):
    count = turn_cos.shape[0]
    left = []
    for i in range(count):
        cos, sin = turn_cos[i], turn_sin[i]
        own_real, own_imag = by_wave[0].astype(F32), by_wave[1].astype(F32)
        real = own_real * cos - own_imag * sin
        minus = -(own_real * sin) - own_imag * cos
        left.append(jnp.concatenate([real, minus], axis=1))
    left = jnp.concatenate(left, axis=0) if count > 1 else left[0]
    high = left.astype(BF16)
    total = dot(jnp.concatenate([high, high], axis=1), table[...])
    if not exact:
        low = (left - high.astype(F32)).astype(BF16)
        total += dot(low, table[: low.shape[1]])
    return total.astype(BF16)


def backward_first_kernel(
    exact, wire, table_hbm, turn_cos, turn_sin, one_hot_hbm, mirror, out, by_wave_out, by_slot, table, one_hot, by_wave, sems
):
    one_hot_copy = pltpu.make_async_copy(one_hot_hbm, one_hot, sems.at[0])
    table_copy = pltpu.make_async_copy(table_hbm, table, sems.at[1])
    by_wave_copy = pltpu.make_async_copy(by_wave, by_wave_out, sems.at[2])
    one_hot_copy.start()
    table_copy.start()
    devices, _, lanes = wire.shape
    rows = out.shape[0]
    waves = one_hot.shape[0]
    width = mirror.shape[0]
    padded = by_slot.shape[0] // devices
    blocks = 2 * rows // lanes
    for device in range(devices):
        for block, piece in enumerate(unpack_rows(wire[device].astype(F32), blocks, padded)):
            by_slot[device * padded : (device + 1) * padded, block * lanes : (block + 1) * lanes] = piece.astype(BF16)
    one_hot_copy.wait()
    wave_ids = lax.broadcasted_iota(jnp.int32, (1, waves), 1)
    weight = jnp.where(wave_ids == 0, 1.0, 2.0).astype(F32)
    for part in range(2):
        ordered = dot(one_hot[...], by_slot[:, part * rows : (part + 1) * rows]).astype(BF16)
        for field in range(2):
            own = slice(field * width, (field + 1) * width)
            by_wave[part, own, :] = (dot(mirror[...], ordered[:, own], NT) * weight).astype(BF16)
    by_wave_copy.start()
    table_copy.wait()
    out[...] = sector_lines(exact, by_wave, table, turn_cos, turn_sin)
    by_wave_copy.wait()


def backward_first(wire, table, turns, one_hot, mirror, exact):
    rows = 2 * mirror.shape[0]
    waves, slots = one_hot.shape
    vmem, hbm = pl.BlockSpec(memory_space=pltpu.VMEM), pl.BlockSpec(memory_space=pl.ANY)
    return pl.pallas_call(
        functools.partial(backward_first_kernel, exact),
        in_specs=[vmem, hbm, vmem, vmem, hbm, vmem],
        out_specs=[vmem, pl.BlockSpec(memory_space=pltpu.HBM)],
        out_shape=[
            jax.ShapeDtypeStruct((rows, table.shape[1]), BF16),
            jax.ShapeDtypeStruct((2, rows, waves), BF16),
        ],
        scratch_shapes=[
            pltpu.VMEM((slots, 2 * rows), BF16),
            pltpu.VMEM(table.shape, BF16),
            pltpu.VMEM(one_hot.shape, BF16),
            pltpu.VMEM((2, rows, waves), BF16),
            pltpu.SemaphoreType.DMA((3,)),
        ],
        cost_estimate=pl.CostEstimate(flops=10**9, bytes_accessed=10**7, transcendentals=0),
        compiler_params=pltpu.CompilerParams(vmem_limit_bytes=VMEM_LIMIT),
        name="backward_first",
    )(wire, table, *turns, one_hot, mirror)


def backward_rest_kernel(exact, by_wave, table, turn_cos, turn_sin, *outs):
    rows = outs[0].shape[0]
    total = sector_lines(exact, by_wave, table, turn_cos, turn_sin)
    for i, out in enumerate(outs):
        out[...] = total[i * rows : (i + 1) * rows]


def backward_rest(by_wave, table, turns, exact):
    _, rows, _ = by_wave.shape
    count = turns[0].shape[0]
    vmem = pl.BlockSpec(memory_space=pltpu.VMEM)
    return pl.pallas_call(
        functools.partial(backward_rest_kernel, exact),
        in_specs=[vmem] * 4,
        out_specs=[vmem] * count,
        out_shape=[jax.ShapeDtypeStruct((rows, table.shape[1]), BF16)] * count,
        cost_estimate=pl.CostEstimate(flops=3 * 10**9, bytes_accessed=10**7, transcendentals=0),
        compiler_params=pltpu.CompilerParams(vmem_limit_bytes=WHOLE_LIMIT),
        name="backward_rest",
    )(by_wave, table, *turns)


def placing_kernel(parts, widths, *refs):
    blocks, (out, wide, sems) = refs[: len(parts)], refs[-3:]
    _, rows, _ = out.shape
    lat_rows = rows // 2
    south, near = band_place(lax.axis_index("lat"), lax.axis_size("lat"))
    copies = []
    for i, (chunk, mask) in enumerate(parts):
        width = widths[chunk]
        start = chunk_start(widths, chunk, near)
        start = jnp.where(south, lat_rows - start - width, start)
        level = lax.axis_index("lon") ^ mask
        for field in range(2):
            own = slice(field * width, (field + 1) * width)
            wide[i, own] = blocks[i][own].astype(F32)
            place = pl.ds(pl.multiple_of(field * lat_rows + start, math.gcd(*widths, lat_rows)), width)
            copies.append(pltpu.make_async_copy(wide.at[i, own], out.at[level, place], sems.at[i, field]))
            copies[-1].start()
    for copy in copies:
        copy.wait()


def placed(blocks, parts, widths, shape, earlier=None):
    count = len(parts)
    vmem, hbm = pl.BlockSpec(memory_space=pltpu.VMEM), pl.BlockSpec(memory_space=pl.ANY)
    more = () if earlier is None else (earlier,)
    return pl.pallas_call(
        functools.partial(placing_kernel, parts, widths),
        in_specs=[vmem] * count + [hbm] * len(more),
        out_specs=hbm,
        out_shape=jax.ShapeDtypeStruct(shape, F32),
        scratch_shapes=[
            pltpu.VMEM((count, 2 * max(widths[chunk] for chunk, _ in parts), shape[2]), F32),
            pltpu.SemaphoreType.DMA((count, 2)),
        ],
        input_output_aliases={count: 0} if more else {},
        compiler_params=pltpu.CompilerParams(vmem_limit_bytes=VMEM_LIMIT),
        name="placed",
    )(*[blocks[part] for part in parts], *more)


def round_up(value, unit):
    return -(-value // unit) * unit


def pack_rows(pieces):
    share = pieces[0].shape[0]
    main = share // 8 * 8
    parts = [piece[:main] for piece in pieces] if main else []
    parts += [piece[main:] for piece in pieces] if main < share else []
    return jnp.concatenate(parts, axis=0) if len(parts) > 1 else parts[0]


def unpack_rows(value, count, fill):
    share = value.shape[0] // count
    main = share // 8 * 8
    rest = share - main
    pieces = []
    for i in range(count):
        parts = [value[i * main : (i + 1) * main]] if main else []
        parts += [value[count * main + i * rest : count * main + (i + 1) * rest]] if rest else []
        parts += [jnp.zeros((fill - share, value.shape[1]), value.dtype)] if fill > share else []
        pieces.append(jnp.concatenate(parts, axis=0) if len(parts) > 1 else parts[0])
    return pieces


def wire_lanes(rows):
    return LANES if 2 * rows % LANES == 0 else 2 * rows


def legendre_kernel(sides, widths, group, place, order, blocks, damping, basis, *rest):
    wires = len(widths)
    received, rest = rest[:wires], rest[wires:]
    spectral_out, returned_out, rest = rest[0], rest[1 : 1 + wires], rest[1 + wires :]
    spectral, returned, (held, buffer, sems, out_sems, spectral_sem) = rest[0], rest[1 : 1 + wires], rest[1 + wires :]
    lat_rows = sum(widths)
    devices = received[0].shape[0]
    sectors, share = spectral.shape[:2]
    slots, degrees, half_lat = basis.shape
    sources = devices // sectors
    fields = sides // 2
    combos = sectors * sides
    lane_blocks = held.shape[0]
    stride = held.shape[1] // (2 * combos)
    groups = share // group
    most = degrees // STEP
    scale = 1.0 / math.sqrt(degrees)
    out_step = devices // out_sems.shape[1]

    def copies(index, count):
        ring = lax.rem(index, DEPTH)
        rows = pl.ds(0, count * STEP)
        return [
            pltpu.make_async_copy(
                basis.at[jnp.minimum(place[0] + order[index * group + i], slots - 1), rows, :],
                buffer.at[ring, i, rows, :],
                sems.at[ring, i],
            )
            for i in range(group)
        ]

    def fetch(index):
        for count in range(1, most + 1):

            @pl.when(blocks[index] == count)
            def _():
                for copy in copies(index, count):
                    copy.start()

    for index in range(min(DEPTH - 1, groups)):
        fetch(index)

    def wire_pieces(wire, device, wire_block):
        source, sector = divmod(device, sectors)
        side, near = (0, source) if source < sources // 2 else (1, sources - 1 - source)
        lanes, chunk_width = received[wire].shape[2], widths[wire]
        begin = near * lat_rows + chunk_start(widths, wire, near)
        column, end = wire_block * lanes, (wire_block + 1) * lanes
        while column < end:
            part_field, lat = divmod(column, chunk_width)
            part, field = divmod(part_field, fields)
            row = (side * combos + sector * sides + field * 2 + part) * stride
            at = begin + lat
            width = min(end - column, chunk_width - lat, LANES - at % LANES)
            yield column - wire_block * lanes, width, row, at // LANES, at % LANES
            column += width

    for wire in range(wires):
        wire_blocks = received[wire].shape[1] // share
        for device in range(devices):
            own_blocks = unpack_rows(received[wire][device].astype(F32), wire_blocks, stride)
            for wire_block, piece in enumerate(own_blocks):
                for at, width, row, block, lane in wire_pieces(wire, device, wire_block):
                    held[block, row : row + stride, lane : lane + width] = piece[:, at : at + width]

    def load_slot(slot):
        rows = pl.ds(slot, 2 * combos, stride=stride)
        return jnp.concatenate([held[block, rows, :] for block in range(lane_blocks)], axis=1)

    def store_slot(slot, value):
        rows = pl.ds(slot, 2 * combos, stride=stride)
        for block in range(lane_blocks):
            held[block, rows, :] = value[:, block * LANES : (block + 1) * LANES]

    def one_group(index, count):
        ring = lax.rem(index, DEPTH)
        here = [order[index * group + i] for i in range(group)]
        if count == 0:
            for slot in here:
                for sector in range(sectors):
                    spectral[place[1] ^ sector, slot] = jnp.zeros(spectral.shape[2:], F32)
                store_slot(slot, jnp.zeros((2 * combos, half_lat), F32))
            return
        width = count * STEP
        for copy in copies(index, count):
            copy.wait()
        parity = 1.0 - 2.0 * (lax.broadcasted_iota(jnp.int32, (1, width), 1) % 2).astype(F32)
        left = [load_slot(slot).astype(BF16) for slot in here]
        sums = [dot(left[i], buffer[ring, i, :width, :], NT) for i in range(group)]
        damped = [
            (sums[i][:combos] + parity * sums[i][combos:]) * damping[slot, :, :width] for i, slot in enumerate(here)
        ]
        turned = [jnp.concatenate([value, parity * value], axis=0).astype(BF16) for value in damped]
        backs = [dot(turned[i], buffer[ring, i, :width, :]) * scale for i in range(group)]
        for i, slot in enumerate(here):
            for sector in range(sectors):
                spectral[place[1] ^ sector, slot, :, :width] = damped[i][sector * sides : (sector + 1) * sides]
                if width < degrees:
                    spectral[place[1] ^ sector, slot, :, width:] = jnp.zeros((sides, degrees - width), F32)
        for i, slot in enumerate(here):
            store_slot(slot, backs[i])

    def loop_body(index, carry):
        @pl.when(index + DEPTH - 1 < groups)
        def _():
            fetch(index + DEPTH - 1)

        for count in range(most + 1):
            pl.when(blocks[index] == count)(functools.partial(one_group, index, count))
        return carry

    lax.fori_loop(0, groups, loop_body, 0)

    spectral_copy = pltpu.make_async_copy(spectral, spectral_out, spectral_sem)
    spectral_copy.start()
    out_copies = []
    for wire in range(wires):
        wire_blocks = received[wire].shape[1] // share
        for device in range(devices):
            pieces = []
            for wire_block in range(wire_blocks):
                parts = [
                    held[block, row : row + share, lane : lane + width]
                    for _, width, row, block, lane in wire_pieces(wire, device, wire_block)
                ]
                pieces.append(jnp.concatenate(parts, axis=1) if len(parts) > 1 else parts[0])
            returned[wire][device] = pack_rows(pieces).astype(BF16)
            if (device + 1) % out_step == 0:
                part = pl.ds(device + 1 - out_step, out_step)
                copy = pltpu.make_async_copy(
                    returned[wire].at[part], returned_out[wire].at[part], out_sems.at[wire, device // out_step]
                )
                copy.start()
                out_copies.append(copy)
    for copy in (*out_copies, spectral_copy):
        copy.wait()


def legendre(received, basis, damping, place, order, blocks, sectors, sides, widths, group):
    share = order.shape[0]
    degrees, half_lat = basis.shape[1:]
    combos = sectors * sides
    smem, vmem, hbm = (pl.BlockSpec(memory_space=space) for space in (pltpu.SMEM, pltpu.VMEM, pl.ANY))
    return pl.pallas_call(
        functools.partial(legendre_kernel, sides, widths, group),
        in_specs=[smem, smem, smem, vmem, hbm] + [vmem] * len(widths),
        out_specs=[pl.BlockSpec(memory_space=pltpu.HBM)] * (1 + len(widths)),
        out_shape=[
            jax.ShapeDtypeStruct((sectors, share, sides, degrees), F32),
            *[jax.ShapeDtypeStruct(wire.shape, BF16) for wire in received],
        ],
        scratch_shapes=[
            pltpu.VMEM((sectors, share, sides, degrees), F32),
            *[pltpu.VMEM(wire.shape, BF16) for wire in received],
            pltpu.VMEM((half_lat // LANES, 2 * combos * round_up(share, 8), LANES), F32),
            pltpu.VMEM((DEPTH, group, degrees, half_lat), BF16),
            pltpu.SemaphoreType.DMA((DEPTH, group)),
            pltpu.SemaphoreType.DMA((len(widths), 8)),
            pltpu.SemaphoreType.DMA,
        ],
        cost_estimate=pl.CostEstimate(
            flops=4 * share * degrees * half_lat * 2 * combos,
            bytes_accessed=2 * share * degrees * half_lat,
            transcendentals=0,
        ),
        compiler_params=pltpu.CompilerParams(vmem_limit_bytes=LEGENDRE_LIMIT),
        name="legendre",
    )(place, order, blocks, damping, basis, *received)


def degree_order(counts):
    size = counts.shape[0]
    ids = jnp.arange(size, dtype=jnp.int32)
    ahead = (counts[None, :] > counts[:, None]) | ((counts[None, :] == counts[:, None]) & (ids[None, :] < ids[:, None]))
    rank = jnp.sum(ahead.astype(jnp.int32), axis=1)
    placed = rank[:, None] == ids[None, :]
    order = jnp.sum(jnp.where(placed, ids[:, None], 0), axis=0)
    sorted_counts = jnp.sum(jnp.where(placed, counts[:, None], 0), axis=0)
    group = max(g for g in range(1, 6) if size % g == 0)
    return order, (sorted_counts[::group] + (STEP - 1)) // STEP, group


def body(wind_u, wind_v, basis, wave_slots, degree_count, viscosity):
    sectors = lax.axis_size("lon")
    owners = lax.axis_size("lat")
    sector_index = lax.axis_index("lon")
    owner_index = lax.axis_index("lat")
    levels, lat_rows, lon_cols = wind_u.shape
    capacity, degrees, half_lat = basis.shape
    waves = wave_slots.shape[0]
    assert levels == sectors and sectors & (sectors - 1) == 0
    rows = 2 * lat_rows
    share = -(-capacity // sectors)
    padded = round_up(share, 8)
    length = sectors * lon_cols
    masks = [sectors // 2] + [mask for mask in range(sectors - 1, 0, -1) if mask != sectors // 2] + [0]

    def across(value, mask):
        return lax.ppermute(value, "lon", [(i, i ^ mask) for i in range(sectors)]) if mask else value

    def partners(some):
        return jnp.stack([sector_index ^ mask for mask in some]).astype(jnp.int32)

    far, rest = masks[:1], masks[1:]
    widths = chunk_widths(lat_rows)
    small_first = list(range(len(widths)))[::-1]

    first_made = wind_products(wind_u, wind_v, far, widths)
    lines = {}
    for chunk in small_first[:1]:
        for mask in far:
            lines[chunk, mask] = across(first_made[chunk, mask], mask)
    made = {**first_made, **wind_products(wind_u, wind_v, rest, widths)}
    for chunk in small_first:
        for mask in masks:
            if (chunk, mask) not in lines:
                lines[chunk, mask] = across(made[chunk, mask], mask)

    wave_ids = jnp.arange(waves, dtype=jnp.int32)
    places = jnp.arange(owners * sectors * padded, dtype=jnp.int32)
    place_owner, place_sector, place_slot = places // (sectors * padded), places // padded % sectors, places % padded
    in_owner = place_sector * share + place_slot
    named = jnp.where((place_slot < share) & (in_owner < capacity), place_owner * capacity + in_owner, -1)
    forward_table, one_hot = wave_table(lon_cols, waves, length, True, named, wave_slots)
    backward_table, one_hot_turned = wave_table(waves, lon_cols, length, False, named, wave_slots)
    forward_table, one_hot, backward_table, one_hot_turned = (
        pltpu.with_memory_space_constraint(value, pltpu.HBM)
        for value in (forward_table, one_hot, backward_table, one_hot_turned)
    )
    turns = sector_turns(sectors, waves)

    def turns_of(some):
        at = partners(some)
        return tuple(jnp.take(turn, at, axis=0) for turn in turns)

    first = sector_index * share
    local_ids = jnp.arange(share, dtype=jnp.int32)
    inside = first + local_ids < capacity
    at = owner_index * capacity + jnp.minimum(first + local_ids, capacity - 1)
    here = at[:, None] == wave_slots[None, :]
    wave_here = jnp.sum(jnp.where(here, wave_ids[None, :], 0), axis=1)
    count_here = jnp.where(inside, jnp.sum(jnp.where(here, degree_count[None, :], 0), axis=1), 0)
    degree_ids = jnp.arange(degrees, dtype=jnp.int32)
    total_degree = wave_here[:, None] + degree_ids[None, :]
    scaled = (total_degree * (total_degree + 1)).astype(F32) / float(degrees * (degrees + 1))
    kept = degree_ids[None, :] < count_here[:, None]
    sides = 4
    rates = jnp.repeat(viscosity, sides)
    damping = 1.0 / (1.0 + rates[None, :, None] * (scaled * scaled)[:, None, :])
    damping = jnp.where(kept[:, None, :], damping * (1.0 / math.sqrt(2 * half_lat)), 0.0)
    order, blocks, group = degree_order(count_here)

    by_arrival = list(dict.fromkeys([0, *[mask for mask in reversed(masks) if mask < sectors // 2], *masks]))
    early, late = by_arrival[:-1], by_arrival[-1:]
    received = [None] * len(widths)
    for chunk in small_first:
        own = {mask: lines[chunk, mask] for mask in masks}
        if chunk == 0:
            sums = forward([own[mask] for mask in early], forward_table, turns_of(early))
            fourier = forward([own[mask] for mask in late], forward_table, turns_of(late), sums, (one_hot, share))
        else:
            fourier = forward([own[mask] for mask in by_arrival], forward_table, turns_of(by_arrival), None, (one_hot, share))
        received[chunk] = lax.all_to_all(fourier, ("lat", "lon"), split_axis=0, concat_axis=0, tiled=True)
    place = jnp.stack([first, sector_index]).astype(jnp.int32)
    spectral, *returned = legendre(
        received, basis, damping, place, order, blocks, sectors, sides, widths, group
    )

    exact = sectors in (1, 2, 4)
    far_turns, rest_turns = turns_of(far), turns_of(rest)
    south, _ = band_place(owner_index, owners)
    back, regrouped = {}, []
    for chunk, wire in enumerate(returned):
        if chunk:
            wire, regrouped[-1] = lax.optimization_barrier((wire, regrouped[-1]))
        regrouped.append(lax.all_to_all(wire, ("lat", "lon"), split_axis=0, concat_axis=0, tiled=True))
    for chunk, width in enumerate(widths):
        ids = jnp.arange(width, dtype=jnp.int32)
        mirror = (ids[:, None] == jnp.where(south, width - 1 - ids, ids)[None, :]).astype(BF16)
        far_lines, by_wave = backward_first(regrouped[chunk], backward_table, far_turns, one_hot_turned, mirror, exact)
        back[chunk, far[0]] = across(far_lines, far[0])
        by_wave = pltpu.with_memory_space_constraint(by_wave, pltpu.HBM)
        others = backward_rest(by_wave, backward_table, rest_turns, exact)
        for mask, value in zip(rest, others):
            back[chunk, mask] = across(value, mask)

    coefficients = jnp.zeros((sectors * share, 1, 2, 2, degrees), F32)
    for mask in masks:
        own = across(spectral[mask].astype(BF16), mask).astype(F32).reshape(share, 1, 2, 2, degrees)
        coefficients = lax.dynamic_update_slice_in_dim(coefficients, own, (sector_index ^ mask) * share, 0)

    arrival = [(chunk, mask) for chunk in range(len(widths)) for mask in by_arrival]
    cuts = [0, len(early), len(arrival) - 1, len(arrival)]
    tendency = None
    for begin, end in zip(cuts, cuts[1:]):
        if end > begin:
            tendency = placed(back, arrival[begin:end], widths, (sectors, rows, lon_cols), tendency)
    return coefficients[:capacity], tendency.reshape(levels, 2, lat_rows, lon_cols)


def solution(mesh):
    return jax.shard_map(
        body,
        mesh=mesh,
        in_specs=(
            P(None, "lat", "lon"),
            P(None, "lat", "lon"),
            P("lat", None, None),
            P(),
            P(),
            P(),
        ),
        out_specs=(P("lat", "lon", None, None, None), P(None, None, "lat", "lon")),
        check_vma=False,
    )
```

```python
import functools
import math

import jax
import jax.numpy as jnp
import numpy as np
from jax import lax
from jax.experimental import pallas as pl
from jax.experimental.pallas import tpu as pltpu
from jax.sharding import PartitionSpec as P


BF16 = jnp.bfloat16
F32 = jnp.float32
MIB = 1024 * 1024
VMEM_LIMIT = 24 * MIB
LEGENDRE_LIMIT = 36 * MIB
WHOLE_LIMIT = 60 * MIB
STEP = 128
LANES = 128
DEPTH = 3
NT = (((1,), (1,)), ((), ()))
NN = (((1,), (0,)), ((), ()))


def dot(a, b, dims=NN):
    return lax.dot_general(a, b, dims, preferred_element_type=F32)


def phases(rows, columns, length):
    turns = 2.0 * np.pi * (rows[:, None] * columns[None, :] % length) / length
    return np.cos(turns), np.sin(turns)


def table_kernel(interleaved, near_cos, near_sin, far_cos, far_sin, named, wave_slots, out, hot_out, space, hot, sems):
    near, lanes = near_cos.shape
    steps = far_cos.shape[0]
    count = steps * near
    size = min(LANES, lanes)
    if interleaved:
        hot[...] = (named[...] == wave_slots[...]).astype(F32).astype(BF16)
    else:
        slots_down = jnp.broadcast_to(wave_slots[...].astype(F32), (8, wave_slots.shape[1])).T[:, :1]
        hot[...] = (slots_down == named[...].astype(F32)).astype(F32).astype(BF16)
    copies = [pltpu.make_async_copy(hot, hot_out, sems.at[0])]
    copies[0].start()
    for step in range(steps):
        cos = far_cos[step] * near_cos[...] - far_sin[step] * near_sin[...]
        sin = far_sin[step] * near_cos[...] + far_cos[step] * near_sin[...]
        high = (cos.astype(BF16), sin.astype(BF16))
        low = tuple((value - top.astype(F32)).astype(BF16) for value, top in zip((cos, sin), high))
        for term, pair in enumerate((high, low)):
            for which, value in enumerate(pair):
                if interleaved:
                    row = term * count + step * near
                    for block in range(lanes // size):
                        lane = (2 * block + which) * size
                        space[row : row + near, lane : lane + size] = value[:, block * size : (block + 1) * size]
                else:
                    row = (2 * term + which) * count + step * near
                    space[row : row + near, :] = value
    copies.append(pltpu.make_async_copy(space, out, sems.at[1]))
    copies[1].start()
    for copy in copies:
        copy.wait()


def wave_table(rows, columns, length, interleaved, named, wave_slots):
    near = 32
    near_cos, near_sin = phases(np.arange(near), np.arange(columns), length)
    far_cos, far_sin = phases(np.arange(rows // near) * near, np.arange(columns), length)
    scaling = 1.0 / math.sqrt(length)
    shape = (2 * rows, 2 * columns) if interleaved else (4 * rows, columns)
    waves, slots = wave_slots.shape[0], named.shape[0]
    hot_shape = (slots, waves) if interleaved else (waves, slots)
    return pl.pallas_call(
        functools.partial(table_kernel, interleaved),
        out_specs=[pl.BlockSpec(memory_space=pltpu.HBM)] * 2,
        out_shape=[jax.ShapeDtypeStruct(shape, BF16), jax.ShapeDtypeStruct(hot_shape, BF16)],
        scratch_shapes=[pltpu.VMEM(shape, BF16), pltpu.VMEM(hot_shape, BF16), pltpu.SemaphoreType.DMA((2,))],
        compiler_params=pltpu.CompilerParams(vmem_limit_bytes=WHOLE_LIMIT),
        name="wave_table",
    )(
        jnp.asarray(near_cos * scaling, F32),
        jnp.asarray(near_sin * scaling, F32),
        jnp.asarray(far_cos[:, None, :], F32),
        jnp.asarray(far_sin[:, None, :], F32),
        named[:, None] if interleaved else named[None, :],
        wave_slots[None, :],
    )


def sector_turns(sectors, waves):
    both = phases(np.arange(sectors), np.arange(waves), sectors)
    return tuple(jnp.asarray(np.round(turn, 12)[:, None, :], F32) for turn in both)


def chunk_widths(lat_rows):
    main = lat_rows // LANES * LANES
    return (main, lat_rows - main) if main and 2 * (lat_rows - main) == LANES else (lat_rows,)


def chunk_start(widths, chunk, near):
    if len(widths) == 1:
        return 0
    odd = near % 2
    return odd * widths[1] if chunk == 0 else (1 - odd) * widths[0]


def band_place(owner_index, owners):
    south = owner_index >= owners // 2
    return south, jnp.where(south, owners - 1 - owner_index, owner_index)


def product_kernel(masks, widths, wind_u, wind_v, *refs):
    outs, (space, sems) = refs[:-2], refs[-2:]
    _, lat_rows, columns = wind_u.shape
    south, near = band_place(lax.axis_index("lat"), lax.axis_size("lat"))
    pieces = sems.shape[2]
    size = columns // pieces
    copies = {}
    for i, mask in enumerate(masks):
        level = lax.axis_index("lon") ^ mask
        for piece in range(pieces):
            own = pl.ds(piece * size, size)
            for which, wind in enumerate((wind_u, wind_v)):
                copy = pltpu.make_async_copy(
                    wind.at[level, :, own], space.at[i, which, :, own], sems.at[i, which, piece]
                )
                copy.start()
                copies[i, piece, which] = copy
    chosen = []
    for chunk, width in enumerate(widths):
        start = chunk_start(widths, chunk, near)
        ids = start + lax.broadcasted_iota(jnp.int32, (width, lat_rows), 0)
        lats = lax.broadcasted_iota(jnp.int32, (width, lat_rows), 1)
        chosen.append((lats == jnp.where(south, lat_rows - 1 - ids, ids)).astype(F32).astype(BF16))
    for i in range(len(masks)):
        for piece in range(pieces):
            own = pl.ds(piece * size, size)
            copies[i, piece, 0].wait()
            copies[i, piece, 1].wait()
            u, v = space[i, 0, :, own], space[i, 1, :, own]
            for field, product in enumerate((u * v, u * u - v * v)):
                product = product.astype(BF16)
                for chunk, width in enumerate(widths):
                    outs[i * len(widths) + chunk][field * width : (field + 1) * width, own] = dot(
                        chosen[chunk], product
                    ).astype(BF16)


def wind_products(wind_u, wind_v, masks, widths):
    _, lat_rows, columns = wind_u.shape
    hbm, vmem = pl.BlockSpec(memory_space=pl.ANY), pl.BlockSpec(memory_space=pltpu.VMEM)
    outs = pl.pallas_call(
        functools.partial(product_kernel, masks, widths),
        in_specs=[hbm, hbm],
        out_specs=[vmem] * (len(masks) * len(widths)),
        out_shape=[jax.ShapeDtypeStruct((2 * width, columns), BF16) for _ in masks for width in widths],
        scratch_shapes=[
            pltpu.VMEM((len(masks), 2, lat_rows, columns), F32),
            pltpu.SemaphoreType.DMA((len(masks), 2, 1)),
        ],
        compiler_params=pltpu.CompilerParams(vmem_limit_bytes=WHOLE_LIMIT),
        name="wind_products",
    )(wind_u, wind_v)
    return {
        (chunk, mask): outs[i * len(widths) + chunk] for i, mask in enumerate(masks) for chunk in range(len(widths))
    }


def forward_kernel(count, begun, ends, *refs):
    lines, refs = refs[:count], refs[count:]
    table, turn_cos, turn_sin = refs[:3]
    earlier, refs = (refs[3], refs[4:]) if begun else (None, refs[3:])
    step = pl.program_id(0)
    size = table.shape[1] // 2
    rows = lines[0].shape[0]
    both = jnp.concatenate([jnp.concatenate([line[...]] * 2, axis=1) for line in lines], axis=0)
    sums = dot(both, table[...])
    real, imag = (earlier[0], earlier[1]) if begun else (None, None)
    for i in range(count):
        own = sums[i * rows : (i + 1) * rows]
        own_cos, own_sin = own[:, :size], own[:, size:]
        cos, sin = turn_cos[i], turn_sin[i]
        own_real, own_imag = own_cos * cos - own_sin * sin, own_cos * sin + own_sin * cos
        real, imag = (own_real, own_imag) if real is None else (real + own_real, imag + own_imag)
    if not ends:
        refs[0][0], refs[0][1] = real, imag
        return
    one_hot, out, by_wave, by_slot, wire, sems = refs
    devices, wire_rows, lanes = out.shape
    padded = one_hot.shape[0] // devices
    blocks = 2 * rows // lanes
    share = wire_rows // blocks
    place = pl.ds(pl.multiple_of(step * size, size), size)
    by_wave[0, :, place] = real.astype(BF16)
    by_wave[1, :, place] = (-imag).astype(BF16)

    @pl.when(step == pl.num_programs(0) - 1)
    def _():
        for part in range(2):
            by_slot[:, part * rows : (part + 1) * rows] = dot(one_hot[...], by_wave[part], NT)
        copies, out_step = [], devices // sems.shape[0]
        for device in range(devices):
            own = by_slot[device * padded : (device + 1) * padded, :]
            wire[device] = pack_rows(
                [own[:share, block * lanes : (block + 1) * lanes] for block in range(blocks)]
            ).astype(BF16)
            if (device + 1) % out_step == 0:
                piece = pl.ds(device + 1 - out_step, out_step)
                copies.append(pltpu.make_async_copy(wire.at[piece], out.at[piece], sems.at[device // out_step]))
                copies[-1].start()
        for copy in copies:
            copy.wait()


def forward(lines, table, turns, earlier=None, end=None):
    rows, columns = lines[0].shape
    waves = table.shape[1] // 2
    size = min(LANES, waves)
    turn_spec = pl.BlockSpec((len(lines), 1, size), lambda i: (0, 0, i))
    sum_spec = pl.BlockSpec((2, rows, size), lambda i: (0, 0, i))
    args = list(lines) + [table, *turns]
    in_specs = [pl.BlockSpec((rows, columns), lambda i: (0, 0))] * len(lines)
    in_specs += [pl.BlockSpec((2 * columns, 2 * size), lambda i: (0, i)), turn_spec, turn_spec]
    if earlier is not None:
        args.append(earlier)
        in_specs.append(sum_spec)
    if end is None:
        out_shape, out_spec, scratch = jax.ShapeDtypeStruct((2, rows, waves), F32), sum_spec, []
    else:
        one_hot, share = end
        slots = one_hot.shape[0]
        lanes = wire_lanes(rows)
        out = (slots // round_up(share, 8), share * (2 * rows // lanes), lanes)
        args.append(one_hot)
        in_specs.append(pl.BlockSpec((slots, waves), lambda i: (0, 0)))
        out_shape, out_spec = jax.ShapeDtypeStruct(out, BF16), pl.BlockSpec(memory_space=pltpu.HBM)
        scratch = [pltpu.VMEM((2, rows, waves), BF16), pltpu.VMEM((slots, 2 * rows), F32)]
        scratch += [pltpu.VMEM(out, BF16), pltpu.SemaphoreType.DMA((4,))]
    return pl.pallas_call(
        functools.partial(forward_kernel, len(lines), earlier is not None, end is not None),
        grid=(waves // size,),
        in_specs=in_specs,
        out_specs=out_spec,
        out_shape=out_shape,
        scratch_shapes=scratch,
        cost_estimate=pl.CostEstimate(
            flops=8 * len(lines) * rows * columns * waves, bytes_accessed=10**7, transcendentals=0
        ),
        compiler_params=pltpu.CompilerParams(vmem_limit_bytes=VMEM_LIMIT),
        name="forward",
    )(*args)


def sector_lines(exact, by_wave, table, turn_cos, turn_sin):
    count = turn_cos.shape[0]
    left = []
    for i in range(count):
        cos, sin = turn_cos[i], turn_sin[i]
        own_real, own_imag = by_wave[0].astype(F32), by_wave[1].astype(F32)
        real = own_real * cos - own_imag * sin
        minus = -(own_real * sin) - own_imag * cos
        left.append(jnp.concatenate([real, minus], axis=1))
    left = jnp.concatenate(left, axis=0) if count > 1 else left[0]
    high = left.astype(BF16)
    total = dot(jnp.concatenate([high, high], axis=1), table[...])
    if not exact:
        low = (left - high.astype(F32)).astype(BF16)
        total += dot(low, table[: low.shape[1]])
    return total.astype(BF16)


def backward_first_kernel(
    exact, wire, table_hbm, turn_cos, turn_sin, one_hot_hbm, mirror, out, by_wave_out, by_slot, table, one_hot, by_wave, sems
):
    one_hot_copy = pltpu.make_async_copy(one_hot_hbm, one_hot, sems.at[0])
    table_copy = pltpu.make_async_copy(table_hbm, table, sems.at[1])
    by_wave_copy = pltpu.make_async_copy(by_wave, by_wave_out, sems.at[2])
    one_hot_copy.start()
    table_copy.start()
    devices, _, lanes = wire.shape
    rows = out.shape[0]
    waves = one_hot.shape[0]
    width = mirror.shape[0]
    padded = by_slot.shape[0] // devices
    blocks = 2 * rows // lanes
    for device in range(devices):
        for block, piece in enumerate(unpack_rows(wire[device].astype(F32), blocks, padded)):
            by_slot[device * padded : (device + 1) * padded, block * lanes : (block + 1) * lanes] = piece.astype(BF16)
    one_hot_copy.wait()
    wave_ids = lax.broadcasted_iota(jnp.int32, (1, waves), 1)
    weight = jnp.where(wave_ids == 0, 1.0, 2.0).astype(F32)
    for part in range(2):
        ordered = dot(one_hot[...], by_slot[:, part * rows : (part + 1) * rows]).astype(BF16)
        for field in range(2):
            own = slice(field * width, (field + 1) * width)
            by_wave[part, own, :] = (dot(mirror[...], ordered[:, own], NT) * weight).astype(BF16)
    by_wave_copy.start()
    table_copy.wait()
    out[...] = sector_lines(exact, by_wave, table, turn_cos, turn_sin)
    by_wave_copy.wait()


def backward_first(wire, table, turns, one_hot, mirror, exact):
    rows = 2 * mirror.shape[0]
    waves, slots = one_hot.shape
    vmem, hbm = pl.BlockSpec(memory_space=pltpu.VMEM), pl.BlockSpec(memory_space=pl.ANY)
    return pl.pallas_call(
        functools.partial(backward_first_kernel, exact),
        in_specs=[vmem, hbm, vmem, vmem, hbm, vmem],
        out_specs=[vmem, pl.BlockSpec(memory_space=pltpu.HBM)],
        out_shape=[
            jax.ShapeDtypeStruct((rows, table.shape[1]), BF16),
            jax.ShapeDtypeStruct((2, rows, waves), BF16),
        ],
        scratch_shapes=[
            pltpu.VMEM((slots, 2 * rows), BF16),
            pltpu.VMEM(table.shape, BF16),
            pltpu.VMEM(one_hot.shape, BF16),
            pltpu.VMEM((2, rows, waves), BF16),
            pltpu.SemaphoreType.DMA((3,)),
        ],
        cost_estimate=pl.CostEstimate(flops=10**9, bytes_accessed=10**7, transcendentals=0),
        compiler_params=pltpu.CompilerParams(vmem_limit_bytes=VMEM_LIMIT),
        name="backward_first",
    )(wire, table, *turns, one_hot, mirror)


def backward_rest_kernel(exact, by_wave, table, turn_cos, turn_sin, *outs):
    rows = outs[0].shape[0]
    total = sector_lines(exact, by_wave, table, turn_cos, turn_sin)
    for i, out in enumerate(outs):
        out[...] = total[i * rows : (i + 1) * rows]


def backward_rest(by_wave, table, turns, exact):
    _, rows, _ = by_wave.shape
    count = turns[0].shape[0]
    vmem = pl.BlockSpec(memory_space=pltpu.VMEM)
    return pl.pallas_call(
        functools.partial(backward_rest_kernel, exact),
        in_specs=[vmem] * 4,
        out_specs=[vmem] * count,
        out_shape=[jax.ShapeDtypeStruct((rows, table.shape[1]), BF16)] * count,
        cost_estimate=pl.CostEstimate(flops=3 * 10**9, bytes_accessed=10**7, transcendentals=0),
        compiler_params=pltpu.CompilerParams(vmem_limit_bytes=VMEM_LIMIT),
        name="backward_rest",
    )(by_wave, table, *turns)


def placing_kernel(parts, widths, *refs):
    blocks, (out, wide, sems) = refs[: len(parts)], refs[-3:]
    _, rows, _ = out.shape
    lat_rows = rows // 2
    south, near = band_place(lax.axis_index("lat"), lax.axis_size("lat"))
    copies = []
    for i, (chunk, mask) in enumerate(parts):
        width = widths[chunk]
        start = chunk_start(widths, chunk, near)
        start = jnp.where(south, lat_rows - start - width, start)
        level = lax.axis_index("lon") ^ mask
        for field in range(2):
            own = slice(field * width, (field + 1) * width)
            wide[i, own] = blocks[i][own].astype(F32)
            place = pl.ds(pl.multiple_of(field * lat_rows + start, math.gcd(*widths, lat_rows)), width)
            copies.append(pltpu.make_async_copy(wide.at[i, own], out.at[level, place], sems.at[i, field]))
            copies[-1].start()
    for copy in copies:
        copy.wait()


def placed(blocks, parts, widths, shape, earlier=None):
    count = len(parts)
    vmem, hbm = pl.BlockSpec(memory_space=pltpu.VMEM), pl.BlockSpec(memory_space=pl.ANY)
    more = () if earlier is None else (earlier,)
    return pl.pallas_call(
        functools.partial(placing_kernel, parts, widths),
        in_specs=[vmem] * count + [hbm] * len(more),
        out_specs=hbm,
        out_shape=jax.ShapeDtypeStruct(shape, F32),
        scratch_shapes=[
            pltpu.VMEM((count, 2 * max(widths[chunk] for chunk, _ in parts), shape[2]), F32),
            pltpu.SemaphoreType.DMA((count, 2)),
        ],
        input_output_aliases={count: 0} if more else {},
        compiler_params=pltpu.CompilerParams(vmem_limit_bytes=VMEM_LIMIT),
        name="placed",
    )(*[blocks[part] for part in parts], *more)


def round_up(value, unit):
    return -(-value // unit) * unit


def pack_rows(pieces):
    share = pieces[0].shape[0]
    main = share // 8 * 8
    parts = [piece[:main] for piece in pieces] if main else []
    parts += [piece[main:] for piece in pieces] if main < share else []
    return jnp.concatenate(parts, axis=0) if len(parts) > 1 else parts[0]


def unpack_rows(value, count, fill):
    share = value.shape[0] // count
    main = share // 8 * 8
    rest = share - main
    pieces = []
    for i in range(count):
        parts = [value[i * main : (i + 1) * main]] if main else []
        parts += [value[count * main + i * rest : count * main + (i + 1) * rest]] if rest else []
        parts += [jnp.zeros((fill - share, value.shape[1]), value.dtype)] if fill > share else []
        pieces.append(jnp.concatenate(parts, axis=0) if len(parts) > 1 else parts[0])
    return pieces


def wire_lanes(rows):
    return LANES if 2 * rows % LANES == 0 else 2 * rows


def legendre_kernel(sides, widths_in, widths, group, place, order, blocks, damping, basis, *rest):
    wires = len(widths)
    received, rest = rest[: len(widths_in)], rest[len(widths_in) :]
    spectral_out, returned_out, rest = rest[0], rest[1 : 1 + wires], rest[1 + wires :]
    spectral, returned, (held, buffer, sems, out_sems, spectral_sem) = rest[0], rest[1 : 1 + wires], rest[1 + wires :]
    lat_rows = sum(widths)
    devices = received[0].shape[0]
    sectors, share = spectral.shape[:2]
    slots, degrees, half_lat = basis.shape
    sources = devices // sectors
    fields = sides // 2
    combos = sectors * sides
    lane_blocks = held.shape[0]
    stride = held.shape[1] // (2 * combos)
    groups = share // group
    most = degrees // STEP
    scale = 1.0 / math.sqrt(degrees)
    out_step = devices // out_sems.shape[1]

    def copies(index, count):
        ring = lax.rem(index, DEPTH)
        rows = pl.ds(0, count * STEP)
        return [
            pltpu.make_async_copy(
                basis.at[jnp.minimum(place[0] + order[index * group + i], slots - 1), rows, :],
                buffer.at[ring, i, rows, :],
                sems.at[ring, i],
            )
            for i in range(group)
        ]

    def fetch(index):
        for count in range(1, most + 1):

            @pl.when(blocks[index] == count)
            def _():
                for copy in copies(index, count):
                    copy.start()

    for index in range(min(DEPTH - 1, groups)):
        fetch(index)

    def wire_pieces(kinds, wire, device, wire_block):
        source, sector = divmod(device, sectors)
        side, near = (0, source) if source < sources // 2 else (1, sources - 1 - source)
        chunk_width = kinds[wire]
        lanes = wire_lanes(fields * chunk_width)
        begin = near * lat_rows + chunk_start(kinds, wire, near)
        column, end = wire_block * lanes, (wire_block + 1) * lanes
        while column < end:
            part_field, lat = divmod(column, chunk_width)
            part, field = divmod(part_field, fields)
            row = (side * combos + sector * sides + field * 2 + part) * stride
            at = begin + lat
            width = min(end - column, chunk_width - lat, LANES - at % LANES)
            yield column - wire_block * lanes, width, row, at // LANES, at % LANES
            column += width

    for wire in range(len(widths_in)):
        wire_blocks = received[wire].shape[1] // share
        for device in range(devices):
            own_blocks = unpack_rows(received[wire][device].astype(F32), wire_blocks, stride)
            for wire_block, piece in enumerate(own_blocks):
                for at, width, row, block, lane in wire_pieces(widths_in, wire, device, wire_block):
                    held[block, row : row + stride, lane : lane + width] = piece[:, at : at + width]

    def load_slot(slot):
        rows = pl.ds(slot, 2 * combos, stride=stride)
        return jnp.concatenate([held[block, rows, :] for block in range(lane_blocks)], axis=1)

    def store_slot(slot, value):
        rows = pl.ds(slot, 2 * combos, stride=stride)
        for block in range(lane_blocks):
            held[block, rows, :] = value[:, block * LANES : (block + 1) * LANES]

    def one_group(index, count):
        ring = lax.rem(index, DEPTH)
        here = [order[index * group + i] for i in range(group)]
        if count == 0:
            for slot in here:
                for sector in range(sectors):
                    spectral[place[1] ^ sector, slot] = jnp.zeros(spectral.shape[2:], F32)
                store_slot(slot, jnp.zeros((2 * combos, half_lat), F32))
            return
        width = count * STEP
        for copy in copies(index, count):
            copy.wait()
        parity = 1.0 - 2.0 * (lax.broadcasted_iota(jnp.int32, (1, width), 1) % 2).astype(F32)
        left = [load_slot(slot).astype(BF16) for slot in here]
        sums = [dot(left[i], buffer[ring, i, :width, :], NT) for i in range(group)]
        damped = [
            (sums[i][:combos] + parity * sums[i][combos:]) * damping[slot, :, :width] for i, slot in enumerate(here)
        ]
        turned = [jnp.concatenate([value, parity * value], axis=0).astype(BF16) for value in damped]
        backs = [dot(turned[i], buffer[ring, i, :width, :]) * scale for i in range(group)]
        for i, slot in enumerate(here):
            for sector in range(sectors):
                spectral[place[1] ^ sector, slot, :, :width] = damped[i][sector * sides : (sector + 1) * sides]
                if width < degrees:
                    spectral[place[1] ^ sector, slot, :, width:] = jnp.zeros((sides, degrees - width), F32)
        for i, slot in enumerate(here):
            store_slot(slot, backs[i])

    def loop_body(index, carry):
        @pl.when(index + DEPTH - 1 < groups)
        def _():
            fetch(index + DEPTH - 1)

        for count in range(most + 1):
            pl.when(blocks[index] == count)(functools.partial(one_group, index, count))
        return carry

    lax.fori_loop(0, groups, loop_body, 0)

    spectral_copy = pltpu.make_async_copy(spectral, spectral_out, spectral_sem)
    spectral_copy.start()
    out_copies = []
    for wire in range(wires):
        wire_blocks = returned[wire].shape[1] // share
        for device in range(devices):
            pieces = []
            for wire_block in range(wire_blocks):
                parts = [
                    held[block, row : row + share, lane : lane + width]
                    for _, width, row, block, lane in wire_pieces(widths, wire, device, wire_block)
                ]
                pieces.append(jnp.concatenate(parts, axis=1) if len(parts) > 1 else parts[0])
            returned[wire][device] = pack_rows(pieces).astype(BF16)
            if (device + 1) % out_step == 0:
                part = pl.ds(device + 1 - out_step, out_step)
                copy = pltpu.make_async_copy(
                    returned[wire].at[part], returned_out[wire].at[part], out_sems.at[wire, device // out_step]
                )
                copy.start()
                out_copies.append(copy)
    for copy in (*out_copies, spectral_copy):
        copy.wait()


def legendre(received, basis, damping, place, order, blocks, sectors, sides, widths_in, widths, group):
    share = order.shape[0]
    devices = received[0].shape[0]
    returned = []
    for width in widths:
        lanes = wire_lanes(2 * width)
        returned.append((devices, share * (4 * width // lanes), lanes))
    degrees, half_lat = basis.shape[1:]
    combos = sectors * sides
    smem, vmem, hbm = (pl.BlockSpec(memory_space=space) for space in (pltpu.SMEM, pltpu.VMEM, pl.ANY))
    return pl.pallas_call(
        functools.partial(legendre_kernel, sides, widths_in, widths, group),
        in_specs=[smem, smem, smem, vmem, hbm] + [vmem] * len(widths_in),
        out_specs=[pl.BlockSpec(memory_space=pltpu.HBM)] * (1 + len(widths)),
        out_shape=[
            jax.ShapeDtypeStruct((sectors, share, sides, degrees), F32),
            *[jax.ShapeDtypeStruct(wire, BF16) for wire in returned],
        ],
        scratch_shapes=[
            pltpu.VMEM((sectors, share, sides, degrees), F32),
            *[pltpu.VMEM(wire, BF16) for wire in returned],
            pltpu.VMEM((half_lat // LANES, 2 * combos * round_up(share, 8), LANES), F32),
            pltpu.VMEM((DEPTH, group, degrees, half_lat), BF16),
            pltpu.SemaphoreType.DMA((DEPTH, group)),
            pltpu.SemaphoreType.DMA((len(widths), 8)),
            pltpu.SemaphoreType.DMA,
        ],
        cost_estimate=pl.CostEstimate(
            flops=4 * share * degrees * half_lat * 2 * combos,
            bytes_accessed=2 * share * degrees * half_lat,
            transcendentals=0,
        ),
        compiler_params=pltpu.CompilerParams(vmem_limit_bytes=LEGENDRE_LIMIT),
        name="legendre",
    )(place, order, blocks, damping, basis, *received)


def degree_order(counts):
    size = counts.shape[0]
    ids = jnp.arange(size, dtype=jnp.int32)
    ahead = (counts[None, :] > counts[:, None]) | ((counts[None, :] == counts[:, None]) & (ids[None, :] < ids[:, None]))
    rank = jnp.sum(ahead.astype(jnp.int32), axis=1)
    placed = rank[:, None] == ids[None, :]
    order = jnp.sum(jnp.where(placed, ids[:, None], 0), axis=0)
    sorted_counts = jnp.sum(jnp.where(placed, counts[:, None], 0), axis=0)
    group = max(g for g in range(1, 6) if size % g == 0)
    return order, (sorted_counts[::group] + (STEP - 1)) // STEP, group


def body(wind_u, wind_v, basis, wave_slots, degree_count, viscosity):
    sectors = lax.axis_size("lon")
    owners = lax.axis_size("lat")
    sector_index = lax.axis_index("lon")
    owner_index = lax.axis_index("lat")
    levels, lat_rows, lon_cols = wind_u.shape
    capacity, degrees, half_lat = basis.shape
    waves = wave_slots.shape[0]
    assert levels == sectors and sectors & (sectors - 1) == 0
    rows = 2 * lat_rows
    share = -(-capacity // sectors)
    padded = round_up(share, 8)
    length = sectors * lon_cols
    masks = [sectors // 2] + [mask for mask in range(sectors - 1, 0, -1) if mask != sectors // 2] + [0]

    def across(value, mask):
        return lax.ppermute(value, "lon", [(i, i ^ mask) for i in range(sectors)]) if mask else value

    def partners(some):
        return jnp.stack([sector_index ^ mask for mask in some]).astype(jnp.int32)

    far, rest = masks[:1], masks[1:]
    whole, widths = (lat_rows,), chunk_widths(lat_rows)
    small_first = [0]

    first_made = wind_products(wind_u, wind_v, far, whole)
    lines = {}
    for chunk in small_first[:1]:
        for mask in far:
            lines[chunk, mask] = across(first_made[chunk, mask], mask)
    made = {**first_made, **wind_products(wind_u, wind_v, rest, whole)}
    for chunk in small_first:
        for mask in masks:
            if (chunk, mask) not in lines:
                lines[chunk, mask] = across(made[chunk, mask], mask)

    wave_ids = jnp.arange(waves, dtype=jnp.int32)
    places = jnp.arange(owners * sectors * padded, dtype=jnp.int32)
    place_owner, place_sector, place_slot = places // (sectors * padded), places // padded % sectors, places % padded
    in_owner = place_sector * share + place_slot
    named = jnp.where((place_slot < share) & (in_owner < capacity), place_owner * capacity + in_owner, -1)
    forward_table, one_hot = wave_table(lon_cols, waves, length, True, named, wave_slots)
    backward_table, one_hot_turned = wave_table(waves, lon_cols, length, False, named, wave_slots)
    backward_table, one_hot_turned = (
        pltpu.with_memory_space_constraint(value, pltpu.HBM) for value in (backward_table, one_hot_turned)
    )
    turns = sector_turns(sectors, waves)

    def turns_of(some):
        at = partners(some)
        return tuple(jnp.take(turn, at, axis=0) for turn in turns)

    first = sector_index * share
    local_ids = jnp.arange(share, dtype=jnp.int32)
    inside = first + local_ids < capacity
    at = owner_index * capacity + jnp.minimum(first + local_ids, capacity - 1)
    here = at[:, None] == wave_slots[None, :]
    wave_here = jnp.sum(jnp.where(here, wave_ids[None, :], 0), axis=1)
    count_here = jnp.where(inside, jnp.sum(jnp.where(here, degree_count[None, :], 0), axis=1), 0)
    degree_ids = jnp.arange(degrees, dtype=jnp.int32)
    total_degree = wave_here[:, None] + degree_ids[None, :]
    scaled = (total_degree * (total_degree + 1)).astype(F32) / float(degrees * (degrees + 1))
    kept = degree_ids[None, :] < count_here[:, None]
    sides = 4
    rates = jnp.repeat(viscosity, sides)
    damping = 1.0 / (1.0 + rates[None, :, None] * (scaled * scaled)[:, None, :])
    damping = jnp.where(kept[:, None, :], damping * (1.0 / math.sqrt(2 * half_lat)), 0.0)
    order, blocks, group = degree_order(count_here)

    by_arrival = list(dict.fromkeys([0, *[mask for mask in reversed(masks) if mask < sectors // 2], *masks]))
    early, late = by_arrival[:-1], by_arrival[-1:]
    received = [None]
    for chunk in small_first:
        own = {mask: lines[chunk, mask] for mask in masks}
        if chunk == 0:
            sums = forward([own[mask] for mask in early], forward_table, turns_of(early))
            fourier = forward([own[mask] for mask in late], forward_table, turns_of(late), sums, (one_hot, share))
        else:
            fourier = forward([own[mask] for mask in by_arrival], forward_table, turns_of(by_arrival), None, (one_hot, share))
        received[chunk] = lax.all_to_all(fourier, ("lat", "lon"), split_axis=0, concat_axis=0, tiled=True)
    place = jnp.stack([first, sector_index]).astype(jnp.int32)
    spectral, *returned = legendre(
        received, basis, damping, place, order, blocks, sectors, sides, whole, widths, group
    )

    exact = sectors in (1, 2, 4)
    far_turns, rest_turns = turns_of(far), turns_of(rest)
    south, _ = band_place(owner_index, owners)
    back, regrouped = {}, []
    for chunk, wire in enumerate(returned):
        if chunk:
            wire, regrouped[-1] = lax.optimization_barrier((wire, regrouped[-1]))
        regrouped.append(lax.all_to_all(wire, ("lat", "lon"), split_axis=0, concat_axis=0, tiled=True))
    for chunk, width in enumerate(widths):
        ids = jnp.arange(width, dtype=jnp.int32)
        mirror = (ids[:, None] == jnp.where(south, width - 1 - ids, ids)[None, :]).astype(BF16)
        far_lines, by_wave = backward_first(regrouped[chunk], backward_table, far_turns, one_hot_turned, mirror, exact)
        back[chunk, far[0]] = across(far_lines, far[0])
        others = backward_rest(by_wave, backward_table, rest_turns, exact)
        for mask, value in zip(rest, others):
            back[chunk, mask] = across(value, mask)

    coefficients = jnp.zeros((sectors * share, 1, 2, 2, degrees), F32)
    for mask in masks:
        own = across(spectral[mask].astype(BF16), mask).astype(F32).reshape(share, 1, 2, 2, degrees)
        coefficients = lax.dynamic_update_slice_in_dim(coefficients, own, (sector_index ^ mask) * share, 0)

    arrival = [(chunk, mask) for chunk in range(len(widths)) for mask in by_arrival]
    cuts = [0, len(early), len(arrival) - 1, len(arrival)]
    tendency = None
    for begin, end in zip(cuts, cuts[1:]):
        if end > begin:
            tendency = placed(back, arrival[begin:end], widths, (sectors, rows, lon_cols), tendency)
    return coefficients[:capacity], tendency.reshape(levels, 2, lat_rows, lon_cols)


def solution(mesh):
    return jax.shard_map(
        body,
        mesh=mesh,
        in_specs=(
            P(None, "lat", "lon"),
            P(None, "lat", "lon"),
            P("lat", None, None),
            P(),
            P(),
            P(),
        ),
        out_specs=(P("lat", "lon", None, None, None), P(None, None, "lat", "lon")),
        check_vma=False,
    )
```

```python
import functools
import math

import jax
import jax.numpy as jnp
import numpy as np
from jax import lax
from jax.experimental import pallas as pl
from jax.experimental.pallas import tpu as pltpu
from jax.sharding import PartitionSpec as P


BF16 = jnp.bfloat16
F32 = jnp.float32
MIB = 1024 * 1024
VMEM_LIMIT = 24 * MIB
LEGENDRE_LIMIT = 36 * MIB
WHOLE_LIMIT = 60 * MIB
STEP = 128
LANES = 128
DEPTH = 3
NT = (((1,), (1,)), ((), ()))
NN = (((1,), (0,)), ((), ()))


def dot(a, b, dims=NN):
    return lax.dot_general(a, b, dims, preferred_element_type=F32)


def phases(rows, columns, length):
    turns = 2.0 * np.pi * (rows[:, None] * columns[None, :] % length) / length
    return np.cos(turns), np.sin(turns)


def table_kernel(interleaved, near_cos, near_sin, far_cos, far_sin, named, wave_slots, out, hot_out, space, hot, sems):
    near, lanes = near_cos.shape
    steps = far_cos.shape[0]
    count = steps * near
    size = min(LANES, lanes)
    if interleaved:
        hot[...] = (named[...] == wave_slots[...]).astype(F32).astype(BF16)
    else:
        slots_down = jnp.broadcast_to(wave_slots[...].astype(F32), (8, wave_slots.shape[1])).T[:, :1]
        hot[...] = (slots_down == named[...].astype(F32)).astype(F32).astype(BF16)
    copies = [pltpu.make_async_copy(hot, hot_out, sems.at[0])]
    copies[0].start()
    for step in range(steps):
        cos = far_cos[step] * near_cos[...] - far_sin[step] * near_sin[...]
        sin = far_sin[step] * near_cos[...] + far_cos[step] * near_sin[...]
        high = (cos.astype(BF16), sin.astype(BF16))
        low = tuple((value - top.astype(F32)).astype(BF16) for value, top in zip((cos, sin), high))
        for term, pair in enumerate((high, low)):
            for which, value in enumerate(pair):
                if interleaved:
                    row = term * count + step * near
                    for block in range(lanes // size):
                        lane = (2 * block + which) * size
                        space[row : row + near, lane : lane + size] = value[:, block * size : (block + 1) * size]
                else:
                    row = (2 * term + which) * count + step * near
                    space[row : row + near, :] = value
    copies.append(pltpu.make_async_copy(space, out, sems.at[1]))
    copies[1].start()
    for copy in copies:
        copy.wait()


def wave_table(rows, columns, length, interleaved, named, wave_slots):
    near = 32
    near_cos, near_sin = phases(np.arange(near), np.arange(columns), length)
    far_cos, far_sin = phases(np.arange(rows // near) * near, np.arange(columns), length)
    scaling = 1.0 / math.sqrt(length)
    shape = (2 * rows, 2 * columns) if interleaved else (4 * rows, columns)
    waves, slots = wave_slots.shape[0], named.shape[0]
    hot_shape = (slots, waves) if interleaved else (waves, slots)
    return pl.pallas_call(
        functools.partial(table_kernel, interleaved),
        out_specs=[pl.BlockSpec(memory_space=pltpu.HBM)] * 2,
        out_shape=[jax.ShapeDtypeStruct(shape, BF16), jax.ShapeDtypeStruct(hot_shape, BF16)],
        scratch_shapes=[pltpu.VMEM(shape, BF16), pltpu.VMEM(hot_shape, BF16), pltpu.SemaphoreType.DMA((2,))],
        compiler_params=pltpu.CompilerParams(vmem_limit_bytes=WHOLE_LIMIT),
        name="wave_table",
    )(
        jnp.asarray(near_cos * scaling, F32),
        jnp.asarray(near_sin * scaling, F32),
        jnp.asarray(far_cos[:, None, :], F32),
        jnp.asarray(far_sin[:, None, :], F32),
        named[:, None] if interleaved else named[None, :],
        wave_slots[None, :],
    )


def sector_turns(sectors, waves):
    both = phases(np.arange(sectors), np.arange(waves), sectors)
    return tuple(jnp.asarray(np.round(turn, 12)[:, None, :], F32) for turn in both)


def chunk_widths(lat_rows):
    main = lat_rows // LANES * LANES
    return (main, lat_rows - main) if main and 2 * (lat_rows - main) == LANES else (lat_rows,)


def chunk_start(widths, chunk, near):
    if len(widths) == 1:
        return 0
    odd = near % 2
    return odd * widths[1] if chunk == 0 else (1 - odd) * widths[0]


def band_place(owner_index, owners):
    south = owner_index >= owners // 2
    return south, jnp.where(south, owners - 1 - owner_index, owner_index)


def product_kernel(masks, widths, wind_u, wind_v, *refs):
    outs, (space, sems) = refs[:-2], refs[-2:]
    _, lat_rows, columns = wind_u.shape
    south, near = band_place(lax.axis_index("lat"), lax.axis_size("lat"))
    pieces = sems.shape[2]
    size = columns // pieces
    copies = {}
    for i, mask in enumerate(masks):
        level = lax.axis_index("lon") ^ mask
        for piece in range(pieces):
            own = pl.ds(piece * size, size)
            for which, wind in enumerate((wind_u, wind_v)):
                copy = pltpu.make_async_copy(
                    wind.at[level, :, own], space.at[i, which, :, own], sems.at[i, which, piece]
                )
                copy.start()
                copies[i, piece, which] = copy
    chosen = []
    for chunk, width in enumerate(widths):
        start = chunk_start(widths, chunk, near)
        ids = start + lax.broadcasted_iota(jnp.int32, (width, lat_rows), 0)
        lats = lax.broadcasted_iota(jnp.int32, (width, lat_rows), 1)
        chosen.append((lats == jnp.where(south, lat_rows - 1 - ids, ids)).astype(F32).astype(BF16))
    for i in range(len(masks)):
        for piece in range(pieces):
            own = pl.ds(piece * size, size)
            copies[i, piece, 0].wait()
            copies[i, piece, 1].wait()
            u, v = space[i, 0, :, own], space[i, 1, :, own]
            for field, product in enumerate((u * v, u * u - v * v)):
                product = product.astype(BF16)
                for chunk, width in enumerate(widths):
                    outs[i * len(widths) + chunk][field * width : (field + 1) * width, own] = dot(
                        chosen[chunk], product
                    ).astype(BF16)


def wind_products(wind_u, wind_v, masks, widths):
    _, lat_rows, columns = wind_u.shape
    hbm, vmem = pl.BlockSpec(memory_space=pl.ANY), pl.BlockSpec(memory_space=pltpu.VMEM)
    outs = pl.pallas_call(
        functools.partial(product_kernel, masks, widths),
        in_specs=[hbm, hbm],
        out_specs=[vmem] * (len(masks) * len(widths)),
        out_shape=[jax.ShapeDtypeStruct((2 * width, columns), BF16) for _ in masks for width in widths],
        scratch_shapes=[
            pltpu.VMEM((len(masks), 2, lat_rows, columns), F32),
            pltpu.SemaphoreType.DMA((len(masks), 2, 1)),
        ],
        compiler_params=pltpu.CompilerParams(vmem_limit_bytes=WHOLE_LIMIT),
        name="wind_products",
    )(wind_u, wind_v)
    return {
        (chunk, mask): outs[i * len(widths) + chunk] for i, mask in enumerate(masks) for chunk in range(len(widths))
    }


def forward_kernel(count, begun, ends, *refs):
    lines, refs = refs[:count], refs[count:]
    table, turn_cos, turn_sin = refs[:3]
    earlier, refs = (refs[3], refs[4:]) if begun else (None, refs[3:])
    step = pl.program_id(0)
    size = table.shape[1] // 2
    rows = lines[0].shape[0]
    both = jnp.concatenate([jnp.concatenate([line[...]] * 2, axis=1) for line in lines], axis=0)
    sums = dot(both, table[...])
    real, imag = (earlier[0], earlier[1]) if begun else (None, None)
    for i in range(count):
        own = sums[i * rows : (i + 1) * rows]
        own_cos, own_sin = own[:, :size], own[:, size:]
        cos, sin = turn_cos[i], turn_sin[i]
        own_real, own_imag = own_cos * cos - own_sin * sin, own_cos * sin + own_sin * cos
        real, imag = (own_real, own_imag) if real is None else (real + own_real, imag + own_imag)
    if not ends:
        refs[0][0], refs[0][1] = real, imag
        return
    one_hot, out, by_wave, by_slot, wire, sems = refs
    devices, wire_rows, lanes = out.shape
    padded = one_hot.shape[0] // devices
    blocks = 2 * rows // lanes
    share = wire_rows // blocks
    place = pl.ds(pl.multiple_of(step * size, size), size)
    by_wave[:rows, place] = real.astype(BF16)
    by_wave[rows:, place] = (-imag).astype(BF16)

    @pl.when(step == pl.num_programs(0) - 1)
    def _():
        by_slot[...] = dot(one_hot[...], by_wave[...], NT)
        copies, out_step = [], devices // sems.shape[0]
        for device in range(devices):
            own = by_slot[device * padded : (device + 1) * padded, :]
            wire[device] = pack_rows(
                [own[:share, block * lanes : (block + 1) * lanes] for block in range(blocks)]
            ).astype(BF16)
            if (device + 1) % out_step == 0:
                piece = pl.ds(device + 1 - out_step, out_step)
                copies.append(pltpu.make_async_copy(wire.at[piece], out.at[piece], sems.at[device // out_step]))
                copies[-1].start()
        for copy in copies:
            copy.wait()


def forward(lines, table, turns, earlier=None, end=None):
    rows, columns = lines[0].shape
    waves = table.shape[1] // 2
    size = min(LANES, waves)
    turn_spec = pl.BlockSpec((len(lines), 1, size), lambda i: (0, 0, i))
    sum_spec = pl.BlockSpec((2, rows, size), lambda i: (0, 0, i))
    args = list(lines) + [table, *turns]
    in_specs = [pl.BlockSpec((rows, columns), lambda i: (0, 0))] * len(lines)
    in_specs += [pl.BlockSpec((2 * columns, 2 * size), lambda i: (0, i)), turn_spec, turn_spec]
    if earlier is not None:
        args.append(earlier)
        in_specs.append(sum_spec)
    if end is None:
        out_shape, out_spec, scratch = jax.ShapeDtypeStruct((2, rows, waves), F32), sum_spec, []
    else:
        one_hot, share = end
        slots = one_hot.shape[0]
        lanes = wire_lanes(rows)
        out = (slots // round_up(share, 8), share * (2 * rows // lanes), lanes)
        args.append(one_hot)
        in_specs.append(pl.BlockSpec((slots, waves), lambda i: (0, 0)))
        out_shape, out_spec = jax.ShapeDtypeStruct(out, BF16), pl.BlockSpec(memory_space=pltpu.HBM)
        scratch = [pltpu.VMEM((2 * rows, waves), BF16), pltpu.VMEM((slots, 2 * rows), F32)]
        scratch += [pltpu.VMEM(out, BF16), pltpu.SemaphoreType.DMA((4,))]
    return pl.pallas_call(
        functools.partial(forward_kernel, len(lines), earlier is not None, end is not None),
        grid=(waves // size,),
        in_specs=in_specs,
        out_specs=out_spec,
        out_shape=out_shape,
        scratch_shapes=scratch,
        cost_estimate=pl.CostEstimate(
            flops=8 * len(lines) * rows * columns * waves, bytes_accessed=10**7, transcendentals=0
        ),
        compiler_params=pltpu.CompilerParams(vmem_limit_bytes=VMEM_LIMIT),
        name="forward",
    )(*args)


def sector_lines(exact, by_wave, table, turn_cos, turn_sin):
    count = turn_cos.shape[0]
    left = []
    for i in range(count):
        cos, sin = turn_cos[i], turn_sin[i]
        own_real, own_imag = by_wave[0].astype(F32), by_wave[1].astype(F32)
        real = own_real * cos - own_imag * sin
        minus = -(own_real * sin) - own_imag * cos
        left.append(jnp.concatenate([real, minus], axis=1))
    left = jnp.concatenate(left, axis=0) if count > 1 else left[0]
    high = left.astype(BF16)
    total = dot(jnp.concatenate([high, high], axis=1), table[...])
    if not exact:
        low = (left - high.astype(F32)).astype(BF16)
        total += dot(low, table[: low.shape[1]])
    return total.astype(BF16)


def backward_first_kernel(
    exact, wire, table_hbm, turn_cos, turn_sin, one_hot_hbm, mirror, out, by_wave_out, by_slot, table, one_hot, by_wave, sems
):
    one_hot_copy = pltpu.make_async_copy(one_hot_hbm, one_hot, sems.at[0])
    table_copy = pltpu.make_async_copy(table_hbm, table, sems.at[1])
    by_wave_copy = pltpu.make_async_copy(by_wave, by_wave_out, sems.at[2])
    one_hot_copy.start()
    table_copy.start()
    devices, _, lanes = wire.shape
    rows = out.shape[0]
    waves = one_hot.shape[0]
    width = mirror.shape[0]
    padded = by_slot.shape[0] // devices
    blocks = 2 * rows // lanes
    for device in range(devices):
        for block, piece in enumerate(unpack_rows(wire[device].astype(F32), blocks, padded)):
            by_slot[device * padded : (device + 1) * padded, block * lanes : (block + 1) * lanes] = piece.astype(BF16)
    one_hot_copy.wait()
    wave_ids = lax.broadcasted_iota(jnp.int32, (1, waves), 1)
    weight = jnp.where(wave_ids == 0, 1.0, 2.0).astype(F32)
    ordered = dot(one_hot[...], by_slot[...]).astype(BF16)
    for part in range(2):
        for field in range(2):
            own = slice(field * width, (field + 1) * width)
            lanes_here = slice(part * rows + field * width, part * rows + (field + 1) * width)
            by_wave[part, own, :] = (dot(mirror[...], ordered[:, lanes_here], NT) * weight).astype(BF16)
    by_wave_copy.start()
    table_copy.wait()
    out[...] = sector_lines(exact, by_wave, table, turn_cos, turn_sin)
    by_wave_copy.wait()


def backward_first(wire, table, turns, one_hot, mirror, exact):
    rows = 2 * mirror.shape[0]
    waves, slots = one_hot.shape
    vmem, hbm = pl.BlockSpec(memory_space=pltpu.VMEM), pl.BlockSpec(memory_space=pl.ANY)
    return pl.pallas_call(
        functools.partial(backward_first_kernel, exact),
        in_specs=[vmem, hbm, vmem, vmem, hbm, vmem],
        out_specs=[vmem, pl.BlockSpec(memory_space=pltpu.HBM)],
        out_shape=[
            jax.ShapeDtypeStruct((rows, table.shape[1]), BF16),
            jax.ShapeDtypeStruct((2, rows, waves), BF16),
        ],
        scratch_shapes=[
            pltpu.VMEM((slots, 2 * rows), BF16),
            pltpu.VMEM(table.shape, BF16),
            pltpu.VMEM(one_hot.shape, BF16),
            pltpu.VMEM((2, rows, waves), BF16),
            pltpu.SemaphoreType.DMA((3,)),
        ],
        cost_estimate=pl.CostEstimate(flops=10**9, bytes_accessed=10**7, transcendentals=0),
        compiler_params=pltpu.CompilerParams(vmem_limit_bytes=VMEM_LIMIT),
        name="backward_first",
    )(wire, table, *turns, one_hot, mirror)


def backward_rest_kernel(exact, by_wave, table, turn_cos, turn_sin, *outs):
    rows = outs[0].shape[0]
    total = sector_lines(exact, by_wave, table, turn_cos, turn_sin)
    for i, out in enumerate(outs):
        out[...] = total[i * rows : (i + 1) * rows]


def backward_rest(by_wave, table, turns, exact):
    _, rows, _ = by_wave.shape
    count = turns[0].shape[0]
    vmem = pl.BlockSpec(memory_space=pltpu.VMEM)
    return pl.pallas_call(
        functools.partial(backward_rest_kernel, exact),
        in_specs=[vmem] * 4,
        out_specs=[vmem] * count,
        out_shape=[jax.ShapeDtypeStruct((rows, table.shape[1]), BF16)] * count,
        cost_estimate=pl.CostEstimate(flops=3 * 10**9, bytes_accessed=10**7, transcendentals=0),
        compiler_params=pltpu.CompilerParams(vmem_limit_bytes=VMEM_LIMIT),
        name="backward_rest",
    )(by_wave, table, *turns)


def placing_kernel(parts, widths, *refs):
    blocks, (out, wide, sems) = refs[: len(parts)], refs[-3:]
    _, rows, _ = out.shape
    lat_rows = rows // 2
    south, near = band_place(lax.axis_index("lat"), lax.axis_size("lat"))
    copies = []
    for i, (chunk, mask) in enumerate(parts):
        width = widths[chunk]
        start = chunk_start(widths, chunk, near)
        start = jnp.where(south, lat_rows - start - width, start)
        level = lax.axis_index("lon") ^ mask
        for field in range(2):
            own = slice(field * width, (field + 1) * width)
            wide[i, own] = blocks[i][own].astype(F32)
            place = pl.ds(pl.multiple_of(field * lat_rows + start, math.gcd(*widths, lat_rows)), width)
            copies.append(pltpu.make_async_copy(wide.at[i, own], out.at[level, place], sems.at[i, field]))
            copies[-1].start()
    for copy in copies:
        copy.wait()


def placed(blocks, parts, widths, shape, earlier=None):
    count = len(parts)
    vmem, hbm = pl.BlockSpec(memory_space=pltpu.VMEM), pl.BlockSpec(memory_space=pl.ANY)
    more = () if earlier is None else (earlier,)
    return pl.pallas_call(
        functools.partial(placing_kernel, parts, widths),
        in_specs=[vmem] * count + [hbm] * len(more),
        out_specs=hbm,
        out_shape=jax.ShapeDtypeStruct(shape, F32),
        scratch_shapes=[
            pltpu.VMEM((count, 2 * max(widths[chunk] for chunk, _ in parts), shape[2]), F32),
            pltpu.SemaphoreType.DMA((count, 2)),
        ],
        input_output_aliases={count: 0} if more else {},
        compiler_params=pltpu.CompilerParams(vmem_limit_bytes=VMEM_LIMIT),
        name="placed",
    )(*[blocks[part] for part in parts], *more)


def round_up(value, unit):
    return -(-value // unit) * unit


def pack_rows(pieces):
    share = pieces[0].shape[0]
    main = share // 8 * 8
    parts = [piece[:main] for piece in pieces] if main else []
    parts += [piece[main:] for piece in pieces] if main < share else []
    return jnp.concatenate(parts, axis=0) if len(parts) > 1 else parts[0]


def unpack_rows(value, count, fill):
    share = value.shape[0] // count
    main = share // 8 * 8
    rest = share - main
    pieces = []
    for i in range(count):
        parts = [value[i * main : (i + 1) * main]] if main else []
        parts += [value[count * main + i * rest : count * main + (i + 1) * rest]] if rest else []
        parts += [jnp.zeros((fill - share, value.shape[1]), value.dtype)] if fill > share else []
        pieces.append(jnp.concatenate(parts, axis=0) if len(parts) > 1 else parts[0])
    return pieces


def wire_lanes(rows):
    return LANES if 2 * rows % LANES == 0 else 2 * rows


def legendre_kernel(sides, widths_in, widths, group, place, order, blocks, damping, basis, *rest):
    wires = len(widths)
    received, rest = rest[: len(widths_in)], rest[len(widths_in) :]
    spectral_out, returned_out, rest = rest[0], rest[1 : 1 + wires], rest[1 + wires :]
    spectral, returned, (held, buffer, sems, out_sems, spectral_sem) = rest[0], rest[1 : 1 + wires], rest[1 + wires :]
    lat_rows = sum(widths)
    devices = received[0].shape[0]
    sectors, share = spectral.shape[:2]
    slots, degrees, half_lat = basis.shape
    sources = devices // sectors
    fields = sides // 2
    combos = sectors * sides
    lane_blocks = held.shape[0]
    stride = held.shape[1] // (2 * combos)
    groups = share // group
    most = degrees // STEP
    scale = 1.0 / math.sqrt(degrees)
    out_step = devices // out_sems.shape[1]

    def copies(index, count):
        ring = lax.rem(index, DEPTH)
        rows = pl.ds(0, count * STEP)
        return [
            pltpu.make_async_copy(
                basis.at[jnp.minimum(place[0] + order[index * group + i], slots - 1), rows, :],
                buffer.at[ring, i, rows, :],
                sems.at[ring, i],
            )
            for i in range(group)
        ]

    def fetch(index):
        for count in range(1, most + 1):

            @pl.when(blocks[index] == count)
            def _():
                for copy in copies(index, count):
                    copy.start()

    for index in range(min(DEPTH - 1, groups)):
        fetch(index)

    def wire_pieces(kinds, wire, device, wire_block):
        source, sector = divmod(device, sectors)
        side, near = (0, source) if source < sources // 2 else (1, sources - 1 - source)
        chunk_width = kinds[wire]
        lanes = wire_lanes(fields * chunk_width)
        begin = near * lat_rows + chunk_start(kinds, wire, near)
        column, end = wire_block * lanes, (wire_block + 1) * lanes
        while column < end:
            part_field, lat = divmod(column, chunk_width)
            part, field = divmod(part_field, fields)
            row = (side * combos + sector * sides + field * 2 + part) * stride
            at = begin + lat
            width = min(end - column, chunk_width - lat, LANES - at % LANES)
            yield column - wire_block * lanes, width, row, at // LANES, at % LANES
            column += width

    for wire in range(len(widths_in)):
        wire_blocks = received[wire].shape[1] // share
        for device in range(devices):
            own_blocks = unpack_rows(received[wire][device].astype(F32), wire_blocks, stride)
            for wire_block, piece in enumerate(own_blocks):
                for at, width, row, block, lane in wire_pieces(widths_in, wire, device, wire_block):
                    held[block, row : row + stride, lane : lane + width] = piece[:, at : at + width]

    def load_slot(slot):
        rows = pl.ds(slot, 2 * combos, stride=stride)
        return jnp.concatenate([held[block, rows, :] for block in range(lane_blocks)], axis=1)

    def store_slot(slot, value):
        rows = pl.ds(slot, 2 * combos, stride=stride)
        for block in range(lane_blocks):
            held[block, rows, :] = value[:, block * LANES : (block + 1) * LANES]

    def one_group(index, count):
        ring = lax.rem(index, DEPTH)
        here = [order[index * group + i] for i in range(group)]
        if count == 0:
            for slot in here:
                for sector in range(sectors):
                    spectral[place[1] ^ sector, slot] = jnp.zeros(spectral.shape[2:], F32)
                store_slot(slot, jnp.zeros((2 * combos, half_lat), F32))
            return
        width = count * STEP
        for copy in copies(index, count):
            copy.wait()
        parity = 1.0 - 2.0 * (lax.broadcasted_iota(jnp.int32, (1, width), 1) % 2).astype(F32)
        left = [load_slot(slot).astype(BF16) for slot in here]
        sums = [dot(left[i], buffer[ring, i, :width, :], NT) for i in range(group)]
        damped = [
            (sums[i][:combos] + parity * sums[i][combos:]) * damping[slot, :, :width] for i, slot in enumerate(here)
        ]
        turned = [jnp.concatenate([value, parity * value], axis=0).astype(BF16) for value in damped]
        backs = [dot(turned[i], buffer[ring, i, :width, :]) * scale for i in range(group)]
        for i, slot in enumerate(here):
            for sector in range(sectors):
                spectral[place[1] ^ sector, slot, :, :width] = damped[i][sector * sides : (sector + 1) * sides]
                if width < degrees:
                    spectral[place[1] ^ sector, slot, :, width:] = jnp.zeros((sides, degrees - width), F32)
        for i, slot in enumerate(here):
            store_slot(slot, backs[i])

    def loop_body(index, carry):
        @pl.when(index + DEPTH - 1 < groups)
        def _():
            fetch(index + DEPTH - 1)

        for count in range(most + 1):
            pl.when(blocks[index] == count)(functools.partial(one_group, index, count))
        return carry

    lax.fori_loop(0, groups, loop_body, 0)

    spectral_copy = pltpu.make_async_copy(spectral, spectral_out, spectral_sem)
    spectral_copy.start()
    out_copies = []
    for wire in range(wires):
        wire_blocks = returned[wire].shape[1] // share
        for device in range(devices):
            pieces = []
            for wire_block in range(wire_blocks):
                parts = [
                    held[block, row : row + share, lane : lane + width]
                    for _, width, row, block, lane in wire_pieces(widths, wire, device, wire_block)
                ]
                pieces.append(jnp.concatenate(parts, axis=1) if len(parts) > 1 else parts[0])
            returned[wire][device] = pack_rows(pieces).astype(BF16)
            if (device + 1) % out_step == 0:
                part = pl.ds(device + 1 - out_step, out_step)
                copy = pltpu.make_async_copy(
                    returned[wire].at[part], returned_out[wire].at[part], out_sems.at[wire, device // out_step]
                )
                copy.start()
                out_copies.append(copy)
    for copy in (*out_copies, spectral_copy):
        copy.wait()


def legendre(received, basis, damping, place, order, blocks, sectors, sides, widths_in, widths, group):
    share = order.shape[0]
    devices = received[0].shape[0]
    returned = []
    for width in widths:
        lanes = wire_lanes(2 * width)
        returned.append((devices, share * (4 * width // lanes), lanes))
    degrees, half_lat = basis.shape[1:]
    combos = sectors * sides
    smem, vmem, hbm = (pl.BlockSpec(memory_space=space) for space in (pltpu.SMEM, pltpu.VMEM, pl.ANY))
    return pl.pallas_call(
        functools.partial(legendre_kernel, sides, widths_in, widths, group),
        in_specs=[smem, smem, smem, vmem, hbm] + [vmem] * len(widths_in),
        out_specs=[pl.BlockSpec(memory_space=pltpu.HBM)] * (1 + len(widths)),
        out_shape=[
            jax.ShapeDtypeStruct((sectors, share, sides, degrees), F32),
            *[jax.ShapeDtypeStruct(wire, BF16) for wire in returned],
        ],
        scratch_shapes=[
            pltpu.VMEM((sectors, share, sides, degrees), F32),
            *[pltpu.VMEM(wire, BF16) for wire in returned],
            pltpu.VMEM((half_lat // LANES, 2 * combos * round_up(share, 8), LANES), F32),
            pltpu.VMEM((DEPTH, group, degrees, half_lat), BF16),
            pltpu.SemaphoreType.DMA((DEPTH, group)),
            pltpu.SemaphoreType.DMA((len(widths), 8)),
            pltpu.SemaphoreType.DMA,
        ],
        cost_estimate=pl.CostEstimate(
            flops=4 * share * degrees * half_lat * 2 * combos,
            bytes_accessed=2 * share * degrees * half_lat,
            transcendentals=0,
        ),
        compiler_params=pltpu.CompilerParams(vmem_limit_bytes=LEGENDRE_LIMIT),
        name="legendre",
    )(place, order, blocks, damping, basis, *received)


def degree_order(counts):
    size = counts.shape[0]
    ids = jnp.arange(size, dtype=jnp.int32)
    ahead = (counts[None, :] > counts[:, None]) | ((counts[None, :] == counts[:, None]) & (ids[None, :] < ids[:, None]))
    rank = jnp.sum(ahead.astype(jnp.int32), axis=1)
    placed = rank[:, None] == ids[None, :]
    order = jnp.sum(jnp.where(placed, ids[:, None], 0), axis=0)
    sorted_counts = jnp.sum(jnp.where(placed, counts[:, None], 0), axis=0)
    group = max(g for g in range(1, 6) if size % g == 0)
    return order, (sorted_counts[::group] + (STEP - 1)) // STEP, group


def body(wind_u, wind_v, basis, wave_slots, degree_count, viscosity):
    sectors = lax.axis_size("lon")
    owners = lax.axis_size("lat")
    sector_index = lax.axis_index("lon")
    owner_index = lax.axis_index("lat")
    levels, lat_rows, lon_cols = wind_u.shape
    capacity, degrees, half_lat = basis.shape
    waves = wave_slots.shape[0]
    assert levels == sectors and sectors & (sectors - 1) == 0
    rows = 2 * lat_rows
    share = -(-capacity // sectors)
    padded = round_up(share, 8)
    length = sectors * lon_cols
    masks = [sectors // 2] + [mask for mask in range(sectors - 1, 0, -1) if mask != sectors // 2] + [0]

    def across(value, mask):
        return lax.ppermute(value, "lon", [(i, i ^ mask) for i in range(sectors)]) if mask else value

    def partners(some):
        return jnp.stack([sector_index ^ mask for mask in some]).astype(jnp.int32)

    far, rest = masks[:1], masks[1:]
    whole, widths = (lat_rows,), chunk_widths(lat_rows)
    small_first = [0]

    first_made = wind_products(wind_u, wind_v, far, whole)
    lines = {}
    for chunk in small_first[:1]:
        for mask in far:
            lines[chunk, mask] = across(first_made[chunk, mask], mask)
    made = {**first_made, **wind_products(wind_u, wind_v, rest, whole)}
    for chunk in small_first:
        for mask in masks:
            if (chunk, mask) not in lines:
                lines[chunk, mask] = across(made[chunk, mask], mask)

    wave_ids = jnp.arange(waves, dtype=jnp.int32)
    places = jnp.arange(owners * sectors * padded, dtype=jnp.int32)
    place_owner, place_sector, place_slot = places // (sectors * padded), places // padded % sectors, places % padded
    in_owner = place_sector * share + place_slot
    named = jnp.where((place_slot < share) & (in_owner < capacity), place_owner * capacity + in_owner, -1)
    forward_table, one_hot = wave_table(lon_cols, waves, length, True, named, wave_slots)
    backward_table, one_hot_turned = wave_table(waves, lon_cols, length, False, named, wave_slots)
    backward_table, one_hot_turned = (
        pltpu.with_memory_space_constraint(value, pltpu.HBM) for value in (backward_table, one_hot_turned)
    )
    turns = sector_turns(sectors, waves)

    def turns_of(some):
        at = partners(some)
        return tuple(jnp.take(turn, at, axis=0) for turn in turns)

    first = sector_index * share
    local_ids = jnp.arange(share, dtype=jnp.int32)
    inside = first + local_ids < capacity
    at = owner_index * capacity + jnp.minimum(first + local_ids, capacity - 1)
    here = at[:, None] == wave_slots[None, :]
    wave_here = jnp.sum(jnp.where(here, wave_ids[None, :], 0), axis=1)
    count_here = jnp.where(inside, jnp.sum(jnp.where(here, degree_count[None, :], 0), axis=1), 0)
    degree_ids = jnp.arange(degrees, dtype=jnp.int32)
    total_degree = wave_here[:, None] + degree_ids[None, :]
    scaled = (total_degree * (total_degree + 1)).astype(F32) / float(degrees * (degrees + 1))
    kept = degree_ids[None, :] < count_here[:, None]
    sides = 4
    rates = jnp.repeat(viscosity, sides)
    damping = 1.0 / (1.0 + rates[None, :, None] * (scaled * scaled)[:, None, :])
    damping = jnp.where(kept[:, None, :], damping * (1.0 / math.sqrt(2 * half_lat)), 0.0)
    order, blocks, group = degree_order(count_here)

    by_arrival = list(dict.fromkeys([0, *[mask for mask in reversed(masks) if mask < sectors // 2], *masks]))
    early, late = by_arrival[:-1], by_arrival[-1:]
    received = [None]
    for chunk in small_first:
        own = {mask: lines[chunk, mask] for mask in masks}
        if chunk == 0:
            sums = forward([own[mask] for mask in early], forward_table, turns_of(early))
            fourier = forward([own[mask] for mask in late], forward_table, turns_of(late), sums, (one_hot, share))
        else:
            fourier = forward([own[mask] for mask in by_arrival], forward_table, turns_of(by_arrival), None, (one_hot, share))
        received[chunk] = lax.all_to_all(fourier, ("lat", "lon"), split_axis=0, concat_axis=0, tiled=True)
    place = jnp.stack([first, sector_index]).astype(jnp.int32)
    spectral, *returned = legendre(
        received, basis, damping, place, order, blocks, sectors, sides, whole, widths, group
    )

    exact = sectors in (1, 2, 4)
    far_turns, rest_turns = turns_of(far), turns_of(rest)
    south, _ = band_place(owner_index, owners)
    back, regrouped = {}, []
    for chunk, wire in enumerate(returned):
        if chunk:
            wire, regrouped[-1] = lax.optimization_barrier((wire, regrouped[-1]))
        regrouped.append(lax.all_to_all(wire, ("lat", "lon"), split_axis=0, concat_axis=0, tiled=True))
    for chunk, width in enumerate(widths):
        ids = jnp.arange(width, dtype=jnp.int32)
        mirror = (ids[:, None] == jnp.where(south, width - 1 - ids, ids)[None, :]).astype(BF16)
        far_lines, by_wave = backward_first(regrouped[chunk], backward_table, far_turns, one_hot_turned, mirror, exact)
        back[chunk, far[0]] = across(far_lines, far[0])
        others = backward_rest(by_wave, backward_table, rest_turns, exact)
        for mask, value in zip(rest, others):
            back[chunk, mask] = across(value, mask)

    coefficients = jnp.zeros((sectors * share, 1, 2, 2, degrees), F32)
    for mask in masks:
        own = across(spectral[mask].astype(BF16), mask).astype(F32).reshape(share, 1, 2, 2, degrees)
        coefficients = lax.dynamic_update_slice_in_dim(coefficients, own, (sector_index ^ mask) * share, 0)

    arrival = [(chunk, mask) for chunk in range(len(widths)) for mask in by_arrival]
    cuts = [0, len(early), len(arrival) - 1, len(arrival)]
    tendency = None
    for begin, end in zip(cuts, cuts[1:]):
        if end > begin:
            tendency = placed(back, arrival[begin:end], widths, (sectors, rows, lon_cols), tendency)
    return coefficients[:capacity], tendency.reshape(levels, 2, lat_rows, lon_cols)


def solution(mesh):
    return jax.shard_map(
        body,
        mesh=mesh,
        in_specs=(
            P(None, "lat", "lon"),
            P(None, "lat", "lon"),
            P("lat", None, None),
            P(),
            P(),
            P(),
        ),
        out_specs=(P("lat", "lon", None, None, None), P(None, None, "lat", "lon")),
        check_vma=False,
    )
```

```python
import functools
import math

import jax
import jax.numpy as jnp
import numpy as np
from jax import lax
from jax.experimental import pallas as pl
from jax.experimental.pallas import tpu as pltpu
from jax.sharding import PartitionSpec as P


BF16 = jnp.bfloat16
F32 = jnp.float32
MIB = 1024 * 1024
VMEM_LIMIT = 24 * MIB
LEGENDRE_LIMIT = 36 * MIB
WHOLE_LIMIT = 60 * MIB
STEP = 128
LANES = 128
DEPTH = 3
NT = (((1,), (1,)), ((), ()))
NN = (((1,), (0,)), ((), ()))


def dot(a, b, dims=NN):
    return lax.dot_general(a, b, dims, preferred_element_type=F32)


def phases(rows, columns, length):
    turns = 2.0 * np.pi * (rows[:, None] * columns[None, :] % length) / length
    return np.cos(turns), np.sin(turns)


def table_kernel(interleaved, near_cos, near_sin, far_cos, far_sin, named, wave_slots, out, hot_out, *rest):
    space, hot, sems = rest[-3:]
    near, lanes = near_cos.shape
    steps = far_cos.shape[0]
    count = steps * near
    size = min(LANES, lanes)
    if interleaved:
        hot[...] = (named[...] == wave_slots[...]).astype(F32).astype(BF16)
    else:
        slots_down = jnp.broadcast_to(wave_slots[...].astype(F32), (8, wave_slots.shape[1])).T[:, :1]
        hot[...] = (slots_down == named[...].astype(F32)).astype(F32).astype(BF16)
    copies = [pltpu.make_async_copy(hot, hot_out, sems.at[0])]
    copies[0].start()
    for step in range(steps):
        cos = far_cos[step] * near_cos[...] - far_sin[step] * near_sin[...]
        sin = far_sin[step] * near_cos[...] + far_cos[step] * near_sin[...]
        high = (cos.astype(BF16), sin.astype(BF16))
        low = tuple((value - top.astype(F32)).astype(BF16) for value, top in zip((cos, sin), high))
        for term, pair in enumerate((high, low)):
            for which, value in enumerate(pair):
                if interleaved:
                    row = term * count + step * near
                    for block in range(lanes // size):
                        lane = (2 * block + which) * size
                        space[row : row + near, lane : lane + size] = value[:, block * size : (block + 1) * size]
                else:
                    row = (2 * term + which) * count + step * near
                    space[row : row + near, :] = value
    copies.append(pltpu.make_async_copy(space, out, sems.at[1]))
    copies[1].start()
    for copy in copies:
        copy.wait()


def wave_table(rows, columns, length, interleaved, named, wave_slots, *spares):
    near = 32
    near_cos, near_sin = phases(np.arange(near), np.arange(columns), length)
    far_cos, far_sin = phases(np.arange(rows // near) * near, np.arange(columns), length)
    scaling = 1.0 / math.sqrt(length)
    shape = (2 * rows, 2 * columns) if interleaved else (4 * rows, columns)
    waves, slots = wave_slots.shape[0], named.shape[0]
    hot_shape = (slots, waves) if interleaved else (waves, slots)
    return pl.pallas_call(
        functools.partial(table_kernel, interleaved),
        out_specs=[pl.BlockSpec(memory_space=pltpu.HBM)] * (2 + len(spares)),
        out_shape=[jax.ShapeDtypeStruct(one, BF16) for one in (shape, hot_shape, *spares)],
        scratch_shapes=[pltpu.VMEM(shape, BF16), pltpu.VMEM(hot_shape, BF16), pltpu.SemaphoreType.DMA((2,))],
        compiler_params=pltpu.CompilerParams(vmem_limit_bytes=WHOLE_LIMIT),
        name="wave_table",
    )(
        jnp.asarray(near_cos * scaling, F32),
        jnp.asarray(near_sin * scaling, F32),
        jnp.asarray(far_cos[:, None, :], F32),
        jnp.asarray(far_sin[:, None, :], F32),
        named[:, None] if interleaved else named[None, :],
        wave_slots[None, :],
    )


def sector_turns(sectors, waves):
    both = phases(np.arange(sectors), np.arange(waves), sectors)
    return tuple(jnp.asarray(np.round(turn, 12)[:, None, :], F32) for turn in both)


def chunk_widths(lat_rows):
    main = lat_rows // LANES * LANES
    return (main, lat_rows - main) if main and 2 * (lat_rows - main) == LANES else (lat_rows,)


def chunk_start(widths, chunk, near):
    if len(widths) == 1:
        return 0
    odd = near % 2
    return odd * widths[1] if chunk == 0 else (1 - odd) * widths[0]


def band_place(owner_index, owners):
    south = owner_index >= owners // 2
    return south, jnp.where(south, owners - 1 - owner_index, owner_index)


def product_kernel(masks, widths, wind_u, wind_v, *refs):
    outs, (space, sems) = refs[:-2], refs[-2:]
    _, lat_rows, columns = wind_u.shape
    south, near = band_place(lax.axis_index("lat"), lax.axis_size("lat"))
    pieces = sems.shape[2]
    size = columns // pieces
    copies = {}
    for i, mask in enumerate(masks):
        level = lax.axis_index("lon") ^ mask
        for piece in range(pieces):
            own = pl.ds(piece * size, size)
            for which, wind in enumerate((wind_u, wind_v)):
                copy = pltpu.make_async_copy(
                    wind.at[level, :, own], space.at[i, which, :, own], sems.at[i, which, piece]
                )
                copy.start()
                copies[i, piece, which] = copy
    chosen = []
    for chunk, width in enumerate(widths):
        start = chunk_start(widths, chunk, near)
        ids = start + lax.broadcasted_iota(jnp.int32, (width, lat_rows), 0)
        lats = lax.broadcasted_iota(jnp.int32, (width, lat_rows), 1)
        chosen.append((lats == jnp.where(south, lat_rows - 1 - ids, ids)).astype(F32).astype(BF16))
    for i in range(len(masks)):
        for piece in range(pieces):
            own = pl.ds(piece * size, size)
            copies[i, piece, 0].wait()
            copies[i, piece, 1].wait()
            u, v = space[i, 0, :, own], space[i, 1, :, own]
            for field, product in enumerate((u * v, u * u - v * v)):
                product = product.astype(BF16)
                for chunk, width in enumerate(widths):
                    outs[i * len(widths) + chunk][field * width : (field + 1) * width, own] = dot(
                        chosen[chunk], product
                    ).astype(BF16)


def wind_products(wind_u, wind_v, masks, widths):
    _, lat_rows, columns = wind_u.shape
    hbm, vmem = pl.BlockSpec(memory_space=pl.ANY), pl.BlockSpec(memory_space=pltpu.VMEM)
    outs = pl.pallas_call(
        functools.partial(product_kernel, masks, widths),
        in_specs=[hbm, hbm],
        out_specs=[vmem] * (len(masks) * len(widths)),
        out_shape=[jax.ShapeDtypeStruct((2 * width, columns), BF16) for _ in masks for width in widths],
        scratch_shapes=[
            pltpu.VMEM((len(masks), 2, lat_rows, columns), F32),
            pltpu.SemaphoreType.DMA((len(masks), 2, 1)),
        ],
        compiler_params=pltpu.CompilerParams(vmem_limit_bytes=WHOLE_LIMIT),
        name="wind_products",
    )(wind_u, wind_v)
    return {
        (chunk, mask): outs[i * len(widths) + chunk] for i, mask in enumerate(masks) for chunk in range(len(widths))
    }


def forward_kernel(count, begun, ends, *refs):
    lines, refs = refs[:count], refs[count:]
    table, turn_cos, turn_sin = refs[:3]
    earlier, refs = (refs[3], refs[4:]) if begun else (None, refs[3:])
    step = pl.program_id(0)
    size = table.shape[1] // 2
    rows = lines[0].shape[0]
    both = jnp.concatenate([jnp.concatenate([line[...]] * 2, axis=1) for line in lines], axis=0)
    sums = dot(both, table[...])
    real, imag = (earlier[0], earlier[1]) if begun else (None, None)
    for i in range(count):
        own = sums[i * rows : (i + 1) * rows]
        own_cos, own_sin = own[:, :size], own[:, size:]
        cos, sin = turn_cos[i], turn_sin[i]
        own_real, own_imag = own_cos * cos - own_sin * sin, own_cos * sin + own_sin * cos
        real, imag = (own_real, own_imag) if real is None else (real + own_real, imag + own_imag)
    if not ends:
        refs[0][0], refs[0][1] = real, imag
        return
    one_hot, out, by_wave, by_slot, wire, sems = refs
    devices, wire_rows, lanes = out.shape
    padded = one_hot.shape[0] // devices
    blocks = 2 * rows // lanes
    share = wire_rows // blocks
    place = pl.ds(pl.multiple_of(step * size, size), size)
    by_wave[:rows, place] = real.astype(BF16)
    by_wave[rows:, place] = (-imag).astype(BF16)

    @pl.when(step == pl.num_programs(0) - 1)
    def _():
        by_slot[...] = dot(one_hot[...], by_wave[...], NT)
        copies, out_step = [], devices // sems.shape[0]
        for device in range(devices):
            own = by_slot[device * padded : (device + 1) * padded, :]
            wire[device] = pack_rows(
                [own[:share, block * lanes : (block + 1) * lanes] for block in range(blocks)]
            ).astype(BF16)
            if (device + 1) % out_step == 0:
                piece = pl.ds(device + 1 - out_step, out_step)
                copies.append(pltpu.make_async_copy(wire.at[piece], out.at[piece], sems.at[device // out_step]))
                copies[-1].start()
        for copy in copies:
            copy.wait()


def forward(lines, table, turns, earlier=None, end=None):
    rows, columns = lines[0].shape
    waves = table.shape[1] // 2
    size = min(LANES, waves)
    turn_spec = pl.BlockSpec((len(lines), 1, size), lambda i: (0, 0, i))
    sum_spec = pl.BlockSpec((2, rows, size), lambda i: (0, 0, i))
    args = list(lines) + [table, *turns]
    in_specs = [pl.BlockSpec((rows, columns), lambda i: (0, 0))] * len(lines)
    in_specs += [pl.BlockSpec((2 * columns, 2 * size), lambda i: (0, i)), turn_spec, turn_spec]
    if earlier is not None:
        args.append(earlier)
        in_specs.append(sum_spec)
    if end is None:
        out_shape, out_spec, scratch = jax.ShapeDtypeStruct((2, rows, waves), F32), sum_spec, []
    else:
        one_hot, share = end
        slots = one_hot.shape[0]
        lanes = wire_lanes(rows)
        out = (slots // round_up(share, 8), share * (2 * rows // lanes), lanes)
        args.append(one_hot)
        in_specs.append(pl.BlockSpec((slots, waves), lambda i: (0, 0)))
        out_shape, out_spec = jax.ShapeDtypeStruct(out, BF16), pl.BlockSpec(memory_space=pltpu.HBM)
        scratch = [pltpu.VMEM((2 * rows, waves), BF16), pltpu.VMEM((slots, 2 * rows), F32)]
        scratch += [pltpu.VMEM(out, BF16), pltpu.SemaphoreType.DMA((4,))]
    return pl.pallas_call(
        functools.partial(forward_kernel, len(lines), earlier is not None, end is not None),
        grid=(waves // size,),
        in_specs=in_specs,
        out_specs=out_spec,
        out_shape=out_shape,
        scratch_shapes=scratch,
        cost_estimate=pl.CostEstimate(
            flops=8 * len(lines) * rows * columns * waves, bytes_accessed=10**7, transcendentals=0
        ),
        compiler_params=pltpu.CompilerParams(vmem_limit_bytes=VMEM_LIMIT),
        name="forward",
    )(*args)


def sector_lines(exact, by_wave, table, turn_cos, turn_sin):
    count = turn_cos.shape[0]
    left = []
    for i in range(count):
        cos, sin = turn_cos[i], turn_sin[i]
        own_real, own_imag = by_wave[0].astype(F32), by_wave[1].astype(F32)
        real = own_real * cos - own_imag * sin
        minus = -(own_real * sin) - own_imag * cos
        left.append(jnp.concatenate([real, minus], axis=1))
    left = jnp.concatenate(left, axis=0) if count > 1 else left[0]
    high = left.astype(BF16)
    total = dot(jnp.concatenate([high, high], axis=1), table[...])
    if not exact:
        low = (left - high.astype(F32)).astype(BF16)
        total += dot(low, table[: low.shape[1]])
    return total.astype(BF16)


def backward_first_kernel(
    exact, wire, table_hbm, turn_cos, turn_sin, one_hot_hbm, mirror, out, by_wave_out, by_slot, table, one_hot, by_wave, sems
):
    one_hot_copy = pltpu.make_async_copy(one_hot_hbm, one_hot, sems.at[0])
    table_copy = pltpu.make_async_copy(table_hbm, table, sems.at[1])
    by_wave_copy = pltpu.make_async_copy(by_wave, by_wave_out, sems.at[2])
    one_hot_copy.start()
    table_copy.start()
    devices, _, lanes = wire.shape
    rows = out.shape[0]
    waves = one_hot.shape[0]
    width = mirror.shape[0]
    padded = by_slot.shape[0] // devices
    blocks = 2 * rows // lanes
    for device in range(devices):
        for block, piece in enumerate(unpack_rows(wire[device].astype(F32), blocks, padded)):
            by_slot[device * padded : (device + 1) * padded, block * lanes : (block + 1) * lanes] = piece.astype(BF16)
    one_hot_copy.wait()
    wave_ids = lax.broadcasted_iota(jnp.int32, (1, waves), 1)
    weight = jnp.where(wave_ids == 0, 1.0, 2.0).astype(F32)
    ordered = dot(one_hot[...], by_slot[...]).astype(BF16)
    for part in range(2):
        for field in range(2):
            own = slice(field * width, (field + 1) * width)
            lanes_here = slice(part * rows + field * width, part * rows + (field + 1) * width)
            by_wave[part, own, :] = (dot(mirror[...], ordered[:, lanes_here], NT) * weight).astype(BF16)
    by_wave_copy.start()
    table_copy.wait()
    out[...] = sector_lines(exact, by_wave, table, turn_cos, turn_sin)
    by_wave_copy.wait()


def backward_first(wire, table, turns, one_hot, mirror, exact):
    rows = 2 * mirror.shape[0]
    waves, slots = one_hot.shape
    vmem, hbm = pl.BlockSpec(memory_space=pltpu.VMEM), pl.BlockSpec(memory_space=pl.ANY)
    return pl.pallas_call(
        functools.partial(backward_first_kernel, exact),
        in_specs=[vmem, hbm, vmem, vmem, hbm, vmem],
        out_specs=[vmem, pl.BlockSpec(memory_space=pltpu.HBM)],
        out_shape=[
            jax.ShapeDtypeStruct((rows, table.shape[1]), BF16),
            jax.ShapeDtypeStruct((2, rows, waves), BF16),
        ],
        scratch_shapes=[
            pltpu.VMEM((slots, 2 * rows), BF16),
            pltpu.VMEM(table.shape, BF16),
            pltpu.VMEM(one_hot.shape, BF16),
            pltpu.VMEM((2, rows, waves), BF16),
            pltpu.SemaphoreType.DMA((3,)),
        ],
        cost_estimate=pl.CostEstimate(flops=10**9, bytes_accessed=10**7, transcendentals=0),
        compiler_params=pltpu.CompilerParams(vmem_limit_bytes=VMEM_LIMIT),
        name="backward_first",
    )(wire, table, *turns, one_hot, mirror)


def backward_rest_kernel(exact, by_wave, table, turn_cos, turn_sin, *outs):
    rows = outs[0].shape[0]
    total = sector_lines(exact, by_wave, table, turn_cos, turn_sin)
    for i, out in enumerate(outs):
        out[...] = total[i * rows : (i + 1) * rows]


def backward_rest(by_wave, table, turns, exact):
    _, rows, _ = by_wave.shape
    count = turns[0].shape[0]
    vmem = pl.BlockSpec(memory_space=pltpu.VMEM)
    return pl.pallas_call(
        functools.partial(backward_rest_kernel, exact),
        in_specs=[vmem] * 4,
        out_specs=[vmem] * count,
        out_shape=[jax.ShapeDtypeStruct((rows, table.shape[1]), BF16)] * count,
        cost_estimate=pl.CostEstimate(flops=3 * 10**9, bytes_accessed=10**7, transcendentals=0),
        compiler_params=pltpu.CompilerParams(vmem_limit_bytes=VMEM_LIMIT),
        name="backward_rest",
    )(by_wave, table, *turns)


def placing_kernel(parts, widths, *refs):
    blocks, (out, wide, sems) = refs[: len(parts)], refs[-3:]
    _, rows, _ = out.shape
    lat_rows = rows // 2
    south, near = band_place(lax.axis_index("lat"), lax.axis_size("lat"))
    copies = []
    for i, (chunk, mask) in enumerate(parts):
        width = widths[chunk]
        start = chunk_start(widths, chunk, near)
        start = jnp.where(south, lat_rows - start - width, start)
        level = lax.axis_index("lon") ^ mask
        for field in range(2):
            own = slice(field * width, (field + 1) * width)
            wide[i, own] = blocks[i][own].astype(F32)
            place = pl.ds(pl.multiple_of(field * lat_rows + start, math.gcd(*widths, lat_rows)), width)
            copies.append(pltpu.make_async_copy(wide.at[i, own], out.at[level, place], sems.at[i, field]))
            copies[-1].start()
    for copy in copies:
        copy.wait()


def placed(blocks, parts, widths, shape, earlier=None):
    count = len(parts)
    vmem, hbm = pl.BlockSpec(memory_space=pltpu.VMEM), pl.BlockSpec(memory_space=pl.ANY)
    more = () if earlier is None else (earlier,)
    return pl.pallas_call(
        functools.partial(placing_kernel, parts, widths),
        in_specs=[vmem] * count + [hbm] * len(more),
        out_specs=hbm,
        out_shape=jax.ShapeDtypeStruct(shape, F32),
        scratch_shapes=[
            pltpu.VMEM((count, 2 * max(widths[chunk] for chunk, _ in parts), shape[2]), F32),
            pltpu.SemaphoreType.DMA((count, 2)),
        ],
        input_output_aliases={count: 0} if more else {},
        compiler_params=pltpu.CompilerParams(vmem_limit_bytes=VMEM_LIMIT),
        name="placed",
    )(*[blocks[part] for part in parts], *more)


def round_up(value, unit):
    return -(-value // unit) * unit


def pack_rows(pieces):
    share = pieces[0].shape[0]
    main = share // 8 * 8
    parts = [piece[:main] for piece in pieces] if main else []
    parts += [piece[main:] for piece in pieces] if main < share else []
    return jnp.concatenate(parts, axis=0) if len(parts) > 1 else parts[0]


def unpack_rows(value, count, fill):
    share = value.shape[0] // count
    main = share // 8 * 8
    rest = share - main
    pieces = []
    for i in range(count):
        parts = [value[i * main : (i + 1) * main]] if main else []
        parts += [value[count * main + i * rest : count * main + (i + 1) * rest]] if rest else []
        parts += [jnp.zeros((fill - share, value.shape[1]), value.dtype)] if fill > share else []
        pieces.append(jnp.concatenate(parts, axis=0) if len(parts) > 1 else parts[0])
    return pieces


def wire_lanes(rows):
    return LANES if 2 * rows % LANES == 0 else 2 * rows


def legendre_kernel(sides, widths_in, widths, group, place, order, blocks, damping, basis, *rest):
    wires = len(widths)
    received, rest = rest[: len(widths_in)], rest[len(widths_in) + 1 :]
    spectral_out, returned_out, rest = rest[0], rest[1 : 1 + wires], rest[1 + wires :]
    spectral, returned, (held, buffer, sems, out_sems, spectral_sem) = rest[0], rest[1 : 1 + wires], rest[1 + wires :]
    lat_rows = sum(widths)
    devices = received[0].shape[0]
    sectors, share = spectral.shape[:2]
    slots, degrees, half_lat = basis.shape
    sources = devices // sectors
    fields = sides // 2
    combos = sectors * sides
    lane_blocks = held.shape[0]
    stride = held.shape[1] // (2 * combos)
    groups = share // group
    most = degrees // STEP
    scale = 1.0 / math.sqrt(degrees)
    out_step = devices // out_sems.shape[1]

    def copies(index, count):
        ring = lax.rem(index, DEPTH)
        rows = pl.ds(0, count * STEP)
        return [
            pltpu.make_async_copy(
                basis.at[jnp.minimum(place[0] + order[index * group + i], slots - 1), rows, :],
                buffer.at[ring, i, rows, :],
                sems.at[ring, i],
            )
            for i in range(group)
        ]

    def fetch(index):
        for count in range(1, most + 1):

            @pl.when(blocks[index] == count)
            def _():
                for copy in copies(index, count):
                    copy.start()

    for index in range(min(DEPTH - 1, groups)):
        fetch(index)

    def wire_pieces(kinds, wire, device, wire_block):
        source, sector = divmod(device, sectors)
        side, near = (0, source) if source < sources // 2 else (1, sources - 1 - source)
        chunk_width = kinds[wire]
        lanes = wire_lanes(fields * chunk_width)
        begin = near * lat_rows + chunk_start(kinds, wire, near)
        column, end = wire_block * lanes, (wire_block + 1) * lanes
        while column < end:
            part_field, lat = divmod(column, chunk_width)
            part, field = divmod(part_field, fields)
            row = (side * combos + sector * sides + field * 2 + part) * stride
            at = begin + lat
            width = min(end - column, chunk_width - lat, LANES - at % LANES)
            yield column - wire_block * lanes, width, row, at // LANES, at % LANES
            column += width

    for wire in range(len(widths_in)):
        wire_blocks = received[wire].shape[1] // share
        for device in range(devices):
            own_blocks = unpack_rows(received[wire][device].astype(F32), wire_blocks, stride)
            for wire_block, piece in enumerate(own_blocks):
                for at, width, row, block, lane in wire_pieces(widths_in, wire, device, wire_block):
                    held[block, row : row + stride, lane : lane + width] = piece[:, at : at + width]

    def load_slot(slot):
        rows = pl.ds(slot, 2 * combos, stride=stride)
        return jnp.concatenate([held[block, rows, :] for block in range(lane_blocks)], axis=1)

    def store_slot(slot, value):
        rows = pl.ds(slot, 2 * combos, stride=stride)
        for block in range(lane_blocks):
            held[block, rows, :] = value[:, block * LANES : (block + 1) * LANES]

    def one_group(index, count):
        ring = lax.rem(index, DEPTH)
        here = [order[index * group + i] for i in range(group)]
        if count == 0:
            for slot in here:
                for sector in range(sectors):
                    spectral[place[1] ^ sector, slot] = jnp.zeros(spectral.shape[2:], F32)
                store_slot(slot, jnp.zeros((2 * combos, half_lat), F32))
            return
        width = count * STEP
        for copy in copies(index, count):
            copy.wait()
        parity = 1.0 - 2.0 * (lax.broadcasted_iota(jnp.int32, (1, width), 1) % 2).astype(F32)
        left = [load_slot(slot).astype(BF16) for slot in here]
        sums = [dot(left[i], buffer[ring, i, :width, :], NT) for i in range(group)]
        damped = [
            (sums[i][:combos] + parity * sums[i][combos:]) * damping[slot, :, :width] for i, slot in enumerate(here)
        ]
        turned = [jnp.concatenate([value, parity * value], axis=0).astype(BF16) for value in damped]
        backs = [dot(turned[i], buffer[ring, i, :width, :]) * scale for i in range(group)]
        for i, slot in enumerate(here):
            for sector in range(sectors):
                spectral[place[1] ^ sector, slot, :, :width] = damped[i][sector * sides : (sector + 1) * sides]
                if width < degrees:
                    spectral[place[1] ^ sector, slot, :, width:] = jnp.zeros((sides, degrees - width), F32)
        for i, slot in enumerate(here):
            store_slot(slot, backs[i])

    def loop_body(index, carry):
        @pl.when(index + DEPTH - 1 < groups)
        def _():
            fetch(index + DEPTH - 1)

        for count in range(most + 1):
            pl.when(blocks[index] == count)(functools.partial(one_group, index, count))
        return carry

    lax.fori_loop(0, groups, loop_body, 0)

    spectral_copy = pltpu.make_async_copy(spectral, spectral_out, spectral_sem)
    spectral_copy.start()
    out_copies = []
    for wire in range(wires):
        wire_blocks = returned[wire].shape[1] // share
        for device in range(devices):
            pieces = []
            for wire_block in range(wire_blocks):
                parts = [
                    held[block, row : row + share, lane : lane + width]
                    for _, width, row, block, lane in wire_pieces(widths, wire, device, wire_block)
                ]
                pieces.append(jnp.concatenate(parts, axis=1) if len(parts) > 1 else parts[0])
            returned[wire][device] = pack_rows(pieces).astype(BF16)
            if (device + 1) % out_step == 0:
                part = pl.ds(device + 1 - out_step, out_step)
                copy = pltpu.make_async_copy(
                    returned[wire].at[part], returned_out[wire].at[part], out_sems.at[wire, device // out_step]
                )
                copy.start()
                out_copies.append(copy)
    for copy in (*out_copies, spectral_copy):
        copy.wait()


def wire_shape(devices, share, width):
    lanes = wire_lanes(2 * width)
    return devices, share * (4 * width // lanes), lanes


def legendre(received, spare, basis, damping, place, order, blocks, sectors, sides, widths_in, widths, group):
    share = order.shape[0]
    devices = received[0].shape[0]
    returned = [wire_shape(devices, share, width) for width in widths]
    degrees, half_lat = basis.shape[1:]
    combos = sectors * sides
    spare = pltpu.with_memory_space_constraint(spare, pltpu.HBM)
    smem, vmem, hbm = (pl.BlockSpec(memory_space=space) for space in (pltpu.SMEM, pltpu.VMEM, pl.ANY))
    return pl.pallas_call(
        functools.partial(legendre_kernel, sides, widths_in, widths, group),
        in_specs=[smem, smem, smem, vmem, hbm] + [vmem] * len(widths_in) + [hbm],
        out_specs=[pl.BlockSpec(memory_space=pltpu.HBM)] * (1 + len(widths)),
        out_shape=[
            jax.ShapeDtypeStruct((sectors, share, sides, degrees), F32),
            *[jax.ShapeDtypeStruct(wire, BF16) for wire in returned],
        ],
        scratch_shapes=[
            pltpu.VMEM((sectors, share, sides, degrees), F32),
            *[pltpu.VMEM(wire, BF16) for wire in returned],
            pltpu.VMEM((half_lat // LANES, 2 * combos * round_up(share, 8), LANES), F32),
            pltpu.VMEM((DEPTH, group, degrees, half_lat), BF16),
            pltpu.SemaphoreType.DMA((DEPTH, group)),
            pltpu.SemaphoreType.DMA((len(widths), 8)),
            pltpu.SemaphoreType.DMA,
        ],
        input_output_aliases={5 + len(widths_in): 1},
        cost_estimate=pl.CostEstimate(
            flops=4 * share * degrees * half_lat * 2 * combos,
            bytes_accessed=2 * share * degrees * half_lat,
            transcendentals=0,
        ),
        compiler_params=pltpu.CompilerParams(vmem_limit_bytes=LEGENDRE_LIMIT),
        name="legendre",
    )(place, order, blocks, damping, basis, *received, spare)


def degree_order(counts):
    size = counts.shape[0]
    ids = jnp.arange(size, dtype=jnp.int32)
    ahead = (counts[None, :] > counts[:, None]) | ((counts[None, :] == counts[:, None]) & (ids[None, :] < ids[:, None]))
    rank = jnp.sum(ahead.astype(jnp.int32), axis=1)
    placed = rank[:, None] == ids[None, :]
    order = jnp.sum(jnp.where(placed, ids[:, None], 0), axis=0)
    sorted_counts = jnp.sum(jnp.where(placed, counts[:, None], 0), axis=0)
    group = max(g for g in range(1, 6) if size % g == 0)
    return order, (sorted_counts[::group] + (STEP - 1)) // STEP, group


def body(wind_u, wind_v, basis, wave_slots, degree_count, viscosity):
    sectors = lax.axis_size("lon")
    owners = lax.axis_size("lat")
    sector_index = lax.axis_index("lon")
    owner_index = lax.axis_index("lat")
    levels, lat_rows, lon_cols = wind_u.shape
    capacity, degrees, half_lat = basis.shape
    waves = wave_slots.shape[0]
    assert levels == sectors and sectors & (sectors - 1) == 0
    rows = 2 * lat_rows
    share = -(-capacity // sectors)
    padded = round_up(share, 8)
    length = sectors * lon_cols
    masks = [sectors // 2] + [mask for mask in range(sectors - 1, 0, -1) if mask != sectors // 2] + [0]

    def across(value, mask):
        return lax.ppermute(value, "lon", [(i, i ^ mask) for i in range(sectors)]) if mask else value

    def partners(some):
        return jnp.stack([sector_index ^ mask for mask in some]).astype(jnp.int32)

    far, rest = masks[:1], masks[1:]
    whole, widths = (lat_rows,), chunk_widths(lat_rows)
    small_first = [0]

    first_made = wind_products(wind_u, wind_v, far, whole)
    lines = {}
    for chunk in small_first[:1]:
        for mask in far:
            lines[chunk, mask] = across(first_made[chunk, mask], mask)
    made = {**first_made, **wind_products(wind_u, wind_v, rest, whole)}
    for chunk in small_first:
        for mask in masks:
            if (chunk, mask) not in lines:
                lines[chunk, mask] = across(made[chunk, mask], mask)

    wave_ids = jnp.arange(waves, dtype=jnp.int32)
    places = jnp.arange(owners * sectors * padded, dtype=jnp.int32)
    place_owner, place_sector, place_slot = places // (sectors * padded), places // padded % sectors, places % padded
    in_owner = place_sector * share + place_slot
    named = jnp.where((place_slot < share) & (in_owner < capacity), place_owner * capacity + in_owner, -1)
    forward_table, one_hot, spare = wave_table(
        lon_cols, waves, length, True, named, wave_slots, wire_shape(owners * sectors, share, widths[0])
    )
    backward_table, one_hot_turned = wave_table(waves, lon_cols, length, False, named, wave_slots)
    backward_table, one_hot_turned = (
        pltpu.with_memory_space_constraint(value, pltpu.HBM) for value in (backward_table, one_hot_turned)
    )
    turns = sector_turns(sectors, waves)

    def turns_of(some):
        at = partners(some)
        return tuple(jnp.take(turn, at, axis=0) for turn in turns)

    first = sector_index * share
    local_ids = jnp.arange(share, dtype=jnp.int32)
    inside = first + local_ids < capacity
    at = owner_index * capacity + jnp.minimum(first + local_ids, capacity - 1)
    here = at[:, None] == wave_slots[None, :]
    wave_here = jnp.sum(jnp.where(here, wave_ids[None, :], 0), axis=1)
    count_here = jnp.where(inside, jnp.sum(jnp.where(here, degree_count[None, :], 0), axis=1), 0)
    degree_ids = jnp.arange(degrees, dtype=jnp.int32)
    total_degree = wave_here[:, None] + degree_ids[None, :]
    scaled = (total_degree * (total_degree + 1)).astype(F32) / float(degrees * (degrees + 1))
    kept = degree_ids[None, :] < count_here[:, None]
    sides = 4
    rates = jnp.repeat(viscosity, sides)
    damping = 1.0 / (1.0 + rates[None, :, None] * (scaled * scaled)[:, None, :])
    damping = jnp.where(kept[:, None, :], damping * (1.0 / math.sqrt(2 * half_lat)), 0.0)
    order, blocks, group = degree_order(count_here)

    by_arrival = list(dict.fromkeys([0, *[mask for mask in reversed(masks) if mask < sectors // 2], *masks]))
    early, late = by_arrival[:-1], by_arrival[-1:]
    received = [None]
    for chunk in small_first:
        own = {mask: lines[chunk, mask] for mask in masks}
        if chunk == 0:
            sums = forward([own[mask] for mask in early], forward_table, turns_of(early))
            fourier = forward([own[mask] for mask in late], forward_table, turns_of(late), sums, (one_hot, share))
        else:
            fourier = forward([own[mask] for mask in by_arrival], forward_table, turns_of(by_arrival), None, (one_hot, share))
        received[chunk] = lax.all_to_all(fourier, ("lat", "lon"), split_axis=0, concat_axis=0, tiled=True)
    place = jnp.stack([first, sector_index]).astype(jnp.int32)
    spectral, *returned = legendre(
        received, spare, basis, damping, place, order, blocks, sectors, sides, whole, widths, group
    )

    exact = sectors in (1, 2, 4)
    far_turns, rest_turns = turns_of(far), turns_of(rest)
    south, _ = band_place(owner_index, owners)
    back, regrouped = {}, []
    for chunk, wire in enumerate(returned):
        if chunk:
            wire, regrouped[-1] = lax.optimization_barrier((wire, regrouped[-1]))
        regrouped.append(lax.all_to_all(wire, ("lat", "lon"), split_axis=0, concat_axis=0, tiled=True))
    for chunk, width in enumerate(widths):
        ids = jnp.arange(width, dtype=jnp.int32)
        mirror = (ids[:, None] == jnp.where(south, width - 1 - ids, ids)[None, :]).astype(BF16)
        far_lines, by_wave = backward_first(regrouped[chunk], backward_table, far_turns, one_hot_turned, mirror, exact)
        back[chunk, far[0]] = across(far_lines, far[0])
        others = backward_rest(by_wave, backward_table, rest_turns, exact)
        for mask, value in zip(rest, others):
            back[chunk, mask] = across(value, mask)

    coefficients = jnp.zeros((sectors * share, 1, 2, 2, degrees), F32)
    for mask in masks:
        own = across(spectral[mask].astype(BF16), mask).astype(F32).reshape(share, 1, 2, 2, degrees)
        coefficients = lax.dynamic_update_slice_in_dim(coefficients, own, (sector_index ^ mask) * share, 0)

    arrival = [(chunk, mask) for chunk in range(len(widths)) for mask in by_arrival]
    cuts = [0, len(early), len(arrival) - 1, len(arrival)]
    tendency = None
    for begin, end in zip(cuts, cuts[1:]):
        if end > begin:
            tendency = placed(back, arrival[begin:end], widths, (sectors, rows, lon_cols), tendency)
    return coefficients[:capacity], tendency.reshape(levels, 2, lat_rows, lon_cols)


def solution(mesh):
    return jax.shard_map(
        body,
        mesh=mesh,
        in_specs=(
            P(None, "lat", "lon"),
            P(None, "lat", "lon"),
            P("lat", None, None),
            P(),
            P(),
            P(),
        ),
        out_specs=(P("lat", "lon", None, None, None), P(None, None, "lat", "lon")),
        check_vma=False,
    )
```
